32 devices in a mesh: seq: 2 (over core), rows: 16 (over z, y, x).
Axes of the slice: x: 2, y: 2, z: 4, core: 2. Of those that a mesh axis runs over, the one named last changes fastest.
Arguments:
- hidden: bfloat16 [16, 1024, 768], P('rows', 'seq'), may hold values from -6 to 6
- segments: int32 [16, 1024], P('rows'), may hold values from 0 to 7, never falling along the last dimension, each value on 1 to 256 neighbouring positions
- thoughts: int32 [16, 1024], P('rows', 'seq'), may hold values 0 or 1
- padding: int32 [16], P('rows'), may hold values from 0 to 511
- cotangent: bfloat16 [16, 1024, 768], P('rows', 'seq'), may hold values from -6 to 6
- first_gain: bfloat16 [768], replicated, may hold values from 0.5 to 1.5
- first_shift: bfloat16 [768], replicated, may hold values from -1.5 to 1.5
- joint_weight: bfloat16 [768, 2304], replicated, may hold values from -0.21875 to 0.21875
- query_bias: bfloat16 [768], replicated, may hold values from -1.5 to 1.5
- value_bias: bfloat16 [768], replicated, may hold values from -1.5 to 1.5
- output_weight: bfloat16 [768, 768], replicated, may hold values from -1.75 to 1.75
- output_bias: bfloat16 [768], replicated, may hold values from -1.5 to 1.5
- second_gain: bfloat16 [768], replicated, may hold values from 0.5 to 1.5
- second_shift: bfloat16 [768], replicated, may hold values from -1.5 to 1.5
- up_weight: bfloat16 [768, 3072], replicated, may hold values from -0.21875 to 0.21875
- up_bias: bfloat16 [3072], replicated, may hold values from -1.5 to 1.5
- down_weight: bfloat16 [3072, 768], replicated, may hold values from -0.109375 to 0.109375
- down_bias: bfloat16 [768], replicated, may hold values from -1.5 to 1.5
Outputs:
- block_output: bfloat16 [16, 1024, 768], P('rows', 'seq')
- hidden_grad: float32 [16, 1024, 768], P('rows', 'seq')
- first_gain_grad: float32 [768], P('rows')
- first_shift_grad: float32 [768], P('rows')
- joint_grad: float32 [768, 2304], P('rows')
- query_bias_grad: float32 [768], P('rows')
- value_bias_grad: float32 [768], P('rows')
- output_weight_grad: float32 [768, 768], P('rows')
- output_bias_grad: float32 [768], P('rows')
- second_gain_grad: float32 [768], P('rows')
- second_shift_grad: float32 [768], P('rows')
- up_weight_grad: float32 [768, 3072], P('rows')
- up_bias_grad: float32 [3072], P('rows')
- down_weight_grad: float32 [3072, 768], P('rows')
- down_bias_grad: float32 [768], P('rows')
The draws below stay inside these ranges and needn't reach their ends.
Inputs may be any that keep to these rules, and one draw needn't show every extreme that they name: `segments`: along each row the segment numbers never fall, and one segment covers at most a quarter of the row's 1024 positions.
All inputs are finite; a program needn't handle non-finite values. No bound on the sum of `thoughts` on one device may be relied on, other than what follows from the above.
Results may differ from the reference program's by a relative error of at most 0.03.
Values may be sent and summed in bfloat16 or wider, within the bound.
A program may use at most 192 MiB of HBM per device.

```python
import math
import jax
import jax.numpy as jnp
import numpy as np
from jax import lax

D = 768
H = 12
HD = 64
FF = 3072
LEN = 1024
SEGS = 8
ROWS = 16


def touch_ends(values, key, smallest, largest):
    spot = [jax.random.randint(jax.random.fold_in(key, axis), (), 0, length) for axis, length in enumerate(values.shape)]
    longest = values.shape.index(max(values.shape))
    next_to = spot[:longest] + [(spot[longest] + 1) % values.shape[longest]] + spot[longest + 1:]
    return values.at[tuple(spot)].set(smallest).at[tuple(next_to)].set(largest)


def shard_levels(own_key, shape, shards, smallest, top_value):
    level, own = 1.0, jax.random.fold_in(own_key, 6)
    for axis_at, blocks in shards:
        draws = jnp.exp(jax.random.uniform(jax.random.fold_in(own, axis_at), (blocks,), jnp.float32, smallest / len(shards), top_value / len(shards)))
        level = level * jnp.repeat(draws, shape[axis_at] // blocks).reshape([-1 if axis == axis_at else 1 for axis in range(len(shape))])
    return level


def length_profile(number_of, total, reach, slope):
    portions = [(1 << 20) // math.isqrt(grade ** slope) + 1 for grade in range(2, number_of + 1)]
    spare, holding = total - reach - (number_of - 1), [1] * (number_of - 1)
    while spare > 0:
        free = [i for i in range(number_of - 1) if holding[i] < reach]
        whole, left = sum([portions[i] for i in free]), spare
        for i in free:
            addition = min(reach - holding[i], max(1, left * portions[i] // whole), spare)
            holding[i] = holding[i] + addition
            spare = spare - addition
    return np.array([reach] + holding)


def uneven(key, number_of, total, most, skew):
    if number_of == 2:
        one = jax.random.randint(key, (), max(1, total - most), min(most, total - 1) + 1)
        return jnp.stack([one, total - one])
    sizes = jnp.asarray(length_profile(number_of, total, most, skew), jnp.int32)
    twos = (number_of - 1) // 2
    giver, receiver = sizes[1:1 + 2 * twos:2], sizes[2:2 + 2 * twos:2]
    slack = jnp.minimum(giver - 1, most - receiver)
    shifted = jax.random.randint(jax.random.fold_in(key, 1), (twos,), 0, 1 << 20) % (slack + 1)
    sizes = sizes.at[1:1 + 2 * twos:2].set(giver - shifted).at[2:2 + 2 * twos:2].set(receiver + shifted)
    return sizes[jax.random.permutation(jax.random.fold_in(key, 2), number_of)]


def noise(own_key, extent, deviation, reach, pieces=(), kind=jnp.bfloat16):
    values = jax.random.normal(own_key, extent, jnp.float32) * deviation
    if len(pieces) > 0:
        values = shard_levels(own_key, extent, pieces, -0.22, 0.18) * values
    return jnp.clip(values, min=-reach, max=reach).astype(kind)


def setup_inputs(seed: int = 0) -> dict:
    seeds = jax.random.split(jax.random.key(seed), 19)
    return {
        "hidden": noise(seeds[0], (ROWS, LEN, D), 1.0, 6.0, ((0, 16), (1, 2))),
        "segments": jax.vmap(lambda own: jnp.searchsorted(jnp.cumsum(uneven(own, SEGS, LEN, LEN // 4, 1)), jnp.arange(LEN), side="right"))(jax.random.split(seeds[1], ROWS)).reshape((ROWS, LEN)).astype(jnp.int32),
        "thoughts": touch_ends((jax.random.randint(seeds[2], (ROWS, LEN), 0, 4) < 1).astype(jnp.int32), jax.random.fold_in(seeds[2], 1), 0, 1),
        "padding": touch_ends(jax.random.randint(seeds[3], (ROWS,), 0, LEN // 2), jax.random.fold_in(seeds[3], 1), 0, (LEN // 2) - 1).astype(jnp.int32),
        "cotangent": noise(seeds[4], (ROWS, LEN, D), 1.0, 6.0, ((0, 16), (1, 2))),
        "first_gain": jnp.clip(1.0 + 0.1 * jax.random.normal(seeds[5], (D,), jnp.float32), 0.5, 1.5).astype(jnp.bfloat16),
        "first_shift": noise(seeds[6], (D,), 0.3, 1.5),
        "joint_weight": noise(seeds[7], (D, 3 * D), D ** -0.5, 0.21875),
        "query_bias": noise(seeds[8], (D,), 0.3, 1.5),
        "value_bias": noise(seeds[9], (D,), 0.3, 1.5),
        "output_weight": noise(seeds[10], (D, D), (max(D // 64, 1)) ** -0.5, 1.75),
        "output_bias": noise(seeds[11], (D,), 0.3, 1.5),
        "second_gain": jnp.clip(1.0 + 0.1 * jax.random.normal(seeds[12], (D,), jnp.float32), 0.5, 1.5).astype(jnp.bfloat16),
        "second_shift": noise(seeds[13], (D,), 0.3, 1.5),
        "up_weight": noise(seeds[14], (D, FF), D ** -0.5, 0.21875),
        "up_bias": noise(seeds[15], (FF,), 0.3, 1.5),
        "down_weight": noise(seeds[16], (FF, D), FF ** -0.5, 0.109375),
        "down_bias": noise(seeds[17], (D,), 0.3, 1.5),
    }


EPSILON = 1e-05
NEGATIVE = -1e+30
GELU_SCALE = math.sqrt(2.0 / math.pi)
GELU_CUBIC = 0.044715
HIGHEST = lax.Precision.HIGHEST

@jax.custom_vjp
def low(v):
    return lax.optimization_barrier(v.astype(jnp.bfloat16)).astype(jnp.float32)

@jax.custom_vjp
def low_back(v):
    return v

def low_keep(v):
    return (low(v), None)

def low_pass(kept, grad):
    return (grad,)

def back_keep(v):
    return (v, None)

def back_low(kept, grad):
    return (low(grad),)
low.defvjp(low_keep, low_pass)
low_back.defvjp(back_keep, back_low)

def normalize(values, gain, shift):
    centered = values - lax.optimization_barrier(jnp.mean(values, axis=-1, keepdims=True))
    scaled = centered * lax.rsqrt(lax.optimization_barrier(jnp.mean(centered * centered, axis=-1, keepdims=True)) + EPSILON)
    return scaled * gain + shift

def gelu_tanh(values):
    inner = GELU_SCALE * (values + GELU_CUBIC * values * values * values)
    return 0.5 * values * (1.0 + jnp.tanh(inner))

def project(values, weight):
    return jnp.einsum('gtd,de->gte', values, weight, precision=HIGHEST)

def attention(query, keys, values, segments, padding):
    groups = query.shape[0]
    block_size = min(512, LEN)
    block_count = LEN // block_size
    positions = jnp.arange(LEN, dtype=jnp.int32)
    limits = (LEN - padding)[:, None, None]

    def one_block(offset):
        query_block = lax.dynamic_slice_in_dim(query, offset, block_size, 1)
        query_place = offset + jnp.arange(block_size, dtype=jnp.int32)
        query_segment = lax.dynamic_slice_in_dim(segments, offset, block_size, 1)
        earlier = positions[None, None, :] <= query_place[None, :, None]
        shared = segments[:, None, :] == query_segment[:, :, None]
        unpadded = (positions[None, None, :] < limits) | (positions[None, None, :] == query_place[None, :, None])
        visible = earlier & shared & unpadded
        scores = low_back(jnp.einsum('gqhd,gkhd->ghqk', query_block, keys, precision=HIGHEST) * HD ** (-0.5))
        scores = jnp.where(visible[:, None], scores, NEGATIVE)
        probs = low(jax.nn.softmax(scores, axis=-1))
        return jnp.einsum('ghqk,gkhd->gqhd', probs, values, precision=HIGHEST)
    offsets = jnp.arange(block_count, dtype=jnp.int32) * block_size
    blocks = lax.map(jax.checkpoint(one_block), offsets)
    return jnp.moveaxis(blocks, 0, 1).reshape(groups, LEN, H * HD)

def forward(hidden, first_gain, first_shift, joint_weight, query_bias, value_bias, output_weight, output_bias, second_gain, second_shift, up_weight, up_bias, down_weight, down_bias, thoughts, segments, padding):
    groups = hidden.shape[0]
    previous = jnp.concatenate([jnp.zeros((groups, 1, D), jnp.float32), hidden[:, :-1]], axis=1)
    mixed = hidden + thoughts[:, :, None] * (previous - hidden)
    normed = low(normalize(mixed, first_gain, first_shift))
    joint = project(normed, joint_weight)
    query = low_back(low(joint[:, :, :D] + query_bias))
    keys = low_back(low(joint[:, :, D:2 * D]))
    values = low_back(low(joint[:, :, 2 * D:] + value_bias))

    def shaped(tensor):
        return tensor.reshape(groups, LEN, H, HD)
    attended = low_back(low(attention(shaped(query), shaped(keys), shaped(values), segments, padding)))
    middle = mixed + low_back(project(attended, output_weight)) + output_bias
    second = low(normalize(middle, second_gain, second_shift))
    units = low_back(project(second, up_weight)) + up_bias
    activated = low(gelu_tanh(units))
    return middle + project(activated, down_weight) + down_bias

def reference(hidden, segments, thoughts, padding, cotangent, first_gain, first_shift, joint_weight, query_bias, value_bias, output_weight, output_bias, second_gain, second_shift, up_weight, up_bias, down_weight, down_bias):
    weights = tuple((weight_arg.astype(jnp.float32) for weight_arg in (first_gain, first_shift, joint_weight, query_bias, value_bias, output_weight, output_bias, second_gain, second_shift, up_weight, up_bias, down_weight, down_bias)))
    group_size = max(1, min(4096 // LEN, 16))
    batches = ROWS // group_size

    def regroup(tensor):
        return tensor.reshape((batches, group_size) + tensor.shape[1:])
    inputs = (regroup(hidden.astype(jnp.float32)), regroup(thoughts.astype(jnp.float32)), regroup(segments), regroup(padding), regroup(cotangent.astype(jnp.float32)))

    def one_group(totals, batch_rows):
        rows_value, thought_rows, segment_rows, padding_rows, cotangent_rows = batch_rows

        def apply_rows(rows_in, *params):
            return forward(rows_in, *params, thought_rows, segment_rows, padding_rows)
        outputs, pullback = jax.vjp(apply_rows, rows_value, *weights)
        gradients = pullback(cotangent_rows)
        totals = tuple((total + gradient for total, gradient in zip(totals, gradients[1:])))
        return (totals, (outputs.astype(jnp.bfloat16), gradients[0]))
    initial = tuple((jnp.zeros(weight_arg.shape, jnp.float32) for weight_arg in weights))
    totals, (outputs, input_grads) = lax.scan(one_group, initial, inputs)
    return (outputs.reshape(ROWS, LEN, D), input_grads.reshape(ROWS, LEN, D), totals[0], totals[1], totals[2], totals[3], totals[4], totals[5], totals[6], totals[7], totals[8], totals[9], totals[10], totals[11], totals[12])
```

```python
import functools
import math

import jax
import jax.numpy as jnp
from jax import lax
from jax.experimental import pallas as pl
from jax.experimental.pallas import tpu as pltpu
from jax.sharding import PartitionSpec as P

D = 768
H = 12
HD = 64
LEN = 1024


EPSILON = 1e-05
NEGATIVE = -1e30
GELU_SCALE = math.sqrt(2.0 / math.pi)
GELU_CUBIC = 0.044715


def from_behind(value, axis, steps):
    count = lax.axis_size(axis)
    leading, last = (max(0, -steps), min(count, count - steps))
    return lax.ppermute(value, axis, [(source, source + steps) for source in range(leading, last)])


def normalize(values):
    centered = values - jnp.mean(values, axis=-1, keepdims=True)
    inverse = lax.rsqrt(jnp.mean(centered * centered, axis=-1, keepdims=True) + EPSILON)
    return (centered * inverse, inverse)


def normalize_back(upstream, scaled, inverse, gain):
    weighted = upstream * gain
    inner = (
        weighted
        - jnp.mean(weighted, axis=-1, keepdims=True)
        - scaled * jnp.mean(weighted * scaled, axis=-1, keepdims=True)
    )
    return (
        inverse * inner,
        jnp.sum(upstream * scaled, axis=(0, 1)),
        jnp.sum(upstream, axis=(0, 1)),
    )


def gelu_pair(values):
    inner = GELU_SCALE * (values + GELU_CUBIC * values * values * values)
    tangent = jnp.tanh(inner)
    result = 0.5 * values * (1.0 + tangent)
    gelu_slope = 0.5 * (1.0 + tangent) + 0.5 * values * (1.0 - tangent * tangent) * GELU_SCALE * (
        1.0 + 3.0 * GELU_CUBIC * values * values
    )
    return (result, gelu_slope)


def project(values, weight):
    return jnp.einsum("rsd,de->rse", values, weight, preferred_element_type=jnp.float32)


def project_back(values, weight):
    return jnp.einsum("rse,de->rsd", values, weight, preferred_element_type=jnp.float32)


def outer_sum(left, right):
    return jnp.einsum("rsd,rse->de", left, right, preferred_element_type=jnp.float32)


def visibility(query_place, query_segment, key_place, key_segment, limits):
    earlier = key_place[None, None, :] <= query_place[None, :, None]
    shared = key_segment[:, None, :] == query_segment[:, :, None]
    unpadded = (key_place[None, None, :] < limits[:, None, None]) | (
        key_place[None, None, :] == query_place[None, :, None]
    )
    return earlier & shared & unpadded


def local(
    hidden,
    segments,
    thoughts,
    padding,
    cotangent,
    first_gain,
    first_shift,
    joint_weight,
    query_bias,
    value_bias,
    output_weight,
    output_bias,
    second_gain,
    second_shift,
    up_weight,
    up_bias,
    down_weight,
    down_bias,
):
    rows_here, span = (hidden.shape[0], hidden.shape[1])
    scale = HD ** (-0.5)
    key_size = min(512, LEN)
    position_base = lax.axis_index("seq") * span
    query_place = position_base + jnp.arange(span, dtype=jnp.int32)
    query_segment = lax.dynamic_slice_in_dim(segments, position_base, span, 1)
    limits = LEN - padding
    thought_mask = thoughts.astype(jnp.float32)[:, :, None]
    gain_first = first_gain.astype(jnp.float32)
    gain_second = second_gain.astype(jnp.float32)
    incoming = from_behind(hidden[:, span - 1, :], "seq", 1)
    inputs = hidden.astype(jnp.float32)
    previous = jnp.concatenate([incoming.astype(jnp.float32)[:, None, :], inputs[:, :-1]], axis=1)
    mixed = inputs + thought_mask * (previous - inputs)
    first_scaled, first_inverse = normalize(mixed)
    normed = (first_scaled * gain_first + first_shift.astype(jnp.float32)).astype(jnp.bfloat16)
    joint = project(normed, joint_weight)
    query_low = (joint[:, :, :D] + query_bias.astype(jnp.float32)).astype(jnp.bfloat16)
    key_low = joint[:, :, D : 2 * D].astype(jnp.bfloat16)
    value_low = (joint[:, :, 2 * D :] + value_bias.astype(jnp.float32)).astype(jnp.bfloat16)
    query_heads = query_low.reshape(rows_here, span, H, HD)

    def allowed_for(width_keys, offset):
        key_place = offset + jnp.arange(width_keys, dtype=jnp.int32)
        key_segment = lax.dynamic_slice_in_dim(segments, offset, width_keys, 1)
        return visibility(query_place, query_segment, key_place, key_segment, limits)[:, None]

    empty_stats = jnp.zeros((rows_here, H, span), jnp.float32)
    initial = (
        empty_stats + NEGATIVE,
        empty_stats,
        jnp.zeros((rows_here, span, H, HD), jnp.float32),
    )
    key_whole, value_whole = (
        lax.all_gather(key_low, "seq", axis=1, tiled=True),
        lax.all_gather(value_low, "seq", axis=1, tiled=True),
    )
    running = initial
    for first_key in range(0, LEN, key_size):
        attend_key_part = key_whole[:, first_key : first_key + key_size]
        attend_value_part = value_whole[:, first_key : first_key + key_size]
        attend_width_keys = attend_key_part.shape[1]
        attend_allowed = allowed_for(attend_width_keys, jnp.int32(first_key))
        update_highest, update_denominator, update_accumulated = running
        update_key_heads = attend_key_part.reshape(rows_here, attend_width_keys, H, HD)
        update_value_heads = attend_value_part.reshape(rows_here, attend_width_keys, H, HD)
        update_scores = (
            jnp.einsum(
                "rshd,rnhd->rhsn", query_heads, update_key_heads, preferred_element_type=jnp.float32
            )
            * scale
        )
        update_scores = jnp.where(attend_allowed, update_scores, NEGATIVE)
        fresh_max = jnp.maximum(update_highest, jnp.max(update_scores, axis=-1))
        exponent = jnp.where(attend_allowed, jnp.exp(update_scores - fresh_max[..., None]), 0.0)
        factor = jnp.exp(update_highest - fresh_max)
        update_denominator = update_denominator * factor + jnp.sum(exponent, axis=-1)
        weighted = jnp.einsum(
            "rhsn,rnhd->rshd",
            exponent.astype(jnp.bfloat16),
            update_value_heads,
            preferred_element_type=jnp.float32,
        )
        update_accumulated = update_accumulated * jnp.swapaxes(factor, 1, 2)[..., None] + weighted
        running = (fresh_max, update_denominator, update_accumulated)
    highest, denominator, accumulated = running
    attention_out = accumulated / jnp.swapaxes(denominator, 1, 2)[..., None]
    logsum = highest + jnp.log(denominator)
    attended = attention_out.reshape(rows_here, span, D).astype(jnp.bfloat16)
    middle = mixed + project(attended, output_weight) + output_bias.astype(jnp.float32)
    second_scaled, second_inverse = normalize(middle)
    second = (second_scaled * gain_second + second_shift.astype(jnp.float32)).astype(jnp.bfloat16)
    units = project(second, up_weight) + up_bias.astype(jnp.float32)
    activated_full, gelu_slope = gelu_pair(units)
    activated = activated_full.astype(jnp.bfloat16)
    block_output = (
        middle + project(activated, down_weight) + down_bias.astype(jnp.float32)
    ).astype(jnp.bfloat16)
    upstream = cotangent.astype(jnp.float32)
    down_bias_grad = jnp.sum(upstream, axis=(0, 1))
    down_weight_grad = outer_sum(activated, cotangent)
    unit_grad = project_back(cotangent, down_weight) * gelu_slope
    up_bias_grad = jnp.sum(unit_grad, axis=(0, 1))
    unit_low = unit_grad.astype(jnp.bfloat16)
    up_weight_grad = outer_sum(second, unit_low)
    middle_part, second_gain_grad, second_shift_grad = normalize_back(
        project_back(unit_low, up_weight), second_scaled, second_inverse, gain_second
    )
    middle_grad = upstream + middle_part
    output_bias_grad = jnp.sum(middle_grad, axis=(0, 1))
    middle_low = middle_grad.astype(jnp.bfloat16)
    output_weight_grad = outer_sum(attended, middle_low)
    attended_grad = project_back(middle_low, output_weight).astype(jnp.bfloat16)
    grad_heads = attended_grad.reshape(rows_here, span, H, HD)
    delta = jnp.swapaxes(jnp.sum(grad_heads.astype(jnp.float32) * attention_out, axis=-1), 1, 2)

    def attend_back(key_part, value_part, offset):
        width_keys = key_part.shape[1]
        allowed = allowed_for(width_keys, offset)
        key_heads = key_part.reshape(rows_here, width_keys, H, HD)
        value_heads = value_part.reshape(rows_here, width_keys, H, HD)
        scores = (
            jnp.einsum(
                "rshd,rnhd->rhsn", query_heads, key_heads, preferred_element_type=jnp.float32
            )
            * scale
        )
        scores = jnp.where(allowed, scores, NEGATIVE)
        probs = jnp.where(allowed, jnp.exp(scores - logsum[..., None]), 0.0)
        probs_low = probs.astype(jnp.bfloat16)
        value_term = jnp.einsum(
            "rhsn,rshd->rnhd", probs_low, grad_heads, preferred_element_type=jnp.float32
        )
        prob_grad = jnp.einsum(
            "rshd,rnhd->rhsn", grad_heads, value_heads, preferred_element_type=jnp.float32
        )
        score_grad = (probs * (prob_grad - delta[..., None])).astype(jnp.bfloat16)
        query_term = (
            jnp.einsum("rhsn,rnhd->rshd", score_grad, key_heads, preferred_element_type=jnp.float32)
            * scale
        )
        key_term = (
            jnp.einsum(
                "rhsn,rshd->rnhd", score_grad, query_heads, preferred_element_type=jnp.float32
            )
            * scale
        )
        return (
            query_term,
            key_term.reshape(rows_here, width_keys, D),
            value_term.reshape(rows_here, width_keys, D),
        )

    back_keys, back_values = (key_whole, value_whole)
    query_grad = jnp.zeros((rows_here, span, H, HD), jnp.float32)
    key_terms = []
    value_terms = []
    for first_key in range(0, LEN, key_size):
        query_term, key_term, value_term = attend_back(
            back_keys[:, first_key : first_key + key_size],
            back_values[:, first_key : first_key + key_size],
            jnp.int32(first_key),
        )
        query_grad = query_grad + query_term
        key_terms.append(key_term)
        value_terms.append(value_term)
    key_grad, value_grad = (
        lax.psum_scatter(
            jnp.concatenate(key_terms, axis=1).astype(jnp.bfloat16),
            "seq",
            scatter_dimension=1,
            tiled=True,
        ).astype(jnp.float32),
        lax.psum_scatter(
            jnp.concatenate(value_terms, axis=1).astype(jnp.bfloat16),
            "seq",
            scatter_dimension=1,
            tiled=True,
        ).astype(jnp.float32),
    )
    query_grad_low = query_grad.reshape(rows_here, span, D).astype(jnp.bfloat16)
    key_grad_low = key_grad.astype(jnp.bfloat16)
    value_grad_low = value_grad.astype(jnp.bfloat16)
    query_bias_grad = jnp.sum(query_grad_low.astype(jnp.float32), axis=(0, 1))
    value_bias_grad = jnp.sum(value_grad_low.astype(jnp.float32), axis=(0, 1))
    joint_low = jnp.concatenate([query_grad_low, key_grad_low, value_grad_low], axis=-1)
    joint_grad = outer_sum(normed, joint_low)
    mixed_part, first_gain_grad, first_shift_grad = normalize_back(
        project_back(joint_low, joint_weight), first_scaled, first_inverse, gain_first
    )
    mixed_grad = middle_grad + mixed_part
    carried = thought_mask * mixed_grad
    following = from_behind(carried[:, 0, :], "seq", -1)
    hidden_grad = (
        mixed_grad - carried + jnp.concatenate([carried[:, 1:], following[:, None, :]], axis=1)
    )
    (
        first_gain_grad,
        first_shift_grad,
        joint_grad,
        query_bias_grad,
        value_bias_grad,
        output_weight_grad,
        output_bias_grad,
        second_gain_grad,
        second_shift_grad,
        up_weight_grad,
        up_bias_grad,
        down_weight_grad,
        down_bias_grad,
    ) = (
        lax.psum_scatter(
            first_gain_grad.astype(jnp.bfloat16), "rows", scatter_dimension=0, tiled=True
        ).astype(jnp.float32),
        lax.psum_scatter(
            first_shift_grad.astype(jnp.bfloat16), "rows", scatter_dimension=0, tiled=True
        ).astype(jnp.float32),
        lax.psum_scatter(
            joint_grad.astype(jnp.bfloat16), "rows", scatter_dimension=0, tiled=True
        ).astype(jnp.float32),
        lax.psum_scatter(
            query_bias_grad.astype(jnp.bfloat16), "rows", scatter_dimension=0, tiled=True
        ).astype(jnp.float32),
        lax.psum_scatter(
            value_bias_grad.astype(jnp.bfloat16), "rows", scatter_dimension=0, tiled=True
        ).astype(jnp.float32),
        lax.psum_scatter(
            output_weight_grad.astype(jnp.bfloat16), "rows", scatter_dimension=0, tiled=True
        ).astype(jnp.float32),
        lax.psum_scatter(
            output_bias_grad.astype(jnp.bfloat16), "rows", scatter_dimension=0, tiled=True
        ).astype(jnp.float32),
        lax.psum_scatter(
            second_gain_grad.astype(jnp.bfloat16), "rows", scatter_dimension=0, tiled=True
        ).astype(jnp.float32),
        lax.psum_scatter(
            second_shift_grad.astype(jnp.bfloat16), "rows", scatter_dimension=0, tiled=True
        ).astype(jnp.float32),
        lax.psum_scatter(
            up_weight_grad.astype(jnp.bfloat16), "rows", scatter_dimension=0, tiled=True
        ).astype(jnp.float32),
        lax.psum_scatter(
            up_bias_grad.astype(jnp.bfloat16), "rows", scatter_dimension=0, tiled=True
        ).astype(jnp.float32),
        lax.psum_scatter(
            down_weight_grad.astype(jnp.bfloat16), "rows", scatter_dimension=0, tiled=True
        ).astype(jnp.float32),
        lax.psum_scatter(
            down_bias_grad.astype(jnp.bfloat16), "rows", scatter_dimension=0, tiled=True
        ).astype(jnp.float32),
    )
    (
        first_gain_grad,
        first_shift_grad,
        joint_grad,
        query_bias_grad,
        value_bias_grad,
        output_weight_grad,
        output_bias_grad,
        second_gain_grad,
        second_shift_grad,
        up_weight_grad,
        up_bias_grad,
        down_weight_grad,
        down_bias_grad,
    ) = (
        lax.psum(first_gain_grad.astype(jnp.bfloat16), "seq").astype(jnp.float32),
        lax.psum(first_shift_grad.astype(jnp.bfloat16), "seq").astype(jnp.float32),
        lax.psum(joint_grad.astype(jnp.bfloat16), "seq").astype(jnp.float32),
        lax.psum(query_bias_grad.astype(jnp.bfloat16), "seq").astype(jnp.float32),
        lax.psum(value_bias_grad.astype(jnp.bfloat16), "seq").astype(jnp.float32),
        lax.psum(output_weight_grad.astype(jnp.bfloat16), "seq").astype(jnp.float32),
        lax.psum(output_bias_grad.astype(jnp.bfloat16), "seq").astype(jnp.float32),
        lax.psum(second_gain_grad.astype(jnp.bfloat16), "seq").astype(jnp.float32),
        lax.psum(second_shift_grad.astype(jnp.bfloat16), "seq").astype(jnp.float32),
        lax.psum(up_weight_grad.astype(jnp.bfloat16), "seq").astype(jnp.float32),
        lax.psum(up_bias_grad.astype(jnp.bfloat16), "seq").astype(jnp.float32),
        lax.psum(down_weight_grad.astype(jnp.bfloat16), "seq").astype(jnp.float32),
        lax.psum(down_bias_grad.astype(jnp.bfloat16), "seq").astype(jnp.float32),
    )
    return (
        block_output,
        hidden_grad,
        first_gain_grad,
        first_shift_grad,
        joint_grad,
        query_bias_grad,
        value_bias_grad,
        output_weight_grad,
        output_bias_grad,
        second_gain_grad,
        second_shift_grad,
        up_weight_grad,
        up_bias_grad,
        down_weight_grad,
        down_bias_grad,
    )


F32, BF16 = (jnp.float32, jnp.bfloat16)
BLOCK = 512
FF = 3072
PIECE = 384
TILE = 48
WINDOW = 384


def nn(left, right):
    return lax.dot_general(left, right, (((1,), (0,)), ((), ())), preferred_element_type=F32)


def nt(left, right):
    return lax.dot_general(left, right, (((1,), (1,)), ((), ())), preferred_element_type=F32)


def tn(left, right):
    return lax.dot_general(left, right, (((0,), (0,)), ((), ())), preferred_element_type=F32)


def wide(column, copies):
    return jnp.concatenate([column] * copies, axis=1)


def row_norm(values):
    centered = values - jnp.mean(values, axis=-1, keepdims=True)
    inverse = lax.rsqrt(jnp.mean(centered * centered, axis=-1, keepdims=True) + EPSILON)
    return (centered * inverse, inverse)


def row_norm_back(upstream, scaled, inverse, gain):
    weighted = upstream * gain
    return inverse * (
        weighted
        - jnp.mean(weighted, axis=-1, keepdims=True)
        - scaled * jnp.mean(weighted * scaled, axis=-1, keepdims=True)
    )


def fold(values):
    return jnp.sum(values.reshape(values.shape[0] // 8, 8, values.shape[1]), axis=0)


def split_pair(values, lane):
    zero = jnp.zeros_like(values)
    return jnp.concatenate([jnp.where(lane < HD, values, zero), jnp.where(lane < HD, zero, values)], axis=0)


def join_pair(values):
    return jnp.concatenate([values[:HD, :128], values[HD:, 128:]], axis=0)


def step_kernel(
    hid, seg, tho, pad, cot, small, jw, ow, uw, dw,
    blk, hg, std, dgo, vec, nth,
    wb1, wb2, wo, fa, fb, fd, nb, st, q, kk, vv, kt, vt, ps, il, at, att, cotp, act, xx, ulo, ulp,
    hin, hs, mlp, do, dka, dva, gd, gs, r1d, r2d, r3d, r4d, r1, r2, r3, r4, mask, ksg, tht, ubg, sv, svr, cin,
    lsem, psend, precv, rsend, rrecv,
):
    core, line = (lax.axis_index("seq"), lax.axis_index("rows"))
    other = 1 - core
    bits = {"x": lax.rem(line, 2), "y": lax.rem(line // 2, 2), "l": lax.rem(line // 4, 2), "h": line // 8}
    peer = {
        "c": (other, line),
        "x": (core, line + 1 - 2 * bits["x"]),
        "y": (core, line + 2 - 4 * bits["y"]),
        "l": (core, line + 4 - 8 * bits["l"]),
        "h": (core, line + 8 - 16 * bits["h"]),
    }
    base = core * BLOCK
    core_f = core.astype(F32)
    half = pl.multiple_of(core * PIECE, 128)
    other_half = pl.multiple_of(other * PIECE, 128)

    def here(src, dst, spot):
        return pltpu.make_async_copy(src, dst, lsem.at[spot])

    def pair(src, dst, spot):
        return pltpu.make_async_remote_copy(
            src_ref=src, dst_ref=dst, send_sem=psend.at[spot], recv_sem=precv.at[spot],
            device_id=peer["c"], device_id_type=MESH,
        )

    def far(src, dst, item, stage, bit):
        return pltpu.make_async_remote_copy(
            src_ref=src, dst_ref=dst, send_sem=rsend.at[item, stage], recv_sem=rrecv.at[item, stage],
            device_id=peer[bit], device_id_type=MESH,
        )

    joint_in = [here(jw.at[:, pl.ds(j * D, D)], wb1.at[pl.ds(j * D, D), :], j) for j in range(3)]
    out_in = here(ow, wo, 3)
    up_in = here(uw, wb2, 4)
    for copy in joint_in + [out_in, up_in]:
        copy.start()

    barrier = pltpu.get_barrier_semaphore()
    for name in "cxylh":
        pl.semaphore_signal(barrier, inc=1, device_id=peer[name], device_id_type=MESH)
    pl.semaphore_wait(barrier, 5)

    edge = pair(hid.at[pl.ds(BLOCK - 16, 16), :], hin, 0)
    edge.start()
    fa[8 : BLOCK + 8, :] = hid[...].astype(F32)
    flags = tho[...].astype(F32)
    tht[...] = jnp.broadcast_to(flags, (128, BLOCK)).T
    first_start = pl.multiple_of(jnp.maximum(base - 256, 0), 128)
    for j, start in enumerate((first_start, base, base + 256)):
        start = pl.multiple_of(start, 128)
        piece = seg[:, pl.ds(start, 256)].astype(F32)
        ksg[256 * j : 256 * j + 256, :] = jnp.broadcast_to(piece, (128, 256)).T
    limit = LEN - pad[0]
    for i in range(4):
        spot = lax.broadcasted_iota(jnp.int32, (WINDOW, 128), 0)
        lane = lax.broadcasted_iota(jnp.int32, (WINDOW, 128), 1)
        key_place = spot + (base - 256 + 128 * i)
        query_place = lane + (base + 128 * i)
        query_segment = seg[:, pl.ds(pl.multiple_of(base + 128 * i, 128), 128)].astype(F32)
        seen = (
            (key_place <= query_place)
            & (ksg[128 * i : 128 * i + WINDOW, :] == query_segment)
            & ((key_place < limit) | (key_place == query_place))
            & (key_place >= 0)
        )
        mask[i] = jnp.where(seen, 0.0, NEGATIVE)
    edge.wait()
    fa[0:8, :] = jnp.broadcast_to(hin[15:16, :].astype(F32) * core_f, (8, D))
    for s in range(8):
        inputs = fa[8 + 64 * s : 72 + 64 * s, :]
        previous = fa[7 + 64 * s : 71 + 64 * s, :]
        mixed = inputs + wide(tht[64 * s : 64 * s + 64, :], 6) * (previous - inputs)
        fb[64 * s : 64 * s + 64, :] = mixed
        scaled, _ = row_norm(mixed)
        nb[64 * s : 64 * s + 64, :] = (scaled * small[0:1, :] + small[1:2, :]).astype(BF16)
    spill = here(fb, hg, 7)
    spill.start()
    st[core] = nb[...].T
    keep_normed = here(st.at[core], nth.at[core], 9)
    send_normed = pair(st.at[core], nth.at[core], 1)
    keep_normed.start()
    send_normed.start()

    for copy in joint_in:
        copy.wait()

    @pl.loop(0, 3)
    def _(n):
        cols = pl.ds(pl.multiple_of(256 * n, 256), 256)
        kk[256:, cols] = nn(nb[...], wb1[768:1536, cols]).astype(BF16)
        vv[256:, cols] = (nn(nb[...], wb1[1536:2304, cols]) + small[3:4, cols]).astype(BF16)

    send_keys = pair(kk.at[pl.ds(BLOCK, 256), :], kk.at[pl.ds(0, 256), :], 2)
    send_values = pair(vv.at[pl.ds(BLOCK, 256), :], vv.at[pl.ds(0, 256), :], 3)
    send_keys.start()
    send_values.start()

    @pl.loop(0, 3)
    def _(n):
        cols = pl.ds(pl.multiple_of(256 * n, 256), 256)
        query = (nn(nb[...], wb1[0:768, cols]) + small[2:3, cols]).astype(BF16)
        q[:, cols] = (query.astype(F32) * 0.125).astype(BF16)

    down_in = here(dw, wb1, 5)
    down_in.start()
    for j in (1, 2):
        kt[:, 256 * j : 256 * j + 256] = kk[256 * j : 256 * j + 256, :].T
        vt[:, 256 * j : 256 * j + 256] = vv[256 * j : 256 * j + 256, :].T
    send_keys.wait()
    send_values.wait()
    kt[:, 0:256] = kk[0:256, :].T
    vt[:, 0:256] = vv[0:256, :].T

    @pl.loop(0, 6)
    def _(p):
        cols = pl.ds(pl.multiple_of(128 * p, 128), 128)
        lane = lax.broadcasted_iota(jnp.int32, (128, 128), 1)
        for i in range(4):
            rows = slice(128 * i, 128 * i + 128)
            keys = slice(128 * i, 128 * i + WINDOW)
            queries = split_pair(q[rows, cols], lane)
            scores = nt(kk[keys, cols], queries) + wide(mask[i], 2)
            highest = jnp.max(scores, axis=0, keepdims=True)
            weights = jnp.exp(scores - highest)
            inverse = 1.0 / jnp.sum(weights, axis=0, keepdims=True)
            low = weights.astype(BF16)
            ps[4 * p + i] = low
            il[4 * p + i] = jnp.broadcast_to(inverse, (8, 256))
            at[core, cols, rows] = join_pair(nn(vt[cols, keys], low) * inverse).astype(BF16)

    send_attended = pair(at.at[core], at.at[core], 4)
    send_attended.start()
    att[...] = at[core].T

    out_in.wait()
    spill.wait()

    @pl.loop(0, 3)
    def _(n):
        cols = pl.ds(pl.multiple_of(256 * n, 256), 256)
        fb[:, cols] = fb[:, cols] + nn(att[...], wo[:, cols]) + small[4:5, cols]

    for s in range(8):
        rows = slice(64 * s, 64 * s + 64)
        scaled, _ = row_norm(fb[rows, :])
        nb[rows, :] = (scaled * small[5:6, :] + small[6:7, :]).astype(BF16)
    keep_normed.wait()
    send_normed.wait_send()
    st[core] = nb[...].T
    send_second = pair(st.at[core], st.at[core], 5)
    send_second.start()
    send_cot = pair(cot.at[:, pl.ds(other_half, PIECE)], cotp, 6)
    send_cot.start()

    up_in.wait()
    down_in.wait()
    fa[...] = jnp.zeros_like(fa)

    def act_copy(f):
        cols = pl.ds(pl.multiple_of(256 * f, 256), 256)
        return pair(act.at[:, cols], xx.at[:, cols], 8 + f)

    @pl.loop(0, 12)
    def _(f):
        cols = pl.ds(pl.multiple_of(256 * f, 256), 256)
        up_part = wb2[:, cols]
        units = nn(nb[...], up_part) + small[pl.ds(8 + f // 3, 1), pl.ds(pl.multiple_of(256 * lax.rem(f, 3), 256), 256)]
        back = nt(cot[...], wb1[cols, :])
        total = jnp.zeros((8, 256), F32)
        for s in range(8):
            rows = slice(64 * s, 64 * s + 64)
            value = units[rows, :]
            square = value * value
            gate = 0.5 + 0.5 * jnp.tanh(value * (GELU_SCALE + GELU_SCALE * GELU_CUBIC * square))
            result = value * gate
            slope = gate + 2.0 * result * (1.0 - gate) * (GELU_SCALE + 3.0 * GELU_SCALE * GELU_CUBIC * square)
            grad = back[rows, :] * slope
            total = total + fold(grad)
            act[rows, cols] = result.astype(BF16)
            ulo[rows, cols] = grad.astype(BF16)
        ubg[:, cols] = total
        act_copy(f).start()
        fa[0:BLOCK, :] += nt(ulo[:, cols], up_part)

    joint_again = here(jw, wb2.at[:, pl.ds(0, 3 * D)], 6)
    joint_again.start()
    send_units = pair(ulo.at[:, pl.ds(pl.multiple_of(other * 1536, 128), 1536)], ulp, 7)
    send_units.start()

    place = {"h": 0, "l": 1, "y": 2, "x": 3}
    recv = (r1, r2, r3, r4)
    orders = ["xylh", "yxlh", "xylh", "yxlh", "xylh", "yxlh", "xylh", "yxlh"]
    live = {}

    def part(ref, item, stage, mine):
        spot = [slice(None)] * 4
        for bit in orders[item][:stage]:
            spot[place[bit]] = bits[bit]
        bit = orders[item][stage]
        spot[place[bit]] = bits[bit] if mine else 1 - bits[bit]
        return (item,) + tuple(spot)

    def launch(item, stage):
        copy = far(gs.at[part(gs, item, stage, False)], recv[stage].at[item], item, stage, orders[item][stage])
        copy.start()
        live[(item, stage)] = copy

    def advance(item, stage):
        live[(item, stage)].wait()
        spot = part(gs, item, stage, True)
        gs[spot] = gs[spot] + recv[stage][item]
        if stage < 3:
            launch(item, stage + 1)
        else:
            share(item)

    mine = (bits["h"], bits["l"], bits["y"], bits["x"])

    def share(item):
        result = gs.at[(item,) + mine]
        local_copy = here(result, std.at[core, item], 16 + item)
        local_copy.start()
        copy = pair(result, std.at[core, item], 24 + item)
        copy.start()
        live[(item, 4)] = (local_copy, copy)

    def plane_part(z, stage, own):
        first, then = ("x", "y") if z % 2 == 0 else ("y", "x")
        spot = {"x": slice(None), "y": slice(None)}
        if stage == 0:
            spot[first] = bits[first] if own else 1 - bits[first]
        else:
            spot[first] = bits[first]
            spot[then] = bits[then] if own else 1 - bits[then]
        return ((z // 2, z % 2, spot["y"], spot["x"]), first if stage == 0 else then)

    def plane_launch(z, stage):
        spot, bit = plane_part(z, stage, False)
        copy = far(gd.at[spot], (r1d, r2d)[stage].at[z], 8 + z, stage, bit)
        copy.start()
        live[(8 + z, stage)] = copy

    def plane_advance(z, stage):
        live[(8 + z, stage)].wait()
        spot, _ = plane_part(z, stage, True)
        gd[spot] = gd[spot] + (r1d, r2d)[stage][z]
        if stage == 0:
            plane_launch(z, 1)

    def down_launch(stage):
        if stage == 2:
            spot, target, bit = ((slice(None), 1 - bits["l"], bits["y"], bits["x"]), r3d, "l")
        else:
            spot, target, bit = ((1 - bits["h"], bits["l"], bits["y"], bits["x"]), r4d, "h")
        copy = far(gd.at[spot], target, 8, stage, bit)
        copy.start()
        live[("d", stage)] = copy

    def down_advance(stage):
        live[("d", stage)].wait()
        if stage == 2:
            spot = (slice(None), bits["l"], bits["y"], bits["x"])
            gd[spot] = gd[spot] + r3d[...]
            down_launch(3)
        else:
            gd[mine] = gd[mine] + r4d[...]
            local_copy = here(gd.at[mine], dgo.at[core], 15)
            local_copy.start()
            copy = pair(gd.at[mine], dgo.at[core], 23)
            copy.start()
            live[("d", 4)] = (local_copy, copy)

    send_cot.wait()

    @pl.loop(0, 12)
    def _(f):
        act_copy(f).wait()

    for z in range(4):

        @pl.loop(0, 2)
        def _(y, z=z):
            cols = pl.ds(pl.multiple_of(768 * z + 384 * y, 128), 384)
            total = tn(act[:, cols], cot[:, pl.ds(half, PIECE)]) + tn(xx[:, cols], cotp[...])
            gd[z // 2, z % 2, y] = total.astype(BF16).reshape(2, 192, PIECE)

        plane_launch(z, 0)

    send_second.wait()
    send_units.wait()
    for n in range(4):
        start = pl.multiple_of(core * 1536 + 384 * n, 128)
        total = nn(st[core], ulo[:, pl.ds(start, PIECE)]) + nn(st[other], ulp[:, 384 * n : 384 * n + 384])
        gs[n] = total.astype(BF16).reshape(2, 2, 2, 2, TILE, PIECE)
        launch(n, 0)
        plane_advance(n, 0)

    sums = [jnp.zeros((8, D), F32) for _ in range(4)]
    for s in range(8):
        rows = slice(64 * s, 64 * s + 64)
        upstream = fa[rows, :]
        scaled, inverse = row_norm(fb[rows, :])
        direct = cot[rows, :].astype(F32)
        result = direct + row_norm_back(upstream, scaled, inverse, small[5:6, :])
        fa[rows, :] = result
        nb[rows, :] = result.astype(BF16)
        for j, term in enumerate((result, upstream * scaled, upstream, direct)):
            sums[j] = sums[j] + fold(term)
    for j in range(4):
        sv[4 + j : 5 + j, :] = jnp.sum(sums[j], axis=0, keepdims=True)
    for j in range(4):
        sv[8 + j : 9 + j, :] = jnp.sum(ubg[:, 768 * j : 768 * j + 768], axis=0, keepdims=True)
    send_middle = pair(nb.at[:, pl.ds(other_half, PIECE)], mlp, 20)
    send_middle.start()

    @pl.loop(0, 3)
    def _(n):
        cols = pl.ds(pl.multiple_of(256 * n, 256), 256)
        do[:, cols] = nt(nb[...], wo[cols, :]).astype(BF16)

    for z in range(4):
        plane_advance(z, 1)
    down_launch(2)
    send_middle.wait()
    send_attended.wait()
    total = nn(at[core], nb[:, pl.ds(half, PIECE)]) + nn(at[other], mlp[...])
    gs[4] = total.astype(BF16).reshape(2, 2, 2, 2, TILE, PIECE)
    launch(4, 0)
    for n in range(4):
        advance(n, 0)
    send_normed.wait_recv()
    normed_again = here(nth, st, 10)
    normed_again.start()

    def attend_back(p):
        cols = pl.ds(pl.multiple_of(128 * p, 128), 128)
        lane = lax.broadcasted_iota(jnp.int32, (128, 128), 1)
        dka[...] = jnp.zeros_like(dka)
        dva[...] = jnp.zeros_like(dva)
        for i in range(4):
            rows = slice(128 * i, 128 * i + 128)
            keys = slice(128 * i, 128 * i + WINDOW)
            inverse = il[4 * p + i]
            spread = jnp.concatenate(
                [jnp.broadcast_to(inverse[0:1, :128], (HD, 128)), jnp.broadcast_to(inverse[0:1, 128:], (HD, 128))], axis=0
            ).T
            grads = (do[rows, cols].astype(F32) * spread).astype(BF16)
            product = (grads.astype(F32) * att[rows, cols].astype(F32)).T
            delta = jnp.concatenate(
                [jnp.sum(product[:HD], axis=0, keepdims=True), jnp.sum(product[HD:], axis=0, keepdims=True)], axis=1
            )
            grads = split_pair(grads, lane)
            queries = split_pair(q[rows, cols], lane)
            low = ps[4 * p + i]
            score = (low.astype(F32) * (nt(vv[keys, cols], grads) - delta)).astype(BF16)
            xx[rows, cols] = (join_pair(nn(kt[cols, keys], score)) * 0.125).T.astype(BF16)
            dka[keys, :] += nn(score, queries)
            dva[keys, :] += nn(low, grads)
        xx[:, pl.ds(pl.multiple_of(768 + 128 * p, 128), 128)] = dka[256:, :].astype(BF16)
        xx[:, pl.ds(pl.multiple_of(1536 + 128 * p, 128), 128)] = dva[256:, :].astype(BF16)
        hs[0:256, cols] = dka[0:256, :].astype(BF16)
        hs[256:512, cols] = dva[0:256, :].astype(BF16)

    def halo(g):
        return pair(hs.at[:, pl.ds(256 * g, 256)], xx.at[:, pl.ds(2304 + 256 * g, 256)], 32 + g)

    def exchange(g, j):
        start = pl.multiple_of(768 * j + 256 * g + 128 * other, 128)
        return pair(xx.at[:, pl.ds(start, 128)], ulp.at[:, pl.ds(384 * g + 128 * j, 128)], 35 + 3 * g + j)

    def settle(g):
        halo(g).wait()
        for j in (1, 2):
            cols = slice(768 * j + 256 * g, 768 * j + 256 * g + 256)
            come = xx[256 * (j - 1) : 256 * j, 2304 + 256 * g : 2560 + 256 * g]
            xx[256:512, cols] = xx[256:512, cols] + come
        for j in range(3):
            exchange(g, j).start()

    def joint_part(g):
        for j in range(3):
            exchange(g, j).wait()
        own = [xx[:, pl.ds(pl.multiple_of(768 * j + 256 * g + 128 * core, 128), 128)] for j in range(3)]
        total = nn(st[core], jnp.concatenate(own, axis=1)) + nn(st[other], ulp[:, 384 * g : 384 * g + 384])
        gs[5 + g] = total.astype(BF16).reshape(2, 2, 2, 2, TILE, PIECE)
        launch(5 + g, 0)

    for g in range(3):

        @pl.loop(2 * g, 2 * g + 2)
        def _(p):
            attend_back(p)

        halo(g).start()
        if g == 0:
            normed_again.wait()
            down_advance(2)
            advance(4, 0)
            for n in range(4):
                advance(n, 1)
        if g == 1:
            settle(0)
            joint_part(0)
            for n in range(4):
                advance(n, 2)
            advance(4, 1)
            down_advance(3)
    settle(1)
    joint_part(1)
    settle(2)
    joint_part(2)

    @pl.loop(0, 3)
    def _(n):
        cols = pl.ds(pl.multiple_of(256 * n, 256), 256)
        do[:, cols] = (fb[:, cols] + nn(act[...], wb1[:, cols]) + small[7:8, cols]).astype(BF16)

    block_out = here(do, blk, 11)
    block_out.start()
    mixed_again = here(hg, fb, 8)
    mixed_again.start()
    for n in range(4):
        advance(n, 3)
    advance(4, 2)
    advance(5, 0)

    sv[2:3, :] = jnp.sum(xx[:, 0:768].astype(F32), axis=0, keepdims=True)
    sv[3:4, :] = jnp.sum(xx[:, 1536:2304].astype(F32), axis=0, keepdims=True)
    joint_again.wait()

    @pl.loop(0, 3)
    def _(n):
        cols = pl.ds(pl.multiple_of(256 * n, 256), 256)
        fd[0:BLOCK, cols] = nt(xx[:, 0:2304], wb2[cols, 0:2304])

    advance(6, 0)
    advance(7, 0)
    advance(5, 1)
    mixed_again.wait()
    sums = [jnp.zeros((8, D), F32) for _ in range(2)]
    for s in range(8):
        rows = slice(64 * s, 64 * s + 64)
        upstream = fd[rows, :]
        scaled, inverse = row_norm(fb[rows, :])
        grad = fa[rows, :] + row_norm_back(upstream, scaled, inverse, small[0:1, :])
        sums[0] = sums[0] + fold(upstream * scaled)
        sums[1] = sums[1] + fold(upstream)
        carried = wide(tht[rows, :], 6) * grad
        fa[rows, :] = grad - carried
        fd[rows, :] = carried
    fd[BLOCK : BLOCK + 8, :] = jnp.zeros((8, D), F32)
    carry = pair(fd.at[pl.ds(0, 8), :], cin, 21)
    carry.start()
    for j in range(2):
        sv[j : j + 1, :] = jnp.sum(sums[j], axis=0, keepdims=True)
    sv[12:16, :] = jnp.zeros((4, D), F32)
    advance(6, 1)
    advance(7, 1)
    advance(4, 3)
    advance(5, 2)

    def small_copy(stage, name):
        if name == "c":
            return pair(sv, svr.at[stage], 22)
        return far(sv, svr.at[stage], 10, stage - 1 if stage < 3 else stage - 1, name)

    carry.wait()
    fd[BLOCK : BLOCK + 1, :] = cin[0:1, :] * (1.0 - core_f)
    for s in range(8):
        rows = slice(64 * s, 64 * s + 64)
        fa[rows, :] = fa[rows, :] + fd[64 * s + 1 : 64 * s + 65, :]
    hidden_out = here(fa.at[pl.ds(0, BLOCK), :], hg, 12)
    hidden_out.start()

    for stage, name in enumerate("cxylh"):
        if stage == 0:
            copy = pair(sv, svr.at[stage], 22)
        else:
            copy = far(sv, svr.at[stage], 12, stage - 1, name)
        copy.start()
        if stage == 0:
            advance(6, 2)
        if stage == 1:
            advance(7, 2)
        if stage == 2:
            advance(5, 3)
        if stage == 3:
            advance(6, 3)
        if stage == 4:
            advance(7, 3)
        copy.wait()
        sv[...] = sv[...] + svr[stage]

    shift = lax.rem(D - TILE * line + D, D)
    vec[0:8, :] = pltpu.roll(sv[0:8, :], shift, 1)[:, 0:256]
    wide_shift = lax.rem(D - 192 * lax.rem(line, 4), D)
    turned = pltpu.roll(sv[8:16, :], wide_shift, 1)[:, 0:256]
    spot = lax.broadcasted_iota(jnp.int32, (8, 256), 0)
    vec[8:16, :] = jnp.broadcast_to(
        jnp.sum(jnp.where(spot == line // 4, turned, 0.0), axis=0, keepdims=True), (8, 256)
    )

    for item in range(8):
        for copy in live[(item, 4)]:
            copy.wait()
    for copy in live[("d", 4)]:
        copy.wait()
    block_out.wait()
    hidden_out.wait()


def finish_kernel(std, dgo, vec, fg, fs, joint, qb, vb, og, ob, sg, ss, ug, ub, dg, db):
    for c in range(2):
        for n in range(4):
            ug[:, 1536 * c + 384 * n : 1536 * c + 384 * n + 384] = std[c, n].astype(F32)
        og[:, 384 * c : 384 * c + 384] = std[c, 4].astype(F32)
        for g in range(3):
            for j in range(3):
                start = 768 * j + 256 * g + 128 * c
                joint[:, start : start + 128] = std[c, 5 + g, :, 128 * j : 128 * j + 128].astype(F32)
        dg[:, 384 * c : 384 * c + 384] = dgo[c].astype(F32)
    for j, ref in enumerate((fg, fs, qb, vb, ob, sg, ss, db)):
        ref[...] = vec[j, 0:48]
    ub[...] = vec[8, 0:192]


def fused_local(
    hidden, segments, thoughts, padding, cotangent, first_gain, first_shift, joint_weight, query_bias, value_bias,
    output_weight, output_bias, second_gain, second_shift, up_weight, up_bias, down_weight, down_bias,
):
    rows = (first_gain, first_shift, query_bias, value_bias, output_bias, second_gain, second_shift, down_bias)
    small = jnp.concatenate([row.reshape(1, D) for row in rows] + [up_bias.reshape(4, D)], axis=0).astype(F32)
    shape = jax.ShapeDtypeStruct
    vmem, anywhere = (pl.BlockSpec(memory_space=pltpu.VMEM), pl.BlockSpec(memory_space=pl.ANY))
    v = pltpu.VMEM
    dma = pltpu.SemaphoreType.DMA
    blk, hg, std, dgo, vec, _ = pl.pallas_call(
        step_kernel,
        out_shape=(
            shape((BLOCK, D), BF16),
            shape((BLOCK, D), F32),
            shape((2, 8, TILE, PIECE), BF16),
            shape((2, 192, PIECE), BF16),
            shape((16, 256), F32),
            shape((2, D, BLOCK), BF16),
        ),
        in_specs=[vmem, vmem, vmem, pl.BlockSpec(memory_space=pltpu.SMEM), vmem, vmem] + [anywhere] * 4,
        out_specs=(anywhere, anywhere, anywhere, anywhere, vmem, anywhere),
        scratch_shapes=[
            v((FF, D), BF16), v((D, FF), BF16), v((D, D), BF16),
            v((BLOCK + 8, D), F32), v((BLOCK, D), F32), v((BLOCK + 8, D), F32),
            v((BLOCK, D), BF16), v((2, D, BLOCK), BF16), v((BLOCK, D), BF16),
            v((768, D), BF16), v((768, D), BF16), v((D, 768), BF16), v((D, 768), BF16),
            v((24, WINDOW, 256), BF16), v((24, 8, 256), F32), v((2, D, BLOCK), BF16), v((BLOCK, D), BF16),
            v((BLOCK, PIECE), BF16), v((BLOCK, FF), BF16), v((BLOCK, FF), BF16), v((BLOCK, FF), BF16), v((BLOCK, 1536), BF16),
            v((16, D), BF16), v((BLOCK, D), BF16), v((BLOCK, PIECE), BF16), v((BLOCK, D), BF16),
            v((768, 128), F32), v((768, 128), F32),
            v((2, 2, 2, 2, 192, PIECE), BF16), v((8, 2, 2, 2, 2, TILE, PIECE), BF16),
            v((4, 2, 192, PIECE), BF16), v((4, 192, PIECE), BF16), v((2, 192, PIECE), BF16), v((192, PIECE), BF16),
            v((8, 2, 2, 2, TILE, PIECE), BF16), v((8, 2, 2, TILE, PIECE), BF16), v((8, 2, TILE, PIECE), BF16), v((8, TILE, PIECE), BF16),
            v((4, WINDOW, 128), F32), v((768, 128), F32), v((BLOCK, 128), F32), v((8, FF), F32),
            v((16, D), F32), v((5, 16, D), F32), v((8, D), F32),
            dma((24,)), dma((44,)), dma((44,)), dma((13, 4)), dma((13, 4)),
        ],
        compiler_params=pltpu.CompilerParams(collective_id=0, has_side_effects=True, vmem_limit_bytes=66 << 20),
    )(
        hidden[0], segments, thoughts, padding, cotangent[0], small, joint_weight, output_weight, up_weight, down_weight
    )
    vector = shape((TILE,), F32)
    fg, fs, joint, qb, vb, og, ob, sg, ss, ug, ub, dg, db = pl.pallas_call(
        finish_kernel,
        out_shape=(
            vector, vector, shape((TILE, 3 * D), F32), vector, vector, shape((TILE, D), F32), vector, vector, vector,
            shape((TILE, FF), F32), shape((192,), F32), shape((192, D), F32), vector,
        ),
        in_specs=[vmem] * 3,
        out_specs=(vmem,) * 13,
    )(std, dgo, vec)
    return (blk[None], hg[None], fg, fs, joint, qb, vb, og, ob, sg, ss, ug, ub, dg, db)


MESH = pl.DeviceIdType.MESH


def solution(mesh):
    placed = (
        P("rows", "seq", None),
        P("rows", None),
        P("rows", "seq"),
        P("rows"),
        P("rows", "seq", None),
        P(),
        P(),
        P(),
        P(),
        P(),
        P(),
        P(),
        P(),
        P(),
        P(),
        P(),
        P(),
        P(),
    )
    fused = mesh.shape["seq"] == 2 and mesh.shape["rows"] == 16
    return jax.shard_map(
        fused_local if fused else local,
        mesh=mesh,
        in_specs=placed,
        out_specs=(
            P("rows", "seq", None),
            P("rows", "seq", None),
            P("rows"),
            P("rows"),
            P("rows", None),
            P("rows"),
            P("rows"),
            P("rows", None),
            P("rows"),
            P("rows"),
            P("rows"),
            P("rows", None),
            P("rows"),
            P("rows", None),
            P("rows"),
        ),
        check_vma=False,
    )
```

```python
import functools
import math

import jax
import jax.numpy as jnp
from jax import lax
from jax.experimental import pallas as pl
from jax.experimental.pallas import tpu as pltpu
from jax.sharding import PartitionSpec as P

D = 768
H = 12
HD = 64
LEN = 1024


EPSILON = 1e-05
NEGATIVE = -1e30
GELU_SCALE = math.sqrt(2.0 / math.pi)
GELU_CUBIC = 0.044715


def from_behind(value, axis, steps):
    count = lax.axis_size(axis)
    leading, last = (max(0, -steps), min(count, count - steps))
    return lax.ppermute(value, axis, [(source, source + steps) for source in range(leading, last)])


def normalize(values):
    centered = values - jnp.mean(values, axis=-1, keepdims=True)
    inverse = lax.rsqrt(jnp.mean(centered * centered, axis=-1, keepdims=True) + EPSILON)
    return (centered * inverse, inverse)


def normalize_back(upstream, scaled, inverse, gain):
    weighted = upstream * gain
    inner = (
        weighted
        - jnp.mean(weighted, axis=-1, keepdims=True)
        - scaled * jnp.mean(weighted * scaled, axis=-1, keepdims=True)
    )
    return (
        inverse * inner,
        jnp.sum(upstream * scaled, axis=(0, 1)),
        jnp.sum(upstream, axis=(0, 1)),
    )


def gelu_pair(values):
    inner = GELU_SCALE * (values + GELU_CUBIC * values * values * values)
    tangent = jnp.tanh(inner)
    result = 0.5 * values * (1.0 + tangent)
    gelu_slope = 0.5 * (1.0 + tangent) + 0.5 * values * (1.0 - tangent * tangent) * GELU_SCALE * (
        1.0 + 3.0 * GELU_CUBIC * values * values
    )
    return (result, gelu_slope)


def project(values, weight):
    return jnp.einsum("rsd,de->rse", values, weight, preferred_element_type=jnp.float32)


def project_back(values, weight):
    return jnp.einsum("rse,de->rsd", values, weight, preferred_element_type=jnp.float32)


def outer_sum(left, right):
    return jnp.einsum("rsd,rse->de", left, right, preferred_element_type=jnp.float32)


def visibility(query_place, query_segment, key_place, key_segment, limits):
    earlier = key_place[None, None, :] <= query_place[None, :, None]
    shared = key_segment[:, None, :] == query_segment[:, :, None]
    unpadded = (key_place[None, None, :] < limits[:, None, None]) | (
        key_place[None, None, :] == query_place[None, :, None]
    )
    return earlier & shared & unpadded


def local(
    hidden,
    segments,
    thoughts,
    padding,
    cotangent,
    first_gain,
    first_shift,
    joint_weight,
    query_bias,
    value_bias,
    output_weight,
    output_bias,
    second_gain,
    second_shift,
    up_weight,
    up_bias,
    down_weight,
    down_bias,
):
    rows_here, span = (hidden.shape[0], hidden.shape[1])
    scale = HD ** (-0.5)
    key_size = min(512, LEN)
    position_base = lax.axis_index("seq") * span
    query_place = position_base + jnp.arange(span, dtype=jnp.int32)
    query_segment = lax.dynamic_slice_in_dim(segments, position_base, span, 1)
    limits = LEN - padding
    thought_mask = thoughts.astype(jnp.float32)[:, :, None]
    gain_first = first_gain.astype(jnp.float32)
    gain_second = second_gain.astype(jnp.float32)
    incoming = from_behind(hidden[:, span - 1, :], "seq", 1)
    inputs = hidden.astype(jnp.float32)
    previous = jnp.concatenate([incoming.astype(jnp.float32)[:, None, :], inputs[:, :-1]], axis=1)
    mixed = inputs + thought_mask * (previous - inputs)
    first_scaled, first_inverse = normalize(mixed)
    normed = (first_scaled * gain_first + first_shift.astype(jnp.float32)).astype(jnp.bfloat16)
    joint = project(normed, joint_weight)
    query_low = (joint[:, :, :D] + query_bias.astype(jnp.float32)).astype(jnp.bfloat16)
    key_low = joint[:, :, D : 2 * D].astype(jnp.bfloat16)
    value_low = (joint[:, :, 2 * D :] + value_bias.astype(jnp.float32)).astype(jnp.bfloat16)
    query_heads = query_low.reshape(rows_here, span, H, HD)

    def allowed_for(width_keys, offset):
        key_place = offset + jnp.arange(width_keys, dtype=jnp.int32)
        key_segment = lax.dynamic_slice_in_dim(segments, offset, width_keys, 1)
        return visibility(query_place, query_segment, key_place, key_segment, limits)[:, None]

    empty_stats = jnp.zeros((rows_here, H, span), jnp.float32)
    initial = (
        empty_stats + NEGATIVE,
        empty_stats,
        jnp.zeros((rows_here, span, H, HD), jnp.float32),
    )
    key_whole, value_whole = (
        lax.all_gather(key_low, "seq", axis=1, tiled=True),
        lax.all_gather(value_low, "seq", axis=1, tiled=True),
    )
    running = initial
    for first_key in range(0, LEN, key_size):
        attend_key_part = key_whole[:, first_key : first_key + key_size]
        attend_value_part = value_whole[:, first_key : first_key + key_size]
        attend_width_keys = attend_key_part.shape[1]
        attend_allowed = allowed_for(attend_width_keys, jnp.int32(first_key))
        update_highest, update_denominator, update_accumulated = running
        update_key_heads = attend_key_part.reshape(rows_here, attend_width_keys, H, HD)
        update_value_heads = attend_value_part.reshape(rows_here, attend_width_keys, H, HD)
        update_scores = (
            jnp.einsum(
                "rshd,rnhd->rhsn", query_heads, update_key_heads, preferred_element_type=jnp.float32
            )
            * scale
        )
        update_scores = jnp.where(attend_allowed, update_scores, NEGATIVE)
        fresh_max = jnp.maximum(update_highest, jnp.max(update_scores, axis=-1))
        exponent = jnp.where(attend_allowed, jnp.exp(update_scores - fresh_max[..., None]), 0.0)
        factor = jnp.exp(update_highest - fresh_max)
        update_denominator = update_denominator * factor + jnp.sum(exponent, axis=-1)
        weighted = jnp.einsum(
            "rhsn,rnhd->rshd",
            exponent.astype(jnp.bfloat16),
            update_value_heads,
            preferred_element_type=jnp.float32,
        )
        update_accumulated = update_accumulated * jnp.swapaxes(factor, 1, 2)[..., None] + weighted
        running = (fresh_max, update_denominator, update_accumulated)
    highest, denominator, accumulated = running
    attention_out = accumulated / jnp.swapaxes(denominator, 1, 2)[..., None]
    logsum = highest + jnp.log(denominator)
    attended = attention_out.reshape(rows_here, span, D).astype(jnp.bfloat16)
    middle = mixed + project(attended, output_weight) + output_bias.astype(jnp.float32)
    second_scaled, second_inverse = normalize(middle)
    second = (second_scaled * gain_second + second_shift.astype(jnp.float32)).astype(jnp.bfloat16)
    units = project(second, up_weight) + up_bias.astype(jnp.float32)
    activated_full, gelu_slope = gelu_pair(units)
    activated = activated_full.astype(jnp.bfloat16)
    block_output = (
        middle + project(activated, down_weight) + down_bias.astype(jnp.float32)
    ).astype(jnp.bfloat16)
    upstream = cotangent.astype(jnp.float32)
    down_bias_grad = jnp.sum(upstream, axis=(0, 1))
    down_weight_grad = outer_sum(activated, cotangent)
    unit_grad = project_back(cotangent, down_weight) * gelu_slope
    up_bias_grad = jnp.sum(unit_grad, axis=(0, 1))
    unit_low = unit_grad.astype(jnp.bfloat16)
    up_weight_grad = outer_sum(second, unit_low)
    middle_part, second_gain_grad, second_shift_grad = normalize_back(
        project_back(unit_low, up_weight), second_scaled, second_inverse, gain_second
    )
    middle_grad = upstream + middle_part
    output_bias_grad = jnp.sum(middle_grad, axis=(0, 1))
    middle_low = middle_grad.astype(jnp.bfloat16)
    output_weight_grad = outer_sum(attended, middle_low)
    attended_grad = project_back(middle_low, output_weight).astype(jnp.bfloat16)
    grad_heads = attended_grad.reshape(rows_here, span, H, HD)
    delta = jnp.swapaxes(jnp.sum(grad_heads.astype(jnp.float32) * attention_out, axis=-1), 1, 2)

    def attend_back(key_part, value_part, offset):
        width_keys = key_part.shape[1]
        allowed = allowed_for(width_keys, offset)
        key_heads = key_part.reshape(rows_here, width_keys, H, HD)
        value_heads = value_part.reshape(rows_here, width_keys, H, HD)
        scores = (
            jnp.einsum(
                "rshd,rnhd->rhsn", query_heads, key_heads, preferred_element_type=jnp.float32
            )
            * scale
        )
        scores = jnp.where(allowed, scores, NEGATIVE)
        probs = jnp.where(allowed, jnp.exp(scores - logsum[..., None]), 0.0)
        probs_low = probs.astype(jnp.bfloat16)
        value_term = jnp.einsum(
            "rhsn,rshd->rnhd", probs_low, grad_heads, preferred_element_type=jnp.float32
        )
        prob_grad = jnp.einsum(
            "rshd,rnhd->rhsn", grad_heads, value_heads, preferred_element_type=jnp.float32
        )
        score_grad = (probs * (prob_grad - delta[..., None])).astype(jnp.bfloat16)
        query_term = (
            jnp.einsum("rhsn,rnhd->rshd", score_grad, key_heads, preferred_element_type=jnp.float32)
            * scale
        )
        key_term = (
            jnp.einsum(
                "rhsn,rshd->rnhd", score_grad, query_heads, preferred_element_type=jnp.float32
            )
            * scale
        )
        return (
            query_term,
            key_term.reshape(rows_here, width_keys, D),
            value_term.reshape(rows_here, width_keys, D),
        )

    back_keys, back_values = (key_whole, value_whole)
    query_grad = jnp.zeros((rows_here, span, H, HD), jnp.float32)
    key_terms = []
    value_terms = []
    for first_key in range(0, LEN, key_size):
        query_term, key_term, value_term = attend_back(
            back_keys[:, first_key : first_key + key_size],
            back_values[:, first_key : first_key + key_size],
            jnp.int32(first_key),
        )
        query_grad = query_grad + query_term
        key_terms.append(key_term)
        value_terms.append(value_term)
    key_grad, value_grad = (
        lax.psum_scatter(
            jnp.concatenate(key_terms, axis=1).astype(jnp.bfloat16),
            "seq",
            scatter_dimension=1,
            tiled=True,
        ).astype(jnp.float32),
        lax.psum_scatter(
            jnp.concatenate(value_terms, axis=1).astype(jnp.bfloat16),
            "seq",
            scatter_dimension=1,
            tiled=True,
        ).astype(jnp.float32),
    )
    query_grad_low = query_grad.reshape(rows_here, span, D).astype(jnp.bfloat16)
    key_grad_low = key_grad.astype(jnp.bfloat16)
    value_grad_low = value_grad.astype(jnp.bfloat16)
    query_bias_grad = jnp.sum(query_grad_low.astype(jnp.float32), axis=(0, 1))
    value_bias_grad = jnp.sum(value_grad_low.astype(jnp.float32), axis=(0, 1))
    joint_low = jnp.concatenate([query_grad_low, key_grad_low, value_grad_low], axis=-1)
    joint_grad = outer_sum(normed, joint_low)
    mixed_part, first_gain_grad, first_shift_grad = normalize_back(
        project_back(joint_low, joint_weight), first_scaled, first_inverse, gain_first
    )
    mixed_grad = middle_grad + mixed_part
    carried = thought_mask * mixed_grad
    following = from_behind(carried[:, 0, :], "seq", -1)
    hidden_grad = (
        mixed_grad - carried + jnp.concatenate([carried[:, 1:], following[:, None, :]], axis=1)
    )
    (
        first_gain_grad,
        first_shift_grad,
        joint_grad,
        query_bias_grad,
        value_bias_grad,
        output_weight_grad,
        output_bias_grad,
        second_gain_grad,
        second_shift_grad,
        up_weight_grad,
        up_bias_grad,
        down_weight_grad,
        down_bias_grad,
    ) = (
        lax.psum_scatter(
            first_gain_grad.astype(jnp.bfloat16), "rows", scatter_dimension=0, tiled=True
        ).astype(jnp.float32),
        lax.psum_scatter(
            first_shift_grad.astype(jnp.bfloat16), "rows", scatter_dimension=0, tiled=True
        ).astype(jnp.float32),
        lax.psum_scatter(
            joint_grad.astype(jnp.bfloat16), "rows", scatter_dimension=0, tiled=True
        ).astype(jnp.float32),
        lax.psum_scatter(
            query_bias_grad.astype(jnp.bfloat16), "rows", scatter_dimension=0, tiled=True
        ).astype(jnp.float32),
        lax.psum_scatter(
            value_bias_grad.astype(jnp.bfloat16), "rows", scatter_dimension=0, tiled=True
        ).astype(jnp.float32),
        lax.psum_scatter(
            output_weight_grad.astype(jnp.bfloat16), "rows", scatter_dimension=0, tiled=True
        ).astype(jnp.float32),
        lax.psum_scatter(
            output_bias_grad.astype(jnp.bfloat16), "rows", scatter_dimension=0, tiled=True
        ).astype(jnp.float32),
        lax.psum_scatter(
            second_gain_grad.astype(jnp.bfloat16), "rows", scatter_dimension=0, tiled=True
        ).astype(jnp.float32),
        lax.psum_scatter(
            second_shift_grad.astype(jnp.bfloat16), "rows", scatter_dimension=0, tiled=True
        ).astype(jnp.float32),
        lax.psum_scatter(
            up_weight_grad.astype(jnp.bfloat16), "rows", scatter_dimension=0, tiled=True
        ).astype(jnp.float32),
        lax.psum_scatter(
            up_bias_grad.astype(jnp.bfloat16), "rows", scatter_dimension=0, tiled=True
        ).astype(jnp.float32),
        lax.psum_scatter(
            down_weight_grad.astype(jnp.bfloat16), "rows", scatter_dimension=0, tiled=True
        ).astype(jnp.float32),
        lax.psum_scatter(
            down_bias_grad.astype(jnp.bfloat16), "rows", scatter_dimension=0, tiled=True
        ).astype(jnp.float32),
    )
    (
        first_gain_grad,
        first_shift_grad,
        joint_grad,
        query_bias_grad,
        value_bias_grad,
        output_weight_grad,
        output_bias_grad,
        second_gain_grad,
        second_shift_grad,
        up_weight_grad,
        up_bias_grad,
        down_weight_grad,
        down_bias_grad,
    ) = (
        lax.psum(first_gain_grad.astype(jnp.bfloat16), "seq").astype(jnp.float32),
        lax.psum(first_shift_grad.astype(jnp.bfloat16), "seq").astype(jnp.float32),
        lax.psum(joint_grad.astype(jnp.bfloat16), "seq").astype(jnp.float32),
        lax.psum(query_bias_grad.astype(jnp.bfloat16), "seq").astype(jnp.float32),
        lax.psum(value_bias_grad.astype(jnp.bfloat16), "seq").astype(jnp.float32),
        lax.psum(output_weight_grad.astype(jnp.bfloat16), "seq").astype(jnp.float32),
        lax.psum(output_bias_grad.astype(jnp.bfloat16), "seq").astype(jnp.float32),
        lax.psum(second_gain_grad.astype(jnp.bfloat16), "seq").astype(jnp.float32),
        lax.psum(second_shift_grad.astype(jnp.bfloat16), "seq").astype(jnp.float32),
        lax.psum(up_weight_grad.astype(jnp.bfloat16), "seq").astype(jnp.float32),
        lax.psum(up_bias_grad.astype(jnp.bfloat16), "seq").astype(jnp.float32),
        lax.psum(down_weight_grad.astype(jnp.bfloat16), "seq").astype(jnp.float32),
        lax.psum(down_bias_grad.astype(jnp.bfloat16), "seq").astype(jnp.float32),
    )
    return (
        block_output,
        hidden_grad,
        first_gain_grad,
        first_shift_grad,
        joint_grad,
        query_bias_grad,
        value_bias_grad,
        output_weight_grad,
        output_bias_grad,
        second_gain_grad,
        second_shift_grad,
        up_weight_grad,
        up_bias_grad,
        down_weight_grad,
        down_bias_grad,
    )


F32, BF16 = (jnp.float32, jnp.bfloat16)
BLOCK = 512
FF = 3072
PIECE = 384
TILE = 48
WINDOW = 384
PLANE_ORDERS = ["yx", "xy", "yx", "yx"]
UNIT_ORDERS = ["lhyx", "lyhx", "xhyl", "lxhy", "yxlh"]
JOINT_ORDERS = ["xlhy", "yxlh", "yxlh", "lhxy", "lxhy", "xhyl", "xlyh", "yxlh", "lxyh"]
SCHEDULE = [
    ("D", 0, 0), ("U", 0, 0), ("D", 1, 0), ("U", 1, 0), ("D", 2, 0), ("U", 0, 1), ("U", 2, 0), ("D", 0, 1),
    ("D", 3, 0), ("D", 2, 1), ("U", 3, 0), ("D", 1, 1), ("U", 5, 0), ("U", 2, 1), ("U", 10, 0), ("U", 8, 0),
    ("U", 9, 0), ("D", 3, 1), ("U", 4, 0), ("U", 5, 1), ("U", 10, 1), ("U", 3, 1), ("U", 13, 0), ("U", 1, 1),
    ("U", 8, 1), ("U", 11, 0), ("U", 0, 2), ("U", 5, 2), ("U", 9, 1), ("U", 6, 0), ("U", 4, 1), ("U", 3, 2),
    ("U", 7, 0), ("Z", 0, 2), ("U", 13, 1), ("U", 8, 2), ("U", 0, 3), ("U", 12, 0), ("U", 11, 1), ("U", 1, 2),
    ("U", 2, 2), ("U", 9, 2), ("U", 6, 1), ("U", 10, 2), ("U", 5, 3), ("U", 7, 1), ("U", 3, 3), ("U", 13, 2),
    ("U", 8, 3), ("U", 12, 1), ("U", 4, 2), ("U", 11, 2), ("U", 9, 3), ("U", 1, 3), ("U", 2, 3), ("U", 6, 2),
    ("U", 10, 3), ("Z", 0, 3), ("U", 7, 2), ("U", 13, 3), ("U", 12, 2), ("U", 11, 3), ("U", 4, 3), ("U", 6, 3),
    ("U", 7, 3), ("U", 12, 3),
]
PUMPS = [0, 0, 2, 0, 1, 0, 0, 0, 1, 3, 0, 1, 1, 2, 2, 2, 0, 1, 4, 2, 7, 5]


def nn(left, right):
    return lax.dot_general(left, right, (((1,), (0,)), ((), ())), preferred_element_type=F32)


def nt(left, right):
    return lax.dot_general(left, right, (((1,), (1,)), ((), ())), preferred_element_type=F32)


def tn(left, right):
    return lax.dot_general(left, right, (((0,), (0,)), ((), ())), preferred_element_type=F32)


def wide(column, copies):
    return jnp.concatenate([column] * copies, axis=1)


def row_norm(values):
    centered = values - jnp.mean(values, axis=-1, keepdims=True)
    inverse = lax.rsqrt(jnp.mean(centered * centered, axis=-1, keepdims=True) + EPSILON)
    return (centered * inverse, inverse)


def row_norm_back(upstream, scaled, inverse, gain):
    weighted = upstream * gain
    return inverse * (
        weighted
        - jnp.mean(weighted, axis=-1, keepdims=True)
        - scaled * jnp.mean(weighted * scaled, axis=-1, keepdims=True)
    )


def fold(values):
    return jnp.sum(values.reshape(values.shape[0] // 8, 8, values.shape[1]), axis=0)


def split_pair(values, lane):
    zero = jnp.zeros_like(values)
    return jnp.concatenate([jnp.where(lane < HD, values, zero), jnp.where(lane < HD, zero, values)], axis=0)


def join_pair(values):
    return jnp.concatenate([values[:HD, :128], values[HD:, 128:]], axis=0)


def step_kernel(
    hid, seg, tho, pad, cott, v0, v1, v2, v3, v4, v5, v6, v7, v8, jw, ow, uw, dw,
    blk, hg, sout, jout, dout, vout, nth,
    wb1, wb2, wo, fa, fb, fd, nb, st, q, kk, vv, kt, vt, ps, il, at, att, cotp, act, xx, ulo, ulp,
    hin, hs, mlp, do, dka, dva, gd, gs, gj, r1d, r2d, r3d, r4d, r1, r2, r3, r4, j1, j2, j3, j4,
    mask, ksg, tht, ubg, sv, svr, svx, svz, cin, small, hidv, cot, vec, lsem, psend, precv, rsend, rrecv,
):
    core, line = (lax.axis_index("seq"), lax.axis_index("rows"))
    other = 1 - core
    bits = {"x": lax.rem(line, 2), "y": lax.rem(line // 2, 2), "l": lax.rem(line // 4, 2), "h": line // 8}
    peer = {
        "c": (other, line),
        "x": (core, line + 1 - 2 * bits["x"]),
        "y": (core, line + 2 - 4 * bits["y"]),
        "l": (core, line + 4 - 8 * bits["l"]),
        "h": (core, line + 8 - 16 * bits["h"]),
    }
    base = core * BLOCK
    core_f = core.astype(F32)
    half = pl.multiple_of(core * PIECE, 128)
    other_half = pl.multiple_of(other * PIECE, 128)

    def here(src, dst, spot):
        return pltpu.make_async_copy(src, dst, lsem.at[spot])

    def pair(src, dst, spot):
        return pltpu.make_async_remote_copy(
            src_ref=src, dst_ref=dst, send_sem=psend.at[spot], recv_sem=precv.at[spot],
            device_id=peer["c"], device_id_type=MESH,
        )

    def far(src, dst, item, stage, bit):
        return pltpu.make_async_remote_copy(
            src_ref=src, dst_ref=dst, send_sem=rsend.at[item, stage], recv_sem=rrecv.at[item, stage],
            device_id=peer[bit], device_id_type=MESH,
        )

    hidden_in = here(hid, hidv, 13)
    hidden_in.start()
    joint_in = [here(jw.at[:, pl.ds(j * D, D)], wb1.at[pl.ds(j * D, D), :], j) for j in range(3)]
    for j in (1, 2, 0):
        joint_in[j].start()
    out_in = here(ow, wo, 3)
    up_in = here(uw, wb2, 4)
    cot_in = here(cott, cot, 14)

    barrier = pltpu.get_barrier_semaphore()
    across = (core, line + 3 - 2 * bits["x"] - 4 * bits["y"])
    along = (core, line + 12 - 8 * bits["l"] - 16 * bits["h"])
    for device in list(peer.values()) + [across, along]:
        pl.semaphore_signal(barrier, inc=1, device_id=device, device_id_type=MESH)

    for j, ref in enumerate((v0, v1, v2, v3, v4, v5, v6, v7)):
        small[j : j + 1, :] = ref[...].astype(F32).reshape(1, D)
    for j in range(4):
        small[8 + j : 9 + j, :] = v8[D * j : D * j + D].astype(F32).reshape(1, D)
    flags = tho[...].astype(F32)
    tht[...] = jnp.broadcast_to(flags, (128, BLOCK)).T
    hidden_in.wait()
    fa[8 : BLOCK + 8, :] = hidv[...].astype(F32)

    def mix(s):
        inputs = fa[8 + 64 * s : 72 + 64 * s, :]
        previous = fa[7 + 64 * s : 71 + 64 * s, :]
        mixed = inputs + wide(tht[64 * s : 64 * s + 64, :], 6) * (previous - inputs)
        fb[64 * s : 64 * s + 64, :] = mixed
        scaled, _ = row_norm(mixed)
        nb[64 * s : 64 * s + 64, :] = (scaled * small[0:1, :] + small[1:2, :]).astype(BF16)

    def project_rows(rows, out):
        @pl.loop(0, 3)
        def _(n):
            cols = pl.ds(pl.multiple_of(256 * n, 256), 256)
            kk[out, cols] = nn(nb[rows, :], wb1[768:1536, cols]).astype(BF16)
            vv[out, cols] = (nn(nb[rows, :], wb1[1536:2304, cols]) + small[3:4, cols]).astype(BF16)
            query = (nn(nb[rows, :], wb1[0:768, cols]) + small[2:3, cols]).astype(BF16)
            q[rows, cols] = (query.astype(F32) * 0.125).astype(BF16)

    for s in range(4, 8):
        mix(s)
    for copy in joint_in:
        copy.wait()
    for copy in (cot_in, out_in, up_in):
        copy.start()
    project_rows(slice(256, 512), slice(512, 768))
    pl.semaphore_wait(barrier, 7)
    edge = pair(hidv.at[pl.ds(BLOCK - 16, 16), :], hin, 0)
    send_keys = pair(kk.at[pl.ds(BLOCK, 256), :], kk.at[pl.ds(0, 256), :], 2)
    send_values = pair(vv.at[pl.ds(BLOCK, 256), :], vv.at[pl.ds(0, 256), :], 3)
    for copy in (edge, send_keys, send_values):
        copy.start()
    for s in range(1, 4):
        mix(s)
    kt[:, 512:768] = kk[512:768, :].T
    vt[:, 512:768] = vv[512:768, :].T

    first_start = pl.multiple_of(jnp.maximum(base - 256, 0), 128)
    for j, start in enumerate((first_start, base, base + 256)):
        start = pl.multiple_of(start, 128)
        piece = seg[:, pl.ds(start, 256)].astype(F32)
        ksg[256 * j : 256 * j + 256, :] = jnp.broadcast_to(piece, (128, 256)).T
    limit = LEN - pad[0]
    for i in range(4):
        spot = lax.broadcasted_iota(jnp.int32, (WINDOW, 128), 0)
        lane = lax.broadcasted_iota(jnp.int32, (WINDOW, 128), 1)
        key_place = spot + (base - 256 + 128 * i)
        query_place = lane + (base + 128 * i)
        query_segment = seg[:, pl.ds(pl.multiple_of(base + 128 * i, 128), 128)].astype(F32)
        seen = (
            (key_place <= query_place)
            & (ksg[128 * i : 128 * i + WINDOW, :] == query_segment)
            & ((key_place < limit) | (key_place == query_place))
            & (key_place >= 0)
        )
        mask[i] = jnp.where(seen, 0.0, NEGATIVE)

    edge.wait()
    fa[0:8, :] = jnp.broadcast_to(hin[15:16, :].astype(F32) * core_f, (8, D))
    mix(0)
    project_rows(slice(0, 256), slice(256, 512))
    spill = here(fb, hg, 7)
    spill.start()
    down_in = here(dw, wb1, 5)
    down_in.start()
    st[core] = nb[...].T
    keep_normed = here(st.at[core], nth.at[core], 9)
    send_normed = pair(st.at[core], nth.at[core], 1)
    keep_normed.start()
    send_normed.start()
    kt[:, 256:512] = kk[256:512, :].T
    vt[:, 256:512] = vv[256:512, :].T
    send_keys.wait()
    send_values.wait()
    kt[:, 0:256] = kk[0:256, :].T
    vt[:, 0:256] = vv[0:256, :].T

    @pl.loop(0, 6)
    def _(p):
        cols = pl.ds(pl.multiple_of(128 * p, 128), 128)
        lane = lax.broadcasted_iota(jnp.int32, (128, 128), 1)
        spans = [(slice(128 * i, 128 * i + 128), slice(128 * i, 128 * i + WINDOW)) for i in range(4)]
        scores = [nt(kk[keys, cols], split_pair(q[rows, cols], lane)) for rows, keys in spans]
        scores = [scores[i] + wide(mask[i], 2) for i in range(4)]
        highest = [jnp.max(score, axis=0, keepdims=True) for score in scores]
        weights = [jnp.exp(scores[i] - highest[i]) for i in range(4)]
        inverse = [1.0 / jnp.sum(weight, axis=0, keepdims=True) for weight in weights]
        low = [weight.astype(BF16) for weight in weights]
        result = [nn(vt[cols, spans[i][1]], low[i]) for i in range(4)]
        for i in range(4):
            ps[4 * p + i] = low[i]
            il[4 * p + i] = jnp.broadcast_to(inverse[i], (8, 256))
            at[core, cols, spans[i][0]] = join_pair(result[i] * inverse[i]).astype(BF16)

    send_attended = pair(at.at[core], at.at[core], 4)
    send_attended.start()
    att[...] = at[core].T

    out_in.wait()
    spill.wait()

    @pl.loop(0, 3)
    def _(n):
        cols = pl.ds(pl.multiple_of(256 * n, 256), 256)
        fb[:, cols] = fb[:, cols] + nn(att[...], wo[:, cols]) + small[4:5, cols]

    for s in range(8):
        rows = slice(64 * s, 64 * s + 64)
        scaled, _ = row_norm(fb[rows, :])
        nb[rows, :] = (scaled * small[5:6, :] + small[6:7, :]).astype(BF16)
    keep_normed.wait()
    send_normed.wait_send()
    st[core] = nb[...].T
    send_second = pair(st.at[core], st.at[core], 5)
    send_second.start()
    cot_in.wait()
    send_cot = pair(cot.at[:, pl.ds(other_half, PIECE)], cotp, 6)
    send_cot.start()

    place = {"h": 0, "l": 1, "y": 2, "x": 3}
    live, ready = ({}, [])
    orders = UNIT_ORDERS + JOINT_ORDERS
    mine = (bits["h"], bits["l"], bits["y"], bits["x"])

    def refs_of(item):
        return (gs, (r1, r2, r3, r4), item) if item < 5 else (gj, (j1, j2, j3, j4), item - 5)

    def part(item, stage, own):
        spot = [slice(None)] * 4
        for bit in orders[item][:stage]:
            spot[place[bit]] = bits[bit]
        bit = orders[item][stage]
        spot[place[bit]] = bits[bit] if own else 1 - bits[bit]
        return (refs_of(item)[2],) + tuple(spot)

    def launch(item, stage):
        ref, recv, at_item = refs_of(item)
        copy = far(ref.at[part(item, stage, False)], recv[stage].at[at_item], item, stage, orders[item][stage])
        copy.start()
        live[(item, stage)] = copy

    def advance(item, stage):
        live[(item, stage)].wait()
        ref, recv, at_item = refs_of(item)
        spot = part(item, stage, True)
        ref[spot] = ref[spot] + recv[stage][at_item]
        if stage < 3:
            launch(item, stage + 1)
            return
        result = ref.at[(at_item,) + mine]
        target = (sout if item < 5 else jout).at[core, at_item]
        copies = (here(result, target, 16 + item), pair(result, target, 30 + item))
        for copy in copies:
            copy.start()
        live[(item, 4)] = copies

    def plane_part(z, stage, own):
        first, then = PLANE_ORDERS[z]
        spot = {"x": slice(None), "y": slice(None)}
        if stage == 0:
            spot[first] = bits[first] if own else 1 - bits[first]
        else:
            spot[first] = bits[first]
            spot[then] = bits[then] if own else 1 - bits[then]
        return ((z // 2, z % 2, spot["y"], spot["x"]), first if stage == 0 else then)

    def plane_launch(z, stage):
        spot, bit = plane_part(z, stage, False)
        copy = far(gd.at[spot], (r1d, r2d)[stage].at[z], 14 + z, stage, bit)
        copy.start()
        live[("plane", z, stage)] = copy

    def plane_advance(z, stage):
        live[("plane", z, stage)].wait()
        spot, _ = plane_part(z, stage, True)
        gd[spot] = gd[spot] + (r1d, r2d)[stage][z]
        live["planes"] = live.get("planes", 0) + stage
        if stage == 0:
            plane_launch(z, 1)
        elif live["planes"] == 4:
            down_launch(2)

    def down_launch(stage):
        if stage == 2:
            spot, target, bit = ((slice(None), 1 - bits["l"], bits["y"], bits["x"]), r3d, "l")
        else:
            spot, target, bit = ((1 - bits["h"], bits["l"], bits["y"], bits["x"]), r4d, "h")
        copy = far(gd.at[spot], target, 14, stage, bit)
        copy.start()
        live[("d", stage)] = copy

    def down_advance(stage):
        live[("d", stage)].wait()
        if stage == 2:
            spot = (slice(None), bits["l"], bits["y"], bits["x"])
            gd[spot] = gd[spot] + r3d[...]
            down_launch(3)
            return
        gd[mine] = gd[mine] + r4d[...]
        copies = (here(gd.at[mine], dout.at[core], 15), pair(gd.at[mine], dout.at[core], 44))
        for copy in copies:
            copy.start()
        live[("d", 4)] = copies

    def act_copies(z):
        cols = pl.ds(768 * z, 768)
        start = pl.multiple_of(768 * z + PIECE * other, 128)
        return (
            pair(act.at[:, cols], xx.at[:, cols], 10 + z),
            pair(ulo.at[:, pl.ds(start, PIECE)], ulp.at[:, pl.ds(PIECE * z, PIECE)], 14 + z),
        )

    def pump(count):
        for _ in range(min(count, len(ready))):
            name, spot, stage = ready.pop(0)
            if name == "D":
                plane_advance(spot, stage)
            elif name == "Z":
                down_advance(stage)
            else:
                advance(spot, stage)

    ready.extend(SCHEDULE)

    up_in.wait()
    down_in.wait()
    fa[...] = jnp.zeros_like(fa)

    def feed(z):
        @pl.loop(0, 3)
        def _(f):
            cols = pl.ds(pl.multiple_of(768 * z + 256 * f, 256), 256)
            up_part = wb2[:, cols]
            units = nn(nb[...], up_part) + small[8 + z : 9 + z, pl.ds(pl.multiple_of(256 * f, 256), 256)]
            back = nt(cot[...], wb1[cols, :])
            total = jnp.zeros((8, 256), F32)
            for s in range(8):
                rows = slice(64 * s, 64 * s + 64)
                value = units[rows, :]
                square = value * value
                gate = 0.5 + 0.5 * jnp.tanh(value * (GELU_SCALE + GELU_SCALE * GELU_CUBIC * square))
                result = value * gate
                slope = gate + 2.0 * result * (1.0 - gate) * (GELU_SCALE + 3.0 * GELU_SCALE * GELU_CUBIC * square)
                grad = back[rows, :] * slope
                total = total + fold(grad)
                act[rows, cols] = result.astype(BF16)
                ulo[rows, cols] = grad.astype(BF16)
            ubg[:, cols] = total
            fa[0:BLOCK, :] += nt(ulo[:, cols], up_part)

        for copy in act_copies(z):
            copy.start()

    def feed_grads(z):
        if z == 0:
            send_cot.wait()
            send_second.wait()
        for copy in act_copies(z):
            copy.wait()

        @pl.loop(0, 2)
        def _(y):
            cols = pl.ds(pl.multiple_of(768 * z + 384 * y, 128), 384)
            total = tn(act[:, cols], cot[:, pl.ds(half, PIECE)]) + tn(xx[:, cols], cotp[...])
            gd[z // 2, z % 2, y] = total.astype(BF16).reshape(2, 192, PIECE)

        plane_launch(z, 0)
        start = pl.multiple_of(768 * z + PIECE * core, 128)
        total = nn(st[core], ulo[:, pl.ds(start, PIECE)]) + nn(st[other], ulp[:, 384 * z : 384 * z + 384])
        gs[z] = total.astype(BF16).reshape(2, 2, 2, 2, TILE, PIECE)
        launch(z, 0)

    feed(0)
    feed(1)
    feed_grads(0)
    pump(PUMPS[0])
    feed(2)
    feed_grads(1)
    pump(PUMPS[1])
    feed(3)
    joint_again = here(jw, wb2.at[:, pl.ds(0, 3 * D)], 6)
    joint_again.start()
    feed_grads(2)
    pump(PUMPS[2])

    sums = [jnp.zeros((8, D), F32) for _ in range(4)]
    for s in range(8):
        rows = slice(64 * s, 64 * s + 64)
        upstream = fa[rows, :]
        scaled, inverse = row_norm(fb[rows, :])
        direct = cot[rows, :].astype(F32)
        result = direct + row_norm_back(upstream, scaled, inverse, small[5:6, :])
        fa[rows, :] = result
        nb[rows, :] = result.astype(BF16)
        for j, term in enumerate((result, upstream * scaled, upstream, direct)):
            sums[j] = sums[j] + fold(term)
    for j in range(4):
        sv[4 + j : 5 + j, :] = jnp.sum(sums[j], axis=0, keepdims=True)
    for j in range(4):
        sv[8 + j : 9 + j, :] = jnp.sum(ubg[:, 768 * j : 768 * j + 768], axis=0, keepdims=True)
    send_middle = pair(nb.at[:, pl.ds(other_half, PIECE)], mlp, 7)
    send_middle.start()
    pump(PUMPS[3])
    feed_grads(3)
    pump(PUMPS[4])

    @pl.loop(0, 3)
    def _(n):
        cols = pl.ds(pl.multiple_of(256 * n, 256), 256)
        do[:, cols] = nt(nb[...], wo[cols, :]).astype(BF16)

    pump(PUMPS[5])
    send_middle.wait()
    send_attended.wait()
    total = nn(at[core], nb[:, pl.ds(half, PIECE)]) + nn(at[other], mlp[...])
    gs[4] = total.astype(BF16).reshape(2, 2, 2, 2, TILE, PIECE)
    launch(4, 0)
    pump(PUMPS[6])
    send_normed.wait_recv()
    normed_again = here(nth, st, 10)
    normed_again.start()

    def attend_back(p):
        cols = slice(128 * p, 128 * p + 128)
        lane = lax.broadcasted_iota(jnp.int32, (128, 128), 1)
        dka[...] = jnp.zeros_like(dka)
        dva[...] = jnp.zeros_like(dva)
        spans = [(slice(128 * i, 128 * i + 128), slice(128 * i, 128 * i + WINDOW)) for i in range(4)]
        grads, deltas = ([], [])
        for i in range(4):
            rows = spans[i][0]
            inverse = il[4 * p + i]
            spread = jnp.concatenate(
                [jnp.broadcast_to(inverse[0:1, :128], (HD, 128)), jnp.broadcast_to(inverse[0:1, 128:], (HD, 128))], axis=0
            ).T
            grad = (do[rows, cols].astype(F32) * spread).astype(BF16)
            product = (grad.astype(F32) * att[rows, cols].astype(F32)).T
            deltas.append(
                jnp.concatenate(
                    [jnp.sum(product[:HD], axis=0, keepdims=True), jnp.sum(product[HD:], axis=0, keepdims=True)], axis=1
                )
            )
            grads.append(split_pair(grad, lane))
        queries = [split_pair(q[rows, cols], lane) for rows, _ in spans]
        prob_grad = [nt(vv[spans[i][1], cols], grads[i]) for i in range(4)]
        low = [ps[4 * p + i] for i in range(4)]
        value_term = [nn(low[i], grads[i]) for i in range(4)]
        score = [(low[i].astype(F32) * (prob_grad[i] - deltas[i])).astype(BF16) for i in range(4)]
        key_term = [nn(score[i], queries[i]) for i in range(4)]
        query_term = [nn(kt[cols, spans[i][1]], score[i]) for i in range(4)]
        for i in range(4):
            xx[spans[i][0], cols] = (join_pair(query_term[i]) * 0.125).T.astype(BF16)
            dka[spans[i][1], :] += key_term[i]
            dva[spans[i][1], :] += value_term[i]
        xx[:, 768 + 128 * p : 896 + 128 * p] = dka[256:, :].astype(BF16)
        xx[:, 1536 + 128 * p : 1664 + 128 * p] = dva[256:, :].astype(BF16)
        hs[0:256, cols] = dka[0:256, :].astype(BF16)
        hs[256:512, cols] = dva[0:256, :].astype(BF16)

    def halo(g):
        return pair(hs.at[:, pl.ds(256 * g, 256)], hidv.at[:, pl.ds(256 * g, 256)], 18 + g)

    def exchange(g, j):
        start = pl.multiple_of(768 * j + 256 * g + 128 * other, 128)
        return pair(xx.at[:, pl.ds(start, 128)], ulp.at[:, pl.ds(384 * g + 128 * j, 128)], 21 + 3 * g + j)

    def settle(g):
        halo(g).wait()
        for j in (1, 2):
            cols = slice(768 * j + 256 * g, 768 * j + 256 * g + 256)
            come = hidv[256 * (j - 1) : 256 * j, 256 * g : 256 * g + 256]
            xx[256:512, cols] = xx[256:512, cols] + come
        for j in range(3):
            exchange(g, j).start()

    def joint_part(g):
        for j in range(3):
            exchange(g, j).wait()
        own = [xx[:, pl.ds(pl.multiple_of(768 * j + 256 * g + 128 * core, 128), 128)] for j in range(3)]
        total = nn(st[core], jnp.concatenate(own, axis=1)) + nn(st[other], ulp[:, 384 * g : 384 * g + 384])
        total = total.astype(BF16)
        for j in range(3):
            gj[3 * g + j] = total[:, 128 * j : 128 * j + 128].reshape(2, 2, 2, 2, TILE, 128)
            launch(5 + 3 * g + j, 0)

    def normed_back(first, count):
        @pl.loop(0, 3)
        def _(n):
            rows = pl.ds(pl.multiple_of(256 * n, 256), 256)
            spans = [slice(768 * j + 256 * first, 768 * j + 256 * (first + count)) for j in range(3)]
            total = sum(nt(xx[:, span], wb2[rows, span]) for span in spans)
            if first > 0:
                total = total + fd[0:BLOCK, rows]
            fd[0:BLOCK, rows] = total

    def output_part(n):
        cols = slice(256 * n, 256 * n + 256)
        do[:, cols] = (fb[:, cols] + nn(act[...], wb1[:, cols]) + small[7:8, cols]).astype(BF16)

    for p in range(6):
        attend_back(p)
        g = p // 2
        if p % 2 == 1:
            halo(g).start()
        elif p > 0:
            if p == 2:
                normed_again.wait()
            settle(g - 1)
        if p in (3, 5):
            joint_part(g - 1)
        pump(PUMPS[7 + p])

    joint_again.wait()
    normed_back(0, 2)
    settle(2)
    pump(PUMPS[13])

    output_part(0)
    pump(PUMPS[14])
    output_part(1)
    joint_part(2)
    pump(PUMPS[15])
    output_part(2)
    block_out = here(do, blk, 11)
    block_out.start()
    mixed_again = here(hg, fb, 8)
    mixed_again.start()
    pump(PUMPS[16])

    normed_back(2, 1)
    pump(PUMPS[17])
    sv[2:3, :] = jnp.sum(xx[:, 0:768].astype(F32), axis=0, keepdims=True)
    sv[3:4, :] = jnp.sum(xx[:, 1536:2304].astype(F32), axis=0, keepdims=True)
    mixed_again.wait()
    sums = [jnp.zeros((8, D), F32) for _ in range(2)]
    for s in range(8):
        rows = slice(64 * s, 64 * s + 64)
        upstream = fd[rows, :]
        scaled, inverse = row_norm(fb[rows, :])
        grad = fa[rows, :] + row_norm_back(upstream, scaled, inverse, small[0:1, :])
        sums[0] = sums[0] + fold(upstream * scaled)
        sums[1] = sums[1] + fold(upstream)
        carried = wide(tht[rows, :], 6) * grad
        fa[rows, :] = grad - carried
        fd[rows, :] = carried
    carry = pair(fd.at[pl.ds(0, 8), :], cin, 8)
    carry.start()
    for j in range(2):
        sv[j : j + 1, :] = jnp.sum(sums[j], axis=0, keepdims=True)
    sv[12:16, :] = jnp.zeros((4, D), F32)
    small_copy = pair(sv, svr, 9)
    small_copy.start()
    fd[BLOCK : BLOCK + 8, :] = jnp.zeros((8, D), F32)
    pump(PUMPS[18])
    small_copy.wait()
    sv[...] = sv[...] + svr[...]

    def spread_small(slots, spot, names, row):
        slots[spot] = sv[...]
        copies = []
        for d in (1, 2, 3):
            step = sum((names[b][1] * (1 - 2 * bits[names[b][0]])) for b in range(2) if d & (1 << b))
            copies.append(
                pltpu.make_async_remote_copy(
                    src_ref=sv, dst_ref=slots.at[spot], send_sem=rsend.at[row, d], recv_sem=rrecv.at[row, d],
                    device_id=(core, line + step), device_id_type=MESH,
                )
            )
        for copy in copies:
            copy.start()
        return copies

    def gather_small(slots, copies):
        for copy in copies:
            copy.wait()
        sv[...] = (slots[0] + slots[1]) + (slots[2] + slots[3])

    copies = spread_small(svx, lax.rem(line, 4), (("x", 1), ("y", 2)), 18)
    carry.wait()
    fd[BLOCK : BLOCK + 1, :] = cin[0:1, :] * (1.0 - core_f)
    for s in range(8):
        rows = slice(64 * s, 64 * s + 64)
        fa[rows, :] = fa[rows, :] + fd[64 * s + 1 : 64 * s + 65, :]
    hidden_out = here(fa.at[pl.ds(0, BLOCK), :], hg, 12)
    hidden_out.start()
    pump(PUMPS[19])
    gather_small(svx, copies)
    copies = spread_small(svz, line // 4, (("l", 4), ("h", 8)), 19)
    pump(PUMPS[20])
    gather_small(svz, copies)

    shift = lax.rem(D - TILE * line + D, D)
    vec[0:8, :] = pltpu.roll(sv[0:8, :], shift, 1)[:, 0:256]
    wide_shift = lax.rem(D - 192 * lax.rem(line, 4), D)
    turned = pltpu.roll(sv[8:16, :], wide_shift, 1)[:, 0:256]
    spot = lax.broadcasted_iota(jnp.int32, (8, 256), 0)
    vec[8:16, :] = jnp.broadcast_to(
        jnp.sum(jnp.where(spot == line // 4, turned, 0.0), axis=0, keepdims=True), (8, 256)
    )
    vec_out = here(vec, vout, 6)
    vec_out.start()
    pump(len(ready))
    vec_out.wait()
    for item in range(14):
        for copy in live[(item, 4)]:
            copy.wait()
    for copy in live[("d", 4)]:
        copy.wait()
    block_out.wait()
    hidden_out.wait()


def finish_kernel(
    blk, hg, sout, jout, dout, vec,
    blk_out, hg_out, fg, fs, joint_out, qb, vb, og_out, ob, sg, ss, ug_out, ub, dg_out, db,
    sin, jin, din, bin_, hin, joint, og, ug, dg, sem,
):
    def move(src, dst, spot):
        copy = pltpu.make_async_copy(src, dst, sem.at[spot])
        copy.start()
        return copy

    wholes = [move(hg, hin, 9), move(blk, bin_, 10)]
    loads = [move(jout, jin, 0), move(sout, sin, 1), move(dout, din, 2)]
    for j, ref in enumerate((fg, fs, qb, vb, ob, sg, ss, db)):
        ref[...] = vec[j, 0:48]
    ub[...] = vec[8, 0:192]
    wholes[0].wait()
    stores = [move(hin, hg_out, 3)]
    wholes[1].wait()
    stores.append(move(bin_, blk_out, 4))
    loads[0].wait()
    for c in range(2):
        for g in range(3):
            for j in range(3):
                start = 768 * j + 256 * g + 128 * c
                joint[:, start : start + 128] = jin[c, 3 * g + j].astype(F32)
    stores.append(move(joint, joint_out, 5))
    loads[1].wait()
    for c in range(2):
        for n in range(4):
            start = 768 * n + 384 * c
            ug[:, start : start + 384] = sin[c, n].astype(F32)
        og[:, 384 * c : 384 * c + 384] = sin[c, 4].astype(F32)
    stores.append(move(ug, ug_out, 6))
    stores.append(move(og, og_out, 7))
    loads[2].wait()
    for c in range(2):
        dg[:, 384 * c : 384 * c + 384] = din[c].astype(F32)
    stores.append(move(dg, dg_out, 8))
    for copy in stores:
        copy.wait()


def fused_local(
    hidden, segments, thoughts, padding, cotangent, first_gain, first_shift, joint_weight, query_bias, value_bias,
    output_weight, output_bias, second_gain, second_shift, up_weight, up_bias, down_weight, down_bias,
):
    rows = (first_gain, first_shift, query_bias, value_bias, output_bias, second_gain, second_shift, down_bias)
    shape = jax.ShapeDtypeStruct
    vmem, anywhere = (pl.BlockSpec(memory_space=pltpu.VMEM), pl.BlockSpec(memory_space=pl.ANY))
    v = pltpu.VMEM
    dma = pltpu.SemaphoreType.DMA
    blk, hg, sout, jout, dout, vec, _ = pl.pallas_call(
        step_kernel,
        out_shape=(
            shape((BLOCK, D), BF16),
            shape((BLOCK, D), F32),
            shape((2, 5, TILE, PIECE), BF16),
            shape((2, 9, TILE, 128), BF16),
            shape((2, 192, PIECE), BF16),
            shape((16, 256), F32),
            shape((2, D, BLOCK), BF16),
        ),
        in_specs=[anywhere, vmem, vmem, pl.BlockSpec(memory_space=pltpu.SMEM), anywhere] + [vmem] * 9 + [anywhere] * 4,
        out_specs=(anywhere,) * 7,
        scratch_shapes=[
            v((FF, D), BF16), v((D, FF), BF16), v((D, D), BF16),
            v((BLOCK + 8, D), F32), v((BLOCK, D), F32), v((BLOCK + 8, D), F32),
            v((BLOCK, D), BF16), v((2, D, BLOCK), BF16), v((BLOCK, D), BF16),
            v((768, D), BF16), v((768, D), BF16), v((D, 768), BF16), v((D, 768), BF16),
            v((24, WINDOW, 256), BF16), v((24, 8, 256), F32), v((2, D, BLOCK), BF16), v((BLOCK, D), BF16),
            v((BLOCK, PIECE), BF16), v((BLOCK, FF), BF16), v((BLOCK, FF), BF16), v((BLOCK, FF), BF16), v((BLOCK, 1536), BF16),
            v((16, D), BF16), v((BLOCK, D), BF16), v((BLOCK, PIECE), BF16), v((BLOCK, D), BF16),
            v((768, 128), F32), v((768, 128), F32),
            v((2, 2, 2, 2, 192, PIECE), BF16), v((5, 2, 2, 2, 2, TILE, PIECE), BF16), v((9, 2, 2, 2, 2, TILE, 128), BF16),
            v((4, 2, 192, PIECE), BF16), v((4, 192, PIECE), BF16), v((2, 192, PIECE), BF16), v((192, PIECE), BF16),
            v((5, 2, 2, 2, TILE, PIECE), BF16), v((5, 2, 2, TILE, PIECE), BF16), v((5, 2, TILE, PIECE), BF16), v((5, TILE, PIECE), BF16),
            v((9, 2, 2, 2, TILE, 128), BF16), v((9, 2, 2, TILE, 128), BF16), v((9, 2, TILE, 128), BF16), v((9, TILE, 128), BF16),
            v((4, WINDOW, 128), F32), v((768, 128), F32), v((BLOCK, 128), F32), v((8, FF), F32),
            v((16, D), F32), v((16, D), F32), v((4, 16, D), F32), v((4, 16, D), F32), v((8, D), F32), v((16, D), F32), v((BLOCK, D), BF16), v((BLOCK, D), BF16), v((16, 256), F32),
            dma((30,)), dma((45,)), dma((45,)), dma((20, 4)), dma((20, 4)),
        ],
        compiler_params=pltpu.CompilerParams(collective_id=0, has_side_effects=True, vmem_limit_bytes=66 << 20),
    )(
        hidden[0], segments, thoughts, padding, cotangent[0], *rows, up_bias, joint_weight, output_weight, up_weight, down_weight
    )
    vector = shape((TILE,), F32)
    results = pl.pallas_call(
        finish_kernel,
        out_shape=(
            shape((BLOCK, D), BF16), shape((BLOCK, D), F32),
            vector, vector, shape((TILE, 3 * D), F32), vector, vector, shape((TILE, D), F32), vector, vector, vector,
            shape((TILE, FF), F32), shape((192,), F32), shape((192, D), F32), vector,
        ),
        in_specs=[anywhere] * 5 + [vmem],
        out_specs=(
            anywhere, anywhere, vmem, vmem, anywhere, vmem, vmem, anywhere, vmem, vmem, vmem, anywhere, vmem, anywhere, vmem,
        ),
        scratch_shapes=[
            v((2, 5, TILE, PIECE), BF16), v((2, 9, TILE, 128), BF16), v((2, 192, PIECE), BF16), v((BLOCK, D), BF16), v((BLOCK, D), F32),
            v((TILE, 3 * D), F32), v((TILE, D), F32), v((TILE, FF), F32), v((192, D), F32), dma((11,)),
        ],
    )(blk, hg, sout, jout, dout, vec)
    return (results[0][None], results[1][None]) + tuple(results[2:])


MESH = pl.DeviceIdType.MESH


def solution(mesh):
    placed = (
        P("rows", "seq", None),
        P("rows", None),
        P("rows", "seq"),
        P("rows"),
        P("rows", "seq", None),
        P(),
        P(),
        P(),
        P(),
        P(),
        P(),
        P(),
        P(),
        P(),
        P(),
        P(),
        P(),
        P(),
    )
    fused = mesh.shape["seq"] == 2 and mesh.shape["rows"] == 16
    return jax.shard_map(
        fused_local if fused else local,
        mesh=mesh,
        in_specs=placed,
        out_specs=(
            P("rows", "seq", None),
            P("rows", "seq", None),
            P("rows"),
            P("rows"),
            P("rows", None),
            P("rows"),
            P("rows"),
            P("rows", None),
            P("rows"),
            P("rows"),
            P("rows"),
            P("rows", None),
            P("rows"),
            P("rows", None),
            P("rows"),
        ),
        check_vma=False,
    )
```

```python
import functools
import math

import jax
import jax.numpy as jnp
from jax import lax
from jax.experimental import pallas as pl
from jax.experimental.pallas import tpu as pltpu
from jax.sharding import PartitionSpec as P

D = 768
H = 12
HD = 64
LEN = 1024


EPSILON = 1e-05
NEGATIVE = -1e30
GELU_SCALE = math.sqrt(2.0 / math.pi)
GELU_CUBIC = 0.044715


def from_behind(value, axis, steps):
    count = lax.axis_size(axis)
    leading, last = (max(0, -steps), min(count, count - steps))
    return lax.ppermute(value, axis, [(source, source + steps) for source in range(leading, last)])


def normalize(values):
    centered = values - jnp.mean(values, axis=-1, keepdims=True)
    inverse = lax.rsqrt(jnp.mean(centered * centered, axis=-1, keepdims=True) + EPSILON)
    return (centered * inverse, inverse)


def normalize_back(upstream, scaled, inverse, gain):
    weighted = upstream * gain
    inner = (
        weighted
        - jnp.mean(weighted, axis=-1, keepdims=True)
        - scaled * jnp.mean(weighted * scaled, axis=-1, keepdims=True)
    )
    return (
        inverse * inner,
        jnp.sum(upstream * scaled, axis=(0, 1)),
        jnp.sum(upstream, axis=(0, 1)),
    )


def gelu_pair(values):
    inner = GELU_SCALE * (values + GELU_CUBIC * values * values * values)
    tangent = jnp.tanh(inner)
    result = 0.5 * values * (1.0 + tangent)
    gelu_slope = 0.5 * (1.0 + tangent) + 0.5 * values * (1.0 - tangent * tangent) * GELU_SCALE * (
        1.0 + 3.0 * GELU_CUBIC * values * values
    )
    return (result, gelu_slope)


def project(values, weight):
    return jnp.einsum("rsd,de->rse", values, weight, preferred_element_type=jnp.float32)


def project_back(values, weight):
    return jnp.einsum("rse,de->rsd", values, weight, preferred_element_type=jnp.float32)


def outer_sum(left, right):
    return jnp.einsum("rsd,rse->de", left, right, preferred_element_type=jnp.float32)


def visibility(query_place, query_segment, key_place, key_segment, limits):
    earlier = key_place[None, None, :] <= query_place[None, :, None]
    shared = key_segment[:, None, :] == query_segment[:, :, None]
    unpadded = (key_place[None, None, :] < limits[:, None, None]) | (
        key_place[None, None, :] == query_place[None, :, None]
    )
    return earlier & shared & unpadded


def local(
    hidden,
    segments,
    thoughts,
    padding,
    cotangent,
    first_gain,
    first_shift,
    joint_weight,
    query_bias,
    value_bias,
    output_weight,
    output_bias,
    second_gain,
    second_shift,
    up_weight,
    up_bias,
    down_weight,
    down_bias,
):
    rows_here, span = (hidden.shape[0], hidden.shape[1])
    scale = HD ** (-0.5)
    key_size = min(512, LEN)
    position_base = lax.axis_index("seq") * span
    query_place = position_base + jnp.arange(span, dtype=jnp.int32)
    query_segment = lax.dynamic_slice_in_dim(segments, position_base, span, 1)
    limits = LEN - padding
    thought_mask = thoughts.astype(jnp.float32)[:, :, None]
    gain_first = first_gain.astype(jnp.float32)
    gain_second = second_gain.astype(jnp.float32)
    incoming = from_behind(hidden[:, span - 1, :], "seq", 1)
    inputs = hidden.astype(jnp.float32)
    previous = jnp.concatenate([incoming.astype(jnp.float32)[:, None, :], inputs[:, :-1]], axis=1)
    mixed = inputs + thought_mask * (previous - inputs)
    first_scaled, first_inverse = normalize(mixed)
    normed = (first_scaled * gain_first + first_shift.astype(jnp.float32)).astype(jnp.bfloat16)
    joint = project(normed, joint_weight)
    query_low = (joint[:, :, :D] + query_bias.astype(jnp.float32)).astype(jnp.bfloat16)
    key_low = joint[:, :, D : 2 * D].astype(jnp.bfloat16)
    value_low = (joint[:, :, 2 * D :] + value_bias.astype(jnp.float32)).astype(jnp.bfloat16)
    query_heads = query_low.reshape(rows_here, span, H, HD)

    def allowed_for(width_keys, offset):
        key_place = offset + jnp.arange(width_keys, dtype=jnp.int32)
        key_segment = lax.dynamic_slice_in_dim(segments, offset, width_keys, 1)
        return visibility(query_place, query_segment, key_place, key_segment, limits)[:, None]

    empty_stats = jnp.zeros((rows_here, H, span), jnp.float32)
    initial = (
        empty_stats + NEGATIVE,
        empty_stats,
        jnp.zeros((rows_here, span, H, HD), jnp.float32),
    )
    key_whole, value_whole = (
        lax.all_gather(key_low, "seq", axis=1, tiled=True),
        lax.all_gather(value_low, "seq", axis=1, tiled=True),
    )
    running = initial
    for first_key in range(0, LEN, key_size):
        attend_key_part = key_whole[:, first_key : first_key + key_size]
        attend_value_part = value_whole[:, first_key : first_key + key_size]
        attend_width_keys = attend_key_part.shape[1]
        attend_allowed = allowed_for(attend_width_keys, jnp.int32(first_key))
        update_highest, update_denominator, update_accumulated = running
        update_key_heads = attend_key_part.reshape(rows_here, attend_width_keys, H, HD)
        update_value_heads = attend_value_part.reshape(rows_here, attend_width_keys, H, HD)
        update_scores = (
            jnp.einsum(
                "rshd,rnhd->rhsn", query_heads, update_key_heads, preferred_element_type=jnp.float32
            )
            * scale
        )
        update_scores = jnp.where(attend_allowed, update_scores, NEGATIVE)
        fresh_max = jnp.maximum(update_highest, jnp.max(update_scores, axis=-1))
        exponent = jnp.where(attend_allowed, jnp.exp(update_scores - fresh_max[..., None]), 0.0)
        factor = jnp.exp(update_highest - fresh_max)
        update_denominator = update_denominator * factor + jnp.sum(exponent, axis=-1)
        weighted = jnp.einsum(
            "rhsn,rnhd->rshd",
            exponent.astype(jnp.bfloat16),
            update_value_heads,
            preferred_element_type=jnp.float32,
        )
        update_accumulated = update_accumulated * jnp.swapaxes(factor, 1, 2)[..., None] + weighted
        running = (fresh_max, update_denominator, update_accumulated)
    highest, denominator, accumulated = running
    attention_out = accumulated / jnp.swapaxes(denominator, 1, 2)[..., None]
    logsum = highest + jnp.log(denominator)
    attended = attention_out.reshape(rows_here, span, D).astype(jnp.bfloat16)
    middle = mixed + project(attended, output_weight) + output_bias.astype(jnp.float32)
    second_scaled, second_inverse = normalize(middle)
    second = (second_scaled * gain_second + second_shift.astype(jnp.float32)).astype(jnp.bfloat16)
    units = project(second, up_weight) + up_bias.astype(jnp.float32)
    activated_full, gelu_slope = gelu_pair(units)
    activated = activated_full.astype(jnp.bfloat16)
    block_output = (
        middle + project(activated, down_weight) + down_bias.astype(jnp.float32)
    ).astype(jnp.bfloat16)
    upstream = cotangent.astype(jnp.float32)
    down_bias_grad = jnp.sum(upstream, axis=(0, 1))
    down_weight_grad = outer_sum(activated, cotangent)
    unit_grad = project_back(cotangent, down_weight) * gelu_slope
    up_bias_grad = jnp.sum(unit_grad, axis=(0, 1))
    unit_low = unit_grad.astype(jnp.bfloat16)
    up_weight_grad = outer_sum(second, unit_low)
    middle_part, second_gain_grad, second_shift_grad = normalize_back(
        project_back(unit_low, up_weight), second_scaled, second_inverse, gain_second
    )
    middle_grad = upstream + middle_part
    output_bias_grad = jnp.sum(middle_grad, axis=(0, 1))
    middle_low = middle_grad.astype(jnp.bfloat16)
    output_weight_grad = outer_sum(attended, middle_low)
    attended_grad = project_back(middle_low, output_weight).astype(jnp.bfloat16)
    grad_heads = attended_grad.reshape(rows_here, span, H, HD)
    delta = jnp.swapaxes(jnp.sum(grad_heads.astype(jnp.float32) * attention_out, axis=-1), 1, 2)

    def attend_back(key_part, value_part, offset):
        width_keys = key_part.shape[1]
        allowed = allowed_for(width_keys, offset)
        key_heads = key_part.reshape(rows_here, width_keys, H, HD)
        value_heads = value_part.reshape(rows_here, width_keys, H, HD)
        scores = (
            jnp.einsum(
                "rshd,rnhd->rhsn", query_heads, key_heads, preferred_element_type=jnp.float32
            )
            * scale
        )
        scores = jnp.where(allowed, scores, NEGATIVE)
        probs = jnp.where(allowed, jnp.exp(scores - logsum[..., None]), 0.0)
        probs_low = probs.astype(jnp.bfloat16)
        value_term = jnp.einsum(
            "rhsn,rshd->rnhd", probs_low, grad_heads, preferred_element_type=jnp.float32
        )
        prob_grad = jnp.einsum(
            "rshd,rnhd->rhsn", grad_heads, value_heads, preferred_element_type=jnp.float32
        )
        score_grad = (probs * (prob_grad - delta[..., None])).astype(jnp.bfloat16)
        query_term = (
            jnp.einsum("rhsn,rnhd->rshd", score_grad, key_heads, preferred_element_type=jnp.float32)
            * scale
        )
        key_term = (
            jnp.einsum(
                "rhsn,rshd->rnhd", score_grad, query_heads, preferred_element_type=jnp.float32
            )
            * scale
        )
        return (
            query_term,
            key_term.reshape(rows_here, width_keys, D),
            value_term.reshape(rows_here, width_keys, D),
        )

    back_keys, back_values = (key_whole, value_whole)
    query_grad = jnp.zeros((rows_here, span, H, HD), jnp.float32)
    key_terms = []
    value_terms = []
    for first_key in range(0, LEN, key_size):
        query_term, key_term, value_term = attend_back(
            back_keys[:, first_key : first_key + key_size],
            back_values[:, first_key : first_key + key_size],
            jnp.int32(first_key),
        )
        query_grad = query_grad + query_term
        key_terms.append(key_term)
        value_terms.append(value_term)
    key_grad, value_grad = (
        lax.psum_scatter(
            jnp.concatenate(key_terms, axis=1).astype(jnp.bfloat16),
            "seq",
            scatter_dimension=1,
            tiled=True,
        ).astype(jnp.float32),
        lax.psum_scatter(
            jnp.concatenate(value_terms, axis=1).astype(jnp.bfloat16),
            "seq",
            scatter_dimension=1,
            tiled=True,
        ).astype(jnp.float32),
    )
    query_grad_low = query_grad.reshape(rows_here, span, D).astype(jnp.bfloat16)
    key_grad_low = key_grad.astype(jnp.bfloat16)
    value_grad_low = value_grad.astype(jnp.bfloat16)
    query_bias_grad = jnp.sum(query_grad_low.astype(jnp.float32), axis=(0, 1))
    value_bias_grad = jnp.sum(value_grad_low.astype(jnp.float32), axis=(0, 1))
    joint_low = jnp.concatenate([query_grad_low, key_grad_low, value_grad_low], axis=-1)
    joint_grad = outer_sum(normed, joint_low)
    mixed_part, first_gain_grad, first_shift_grad = normalize_back(
        project_back(joint_low, joint_weight), first_scaled, first_inverse, gain_first
    )
    mixed_grad = middle_grad + mixed_part
    carried = thought_mask * mixed_grad
    following = from_behind(carried[:, 0, :], "seq", -1)
    hidden_grad = (
        mixed_grad - carried + jnp.concatenate([carried[:, 1:], following[:, None, :]], axis=1)
    )
    (
        first_gain_grad,
        first_shift_grad,
        joint_grad,
        query_bias_grad,
        value_bias_grad,
        output_weight_grad,
        output_bias_grad,
        second_gain_grad,
        second_shift_grad,
        up_weight_grad,
        up_bias_grad,
        down_weight_grad,
        down_bias_grad,
    ) = (
        lax.psum_scatter(
            first_gain_grad.astype(jnp.bfloat16), "rows", scatter_dimension=0, tiled=True
        ).astype(jnp.float32),
        lax.psum_scatter(
            first_shift_grad.astype(jnp.bfloat16), "rows", scatter_dimension=0, tiled=True
        ).astype(jnp.float32),
        lax.psum_scatter(
            joint_grad.astype(jnp.bfloat16), "rows", scatter_dimension=0, tiled=True
        ).astype(jnp.float32),
        lax.psum_scatter(
            query_bias_grad.astype(jnp.bfloat16), "rows", scatter_dimension=0, tiled=True
        ).astype(jnp.float32),
        lax.psum_scatter(
            value_bias_grad.astype(jnp.bfloat16), "rows", scatter_dimension=0, tiled=True
        ).astype(jnp.float32),
        lax.psum_scatter(
            output_weight_grad.astype(jnp.bfloat16), "rows", scatter_dimension=0, tiled=True
        ).astype(jnp.float32),
        lax.psum_scatter(
            output_bias_grad.astype(jnp.bfloat16), "rows", scatter_dimension=0, tiled=True
        ).astype(jnp.float32),
        lax.psum_scatter(
            second_gain_grad.astype(jnp.bfloat16), "rows", scatter_dimension=0, tiled=True
        ).astype(jnp.float32),
        lax.psum_scatter(
            second_shift_grad.astype(jnp.bfloat16), "rows", scatter_dimension=0, tiled=True
        ).astype(jnp.float32),
        lax.psum_scatter(
            up_weight_grad.astype(jnp.bfloat16), "rows", scatter_dimension=0, tiled=True
        ).astype(jnp.float32),
        lax.psum_scatter(
            up_bias_grad.astype(jnp.bfloat16), "rows", scatter_dimension=0, tiled=True
        ).astype(jnp.float32),
        lax.psum_scatter(
            down_weight_grad.astype(jnp.bfloat16), "rows", scatter_dimension=0, tiled=True
        ).astype(jnp.float32),
        lax.psum_scatter(
            down_bias_grad.astype(jnp.bfloat16), "rows", scatter_dimension=0, tiled=True
        ).astype(jnp.float32),
    )
    (
        first_gain_grad,
        first_shift_grad,
        joint_grad,
        query_bias_grad,
        value_bias_grad,
        output_weight_grad,
        output_bias_grad,
        second_gain_grad,
        second_shift_grad,
        up_weight_grad,
        up_bias_grad,
        down_weight_grad,
        down_bias_grad,
    ) = (
        lax.psum(first_gain_grad.astype(jnp.bfloat16), "seq").astype(jnp.float32),
        lax.psum(first_shift_grad.astype(jnp.bfloat16), "seq").astype(jnp.float32),
        lax.psum(joint_grad.astype(jnp.bfloat16), "seq").astype(jnp.float32),
        lax.psum(query_bias_grad.astype(jnp.bfloat16), "seq").astype(jnp.float32),
        lax.psum(value_bias_grad.astype(jnp.bfloat16), "seq").astype(jnp.float32),
        lax.psum(output_weight_grad.astype(jnp.bfloat16), "seq").astype(jnp.float32),
        lax.psum(output_bias_grad.astype(jnp.bfloat16), "seq").astype(jnp.float32),
        lax.psum(second_gain_grad.astype(jnp.bfloat16), "seq").astype(jnp.float32),
        lax.psum(second_shift_grad.astype(jnp.bfloat16), "seq").astype(jnp.float32),
        lax.psum(up_weight_grad.astype(jnp.bfloat16), "seq").astype(jnp.float32),
        lax.psum(up_bias_grad.astype(jnp.bfloat16), "seq").astype(jnp.float32),
        lax.psum(down_weight_grad.astype(jnp.bfloat16), "seq").astype(jnp.float32),
        lax.psum(down_bias_grad.astype(jnp.bfloat16), "seq").astype(jnp.float32),
    )
    return (
        block_output,
        hidden_grad,
        first_gain_grad,
        first_shift_grad,
        joint_grad,
        query_bias_grad,
        value_bias_grad,
        output_weight_grad,
        output_bias_grad,
        second_gain_grad,
        second_shift_grad,
        up_weight_grad,
        up_bias_grad,
        down_weight_grad,
        down_bias_grad,
    )


F32, BF16 = (jnp.float32, jnp.bfloat16)
BLOCK = 512
FF = 3072
PIECE = 384
TILE = 48
WINDOW = 384
PLANE_ORDERS = ["xy", "yx", "xy", "yx"]
UNIT_ORDERS = ["lyhx", "lhyx", "lyxh", "xylh", "lxyh"]
JOINT_ORDERS = ["yxlh", "lyxh", "yxlh", "xylh", "lyxh", "xhly", "lxyh", "yxlh", "yxlh"]
SCHEDULE = [
    ("D", 0, 0), ("U", 0, 0), ("D", 1, 0), ("D", 0, 1), ("U", 1, 0), ("D", 2, 0), ("U", 0, 1), ("D", 1, 1),
    ("U", 2, 0), ("D", 3, 0), ("U", 1, 1), ("U", 3, 0), ("D", 2, 1), ("U", 0, 2), ("D", 3, 1), ("U", 2, 1),
    ("U", 6, 0), ("U", 8, 0), ("U", 5, 0), ("U", 4, 0), ("U", 10, 0), ("U", 7, 0), ("U", 9, 0), ("U", 0, 3),
    ("U", 1, 2), ("U", 2, 2), ("Z", 0, 2), ("U", 5, 1), ("U", 3, 1), ("U", 10, 1), ("U", 12, 0), ("U", 11, 0),
    ("U", 4, 1), ("U", 2, 3), ("U", 7, 1), ("U", 5, 2), ("U", 13, 0), ("U", 1, 3), ("U", 6, 1), ("U", 8, 1),
    ("U", 3, 2), ("U", 9, 1), ("U", 10, 2), ("U", 12, 1), ("Z", 0, 3), ("U", 7, 2), ("U", 11, 1), ("U", 5, 3),
    ("S", 0, 0), ("U", 8, 2), ("U", 13, 1), ("U", 6, 2), ("U", 3, 3), ("U", 12, 2), ("U", 4, 2), ("U", 9, 2),
    ("U", 10, 3), ("U", 7, 3), ("U", 11, 2), ("S", 0, 1), ("U", 8, 3), ("U", 6, 3), ("U", 13, 2), ("U", 12, 3),
    ("U", 9, 3), ("U", 11, 3), ("U", 4, 3), ("U", 13, 3),
]
PUMPS = [0, 0, 0, 0, 2, 0, 1, 1, 1, 1, 1, 0, 2, 0, 1, 2, 2, 2, 6, 4, 2, 2]


def nn(left, right):
    return lax.dot_general(left, right, (((1,), (0,)), ((), ())), preferred_element_type=F32)


def nt(left, right):
    return lax.dot_general(left, right, (((1,), (1,)), ((), ())), preferred_element_type=F32)


def tn(left, right):
    return lax.dot_general(left, right, (((0,), (0,)), ((), ())), preferred_element_type=F32)


def wide(column, copies):
    return jnp.concatenate([column] * copies, axis=1)


def row_norm(values):
    centered = values - jnp.mean(values, axis=-1, keepdims=True)
    inverse = lax.rsqrt(jnp.mean(centered * centered, axis=-1, keepdims=True) + EPSILON)
    return (centered * inverse, inverse)


def row_norm_back(upstream, scaled, inverse, gain):
    weighted = upstream * gain
    return inverse * (
        weighted
        - jnp.mean(weighted, axis=-1, keepdims=True)
        - scaled * jnp.mean(weighted * scaled, axis=-1, keepdims=True)
    )


def fold(values):
    return jnp.sum(values.reshape(values.shape[0] // 8, 8, values.shape[1]), axis=0)


def split_pair(values, lane):
    zero = jnp.zeros_like(values)
    return jnp.concatenate([jnp.where(lane < HD, values, zero), jnp.where(lane < HD, zero, values)], axis=0)


def join_pair(values):
    return jnp.concatenate([values[:HD, :128], values[HD:, 128:]], axis=0)


def step_kernel(
    hid, seg, tho, pad, cott, v0, v1, v2, v3, v4, v5, v6, v7, v8, jw, ow, uw, dw,
    blk, hg, sout, jout, dout, vout, nth,
    wb1, wb2, wo, fa, fb, fd, nb, st, q, kk, vv, kt, vt, ps, il, at, att, cotp, act, xx, ulo, ulp,
    hin, hs, mlp, do, dka, dva, gd, gs, gj, r1d, r2d, r3d, r4d, r1, r2, r3, r4, j1, j2, j3, j4,
    mask, ksg, tht, ubg, sv, svr, svx, svz, cin, small, hidv, cot, vec, lsem, psend, precv, rsend, rrecv,
):
    core, line = (lax.axis_index("seq"), lax.axis_index("rows"))
    other = 1 - core
    bits = {"x": lax.rem(line, 2), "y": lax.rem(line // 2, 2), "l": lax.rem(line // 4, 2), "h": line // 8}
    peer = {
        "c": (other, line),
        "x": (core, line + 1 - 2 * bits["x"]),
        "y": (core, line + 2 - 4 * bits["y"]),
        "l": (core, line + 4 - 8 * bits["l"]),
        "h": (core, line + 8 - 16 * bits["h"]),
    }
    base = core * BLOCK
    core_f = core.astype(F32)
    half = pl.multiple_of(core * PIECE, 128)
    other_half = pl.multiple_of(other * PIECE, 128)

    def here(src, dst, spot):
        return pltpu.make_async_copy(src, dst, lsem.at[spot])

    def pair(src, dst, spot):
        return pltpu.make_async_remote_copy(
            src_ref=src, dst_ref=dst, send_sem=psend.at[spot], recv_sem=precv.at[spot],
            device_id=peer["c"], device_id_type=MESH,
        )

    def far(src, dst, group, spot, bit):
        return pltpu.make_async_remote_copy(
            src_ref=src, dst_ref=dst, send_sem=rsend.at[group], recv_sem=rrecv.at[spot],
            device_id=peer[bit], device_id_type=MESH,
        )

    hidden_in = here(hid, hidv, 13)
    hidden_in.start()
    joint_in = [here(jw.at[:, pl.ds(j * D, D)], wb1.at[pl.ds(j * D, D), :], j) for j in range(3)]
    for j in (1, 2, 0):
        joint_in[j].start()
    out_in = here(ow, wo, 3)
    up_in = here(uw, wb2, 4)
    cot_in = here(cott, cot, 14)

    barrier = pltpu.get_barrier_semaphore()
    across = (core, line + 3 - 2 * bits["x"] - 4 * bits["y"])
    along = (core, line + 12 - 8 * bits["l"] - 16 * bits["h"])
    for device in list(peer.values()) + [across, along]:
        pl.semaphore_signal(barrier, inc=1, device_id=device, device_id_type=MESH)

    for j, ref in enumerate((v0, v1, v2, v3, v4, v5, v6, v7)):
        small[j : j + 1, :] = ref[...].astype(F32).reshape(1, D)
    for j in range(4):
        small[8 + j : 9 + j, :] = v8[D * j : D * j + D].astype(F32).reshape(1, D)
    flags = tho[...].astype(F32)
    tht[...] = jnp.broadcast_to(flags, (128, BLOCK)).T
    hidden_in.wait()
    fa[8 : BLOCK + 8, :] = hidv[...].astype(F32)

    def mix(s):
        inputs = fa[8 + 64 * s : 72 + 64 * s, :]
        previous = fa[7 + 64 * s : 71 + 64 * s, :]
        mixed = inputs + wide(tht[64 * s : 64 * s + 64, :], 6) * (previous - inputs)
        fb[64 * s : 64 * s + 64, :] = mixed
        scaled, _ = row_norm(mixed)
        nb[64 * s : 64 * s + 64, :] = (scaled * small[0:1, :] + small[1:2, :]).astype(BF16)

    def project_rows(rows, out):
        @pl.loop(0, 3)
        def _(n):
            cols = pl.ds(pl.multiple_of(256 * n, 256), 256)
            kk[out, cols] = nn(nb[rows, :], wb1[768:1536, cols]).astype(BF16)
            vv[out, cols] = (nn(nb[rows, :], wb1[1536:2304, cols]) + small[3:4, cols]).astype(BF16)
            query = (nn(nb[rows, :], wb1[0:768, cols]) + small[2:3, cols]).astype(BF16)
            q[rows, cols] = (query.astype(F32) * 0.125).astype(BF16)

    for s in range(4, 8):
        mix(s)
    for copy in joint_in:
        copy.wait()
    for copy in (cot_in, out_in, up_in):
        copy.start()
    project_rows(slice(256, 512), slice(512, 768))
    pl.semaphore_wait(barrier, 7)
    edge = pair(hidv.at[pl.ds(BLOCK - 16, 16), :], hin, 0)
    send_keys = pair(kk.at[pl.ds(BLOCK, 256), :], kk.at[pl.ds(0, 256), :], 2)
    send_values = pair(vv.at[pl.ds(BLOCK, 256), :], vv.at[pl.ds(0, 256), :], 3)
    for copy in (edge, send_keys, send_values):
        copy.start()
    for s in range(1, 4):
        mix(s)
    vt[:, 512:768] = vv[512:768, :].T

    first_start = pl.multiple_of(jnp.maximum(base - 256, 0), 128)
    for j, start in enumerate((first_start, base, base + 256)):
        start = pl.multiple_of(start, 128)
        piece = seg[:, pl.ds(start, 256)].astype(F32)
        ksg[256 * j : 256 * j + 256, :] = jnp.broadcast_to(piece, (128, 256)).T
    limit = LEN - pad[0]
    for i in range(4):
        spot = lax.broadcasted_iota(jnp.int32, (WINDOW, 128), 0)
        lane = lax.broadcasted_iota(jnp.int32, (WINDOW, 128), 1)
        key_place = spot + (base - 256 + 128 * i)
        query_place = lane + (base + 128 * i)
        query_segment = seg[:, pl.ds(pl.multiple_of(base + 128 * i, 128), 128)].astype(F32)
        seen = (
            (key_place <= query_place)
            & (ksg[128 * i : 128 * i + WINDOW, :] == query_segment)
            & ((key_place < limit) | (key_place == query_place))
            & (key_place >= 0)
        )
        mask[i] = jnp.where(seen, 0.0, NEGATIVE)

    edge.wait()
    fa[0:8, :] = jnp.broadcast_to(hin[15:16, :].astype(F32) * core_f, (8, D))
    mix(0)
    project_rows(slice(0, 256), slice(256, 512))
    spill = here(fb, hg, 7)
    spill.start()
    down_in = here(dw, wb1, 5)
    down_in.start()
    vt[:, 256:512] = vv[256:512, :].T
    send_keys.wait()
    send_values.wait()
    vt[:, 0:256] = vv[0:256, :].T

    @pl.loop(0, 6)
    def _(p):
        cols = pl.ds(pl.multiple_of(128 * p, 128), 128)
        lane = lax.broadcasted_iota(jnp.int32, (128, 128), 1)
        spans = [(slice(128 * i, 128 * i + 128), slice(128 * i, 128 * i + WINDOW)) for i in range(4)]
        scores = [nt(kk[keys, cols], split_pair(q[rows, cols], lane)) for rows, keys in spans]
        scores = [scores[i] + wide(mask[i], 2) for i in range(4)]
        highest = [jnp.max(score, axis=0, keepdims=True) for score in scores]
        weights = [jnp.exp(scores[i] - highest[i]) for i in range(4)]
        inverse = [1.0 / jnp.sum(weight, axis=0, keepdims=True) for weight in weights]
        low = [weight.astype(BF16) for weight in weights]
        result = [nn(vt[cols, spans[i][1]], low[i]) for i in range(4)]
        for i in range(4):
            ps[4 * p + i] = low[i]
            il[4 * p + i] = jnp.broadcast_to(inverse[i], (8, 256))
            at[core, cols, spans[i][0]] = join_pair(result[i] * inverse[i]).astype(BF16)

    send_attended = pair(at.at[core], at.at[core], 4)
    send_attended.start()
    att[...] = at[core].T

    out_in.wait()
    spill.wait()

    @pl.loop(0, 3)
    def _(n):
        cols = pl.ds(pl.multiple_of(256 * n, 256), 256)
        fb[:, cols] = fb[:, cols] + nn(att[...], wo[:, cols]) + small[4:5, cols]

    for s in range(8):
        rows = slice(64 * s, 64 * s + 64)
        scaled, _ = row_norm(fb[rows, :])
        do[rows, :] = (scaled * small[5:6, :] + small[6:7, :]).astype(BF16)
    st[core] = do[...].T
    send_second = pair(st.at[core], st.at[core], 5)
    send_second.start()
    cot_in.wait()
    send_cot = pair(cot.at[:, pl.ds(other_half, PIECE)], cotp, 6)
    send_cot.start()

    place = {"h": 0, "l": 1, "y": 2, "x": 3}
    live, ready = ({}, [])
    orders = UNIT_ORDERS + JOINT_ORDERS
    mine = (bits["h"], bits["l"], bits["y"], bits["x"])

    def refs_of(item):
        return (gs, (r1, r2, r3, r4), item) if item < 5 else (gj, (j1, j2, j3, j4), item - 5)

    def part(item, stage, own):
        spot = [slice(None)] * 4
        for bit in orders[item][:stage]:
            spot[place[bit]] = bits[bit]
        bit = orders[item][stage]
        spot[place[bit]] = bits[bit] if own else 1 - bits[bit]
        return (refs_of(item)[2],) + tuple(spot)

    def launch(item, stage):
        ref, recv, at_item = refs_of(item)
        group = stage if item < 5 else 4 + stage
        copy = far(ref.at[part(item, stage, False)], recv[stage].at[at_item], group, 4 * item + stage, orders[item][stage])
        copy.start()
        live[(item, stage)] = copy

    def advance(item, stage):
        live[(item, stage)].wait_recv()
        ref, recv, at_item = refs_of(item)
        spot = part(item, stage, True)
        ref[spot] = ref[spot] + recv[stage][at_item]
        if stage < 3:
            launch(item, stage + 1)
            return
        result = ref.at[(at_item,) + mine]
        target = (sout if item < 5 else jout).at[core, at_item]
        for copy in (here(result, target, 16 if item < 5 else 17), pair(result, target, 24 if item < 5 else 25)):
            copy.start()

    def plane_part(z, stage, own):
        first, then = PLANE_ORDERS[z]
        spot = {"x": slice(None), "y": slice(None)}
        if stage == 0:
            spot[first] = bits[first] if own else 1 - bits[first]
        else:
            spot[first] = bits[first]
            spot[then] = bits[then] if own else 1 - bits[then]
        return ((z // 2, z % 2, spot["y"], spot["x"]), first if stage == 0 else then)

    def plane_launch(z, stage):
        spot, bit = plane_part(z, stage, False)
        copy = far(gd.at[spot], (r1d, r2d)[stage].at[z], 8 + stage, 56 + 2 * z + stage, bit)
        copy.start()
        live[("plane", z, stage)] = copy

    def plane_advance(z, stage):
        live[("plane", z, stage)].wait_recv()
        spot, _ = plane_part(z, stage, True)
        gd[spot] = gd[spot] + (r1d, r2d)[stage][z]
        live["planes"] = live.get("planes", 0) + stage
        if stage == 0:
            plane_launch(z, 1)
        elif live["planes"] == 4:
            down_launch(2)

    def down_launch(stage):
        if stage == 2:
            spot, target, bit = ((slice(None), 1 - bits["l"], bits["y"], bits["x"]), r3d, "l")
        else:
            spot, target, bit = ((1 - bits["h"], bits["l"], bits["y"], bits["x"]), r4d, "h")
        copy = far(gd.at[spot], target, 8 + stage, 62 + stage, bit)
        copy.start()
        live[("d", stage)] = copy

    def down_advance(stage):
        live[("d", stage)].wait_recv()
        if stage == 2:
            spot = (slice(None), bits["l"], bits["y"], bits["x"])
            gd[spot] = gd[spot] + r3d[...]
            down_launch(3)
            return
        gd[mine] = gd[mine] + r4d[...]
        copies = (here(gd.at[mine], dout.at[core], 15), pair(gd.at[mine], dout.at[core], 26))
        for copy in copies:
            copy.start()
        live[("d", 4)] = copies

    def act_copy(z, start, width):
        cols = pl.ds(start, width)
        return pair(act.at[:, cols], xx.at[:, cols], 10 + z)

    def unit_copy(z):
        start = pl.multiple_of(768 * z + PIECE * other, 128)
        return pair(ulo.at[:, pl.ds(start, PIECE)], ulp.at[:, pl.ds(PIECE * z, PIECE)], 14 + z)

    def pump(count):
        for _ in range(min(count, len(ready))):
            name, spot, stage = ready.pop(0)
            if name == "D":
                plane_advance(spot, stage)
            elif name == "Z":
                down_advance(stage)
            elif name == "S":
                small_advance(stage)
            else:
                advance(spot, stage)

    ready.extend(SCHEDULE)

    up_in.wait()
    down_in.wait()
    fa[...] = jnp.zeros_like(fa)

    def feed(z, first, last):
        @pl.loop(first, last)
        def _(f):
            cols = pl.ds(pl.multiple_of(768 * z + 256 * f, 256), 256)
            up_part = wb2[:, cols]
            units = nn(do[...], up_part) + small[8 + z : 9 + z, pl.ds(pl.multiple_of(256 * f, 256), 256)]
            back = nt(cot[...], wb1[cols, :])
            total = jnp.zeros((8, 256), F32)
            for s in range(8):
                rows = slice(64 * s, 64 * s + 64)
                value = units[rows, :]
                square = value * value
                gate = 0.5 + 0.5 * jnp.tanh(value * (GELU_SCALE + GELU_SCALE * GELU_CUBIC * square))
                result = value * gate
                slope = gate + 2.0 * result * (1.0 - gate) * (GELU_SCALE + 3.0 * GELU_SCALE * GELU_CUBIC * square)
                grad = back[rows, :] * slope
                total = total + fold(grad)
                act[rows, cols] = result.astype(BF16)
                ulo[rows, cols] = grad.astype(BF16)
            ubg[:, cols] = total
            fa[0:BLOCK, :] += nt(ulo[:, cols], up_part)
            act_copy(z, pl.multiple_of(768 * z + 256 * f, 256), 256).start()

        if last == 3:
            unit_copy(z).start()

    def feed_grads(z):
        if z == 0:
            send_cot.wait()
        act_copy(z, 768 * z, 768).wait()

        @pl.loop(0, 2)
        def _(y):
            cols = pl.ds(pl.multiple_of(768 * z + 384 * y, 128), 384)
            total = tn(act[:, cols], cot[:, pl.ds(half, PIECE)]) + tn(xx[:, cols], cotp[...])
            gd[z // 2, z % 2, y] = total.astype(BF16).reshape(2, 192, PIECE)

        plane_launch(z, 0)
        if z == 0:
            send_second.wait()
        unit_copy(z).wait()
        start = pl.multiple_of(768 * z + PIECE * core, 128)
        total = nn(st[core], ulo[:, pl.ds(start, PIECE)]) + nn(st[other], ulp[:, 384 * z : 384 * z + 384])
        gs[z] = total.astype(BF16).reshape(2, 2, 2, 2, TILE, PIECE)
        launch(z, 0)

    feed(0, 0, 3)
    feed(1, 0, 1)
    feed_grads(0)
    kt[:, 0:BLOCK] = nb[...].T
    keep_normed = here(kt.at[:, pl.ds(0, BLOCK)], nth.at[core], 9)
    send_normed = pair(kt.at[:, pl.ds(0, BLOCK)], nth.at[core], 1)
    keep_normed.start()
    send_normed.start()
    pump(PUMPS[0])
    feed(1, 1, 3)
    pump(PUMPS[1])
    feed(2, 0, 1)
    feed_grads(1)
    pump(PUMPS[2])
    feed(2, 1, 3)
    pump(PUMPS[3])
    feed(3, 0, 1)
    feed_grads(2)
    pump(PUMPS[4])
    feed(3, 1, 3)
    pump(PUMPS[5])
    joint_again = here(jw, wb2.at[:, pl.ds(0, 3 * D)], 6)
    joint_again.start()

    sums = [jnp.zeros((8, D), F32) for _ in range(4)]
    for s in range(8):
        rows = slice(64 * s, 64 * s + 64)
        upstream = fa[rows, :]
        scaled, inverse = row_norm(fb[rows, :])
        direct = cot[rows, :].astype(F32)
        result = direct + row_norm_back(upstream, scaled, inverse, small[5:6, :])
        fa[rows, :] = result
        nb[rows, :] = result.astype(BF16)
        for j, term in enumerate((result, upstream * scaled, upstream, direct)):
            sums[j] = sums[j] + fold(term)
    for j in range(4):
        sv[4 + j : 5 + j, :] = jnp.sum(sums[j], axis=0, keepdims=True)
    for j in range(4):
        sv[8 + j : 9 + j, :] = jnp.sum(ubg[:, 768 * j : 768 * j + 768], axis=0, keepdims=True)
    send_middle = pair(nb.at[:, pl.ds(other_half, PIECE)], mlp, 7)
    send_middle.start()
    pump(PUMPS[6])
    feed_grads(3)
    pump(PUMPS[7])

    @pl.loop(0, 3)
    def _(n):
        cols = pl.ds(pl.multiple_of(256 * n, 256), 256)
        do[:, cols] = nt(nb[...], wo[cols, :]).astype(BF16)

    pump(PUMPS[8])
    send_middle.wait()
    send_attended.wait()
    total = nn(at[core], nb[:, pl.ds(half, PIECE)]) + nn(at[other], mlp[...])
    gs[4] = total.astype(BF16).reshape(2, 2, 2, 2, TILE, PIECE)
    launch(4, 0)
    pump(PUMPS[9])
    keep_normed.wait()
    send_normed.wait()
    for j in range(3):
        kt[:, 256 * j : 256 * j + 256] = kk[256 * j : 256 * j + 256, :].T
    normed_again = here(nth, st, 10)
    normed_again.start()

    def attend_back(p):
        cols = slice(128 * p, 128 * p + 128)
        lane = lax.broadcasted_iota(jnp.int32, (128, 128), 1)
        dka[...] = jnp.zeros_like(dka)
        dva[...] = jnp.zeros_like(dva)
        spans = [(slice(128 * i, 128 * i + 128), slice(128 * i, 128 * i + WINDOW)) for i in range(4)]
        grads, deltas = ([], [])
        for i in range(4):
            rows = spans[i][0]
            inverse = il[4 * p + i]
            spread = jnp.concatenate(
                [jnp.broadcast_to(inverse[0:1, :128], (HD, 128)), jnp.broadcast_to(inverse[0:1, 128:], (HD, 128))], axis=0
            ).T
            grad = (do[rows, cols].astype(F32) * spread).astype(BF16)
            product = (grad.astype(F32) * att[rows, cols].astype(F32)).T
            deltas.append(
                jnp.concatenate(
                    [jnp.sum(product[:HD], axis=0, keepdims=True), jnp.sum(product[HD:], axis=0, keepdims=True)], axis=1
                )
            )
            grads.append(split_pair(grad, lane))
        queries = [split_pair(q[rows, cols], lane) for rows, _ in spans]
        prob_grad = [nt(vv[spans[i][1], cols], grads[i]) for i in range(4)]
        low = [ps[4 * p + i] for i in range(4)]
        value_term = [nn(low[i], grads[i]) for i in range(4)]
        score = [(low[i].astype(F32) * (prob_grad[i] - deltas[i])).astype(BF16) for i in range(4)]
        key_term = [nn(score[i], queries[i]) for i in range(4)]
        query_term = [nn(kt[cols, spans[i][1]], score[i]) for i in range(4)]
        for i in range(4):
            xx[spans[i][0], cols] = (join_pair(query_term[i]) * 0.125).T.astype(BF16)
            dka[spans[i][1], :] += key_term[i]
            dva[spans[i][1], :] += value_term[i]
        xx[:, 768 + 128 * p : 896 + 128 * p] = dka[256:, :].astype(BF16)
        xx[:, 1536 + 128 * p : 1664 + 128 * p] = dva[256:, :].astype(BF16)
        hs[0:256, cols] = dka[0:256, :].astype(BF16)
        hs[256:512, cols] = dva[0:256, :].astype(BF16)

    def halo(g):
        return pair(hs.at[:, pl.ds(256 * g, 256)], hidv.at[:, pl.ds(256 * g, 256)], 18 + g)

    def exchange(g, j):
        start = pl.multiple_of(768 * j + 256 * g + 128 * other, 128)
        return pair(xx.at[:, pl.ds(start, 128)], ulp.at[:, pl.ds(384 * g + 128 * j, 128)], 21 + g)

    def settle(g):
        halo(g).wait()
        for j in (1, 2):
            cols = slice(768 * j + 256 * g, 768 * j + 256 * g + 256)
            come = hidv[256 * (j - 1) : 256 * j, 256 * g : 256 * g + 256]
            xx[256:512, cols] = xx[256:512, cols] + come
        for j in range(3):
            exchange(g, j).start()

    def joint_part(g):
        pair(xx.at[:, pl.ds(0, PIECE)], ulp.at[:, pl.ds(384 * g, PIECE)], 21 + g).wait()
        own = [xx[:, pl.ds(pl.multiple_of(768 * j + 256 * g + 128 * core, 128), 128)] for j in range(3)]
        total = nn(st[core], jnp.concatenate(own, axis=1)) + nn(st[other], ulp[:, 384 * g : 384 * g + 384])
        total = total.astype(BF16)
        for j in range(3):
            gj[3 * g + j] = total[:, 128 * j : 128 * j + 128].reshape(2, 2, 2, 2, TILE, 128)
            launch(5 + 3 * g + j, 0)

    def normed_back(first, count):
        @pl.loop(0, 3)
        def _(n):
            rows = pl.ds(pl.multiple_of(256 * n, 256), 256)
            spans = [slice(768 * j + 256 * first, 768 * j + 256 * (first + count)) for j in range(3)]
            total = sum(nt(xx[:, span], wb2[rows, span]) for span in spans)
            if first > 0:
                total = total + fd[0:BLOCK, rows]
            fd[0:BLOCK, rows] = total

    def output_part(n):
        cols = slice(256 * n, 256 * n + 256)
        do[:, cols] = (fb[:, cols] + nn(act[...], wb1[:, cols]) + small[7:8, cols]).astype(BF16)

    for p in range(6):
        attend_back(p)
        g = p // 2
        if p % 2 == 1:
            halo(g).start()
        elif p > 0:
            if p == 2:
                normed_again.wait()
            settle(g - 1)
        if p in (3, 5):
            joint_part(g - 1)
        pump(PUMPS[10 + p])

    joint_again.wait()
    normed_back(0, 2)
    settle(2)
    pump(PUMPS[16])

    output_part(0)
    pump(PUMPS[17])
    output_part(1)
    joint_part(2)
    pump(PUMPS[18])
    output_part(2)
    block_out = here(do, blk, 11)
    block_out.start()
    mixed_again = here(hg, fb, 8)
    mixed_again.start()
    pump(PUMPS[19])

    normed_back(2, 1)
    pump(PUMPS[20])
    sv[2:3, :] = jnp.sum(xx[:, 0:768].astype(F32), axis=0, keepdims=True)
    sv[3:4, :] = jnp.sum(xx[:, 1536:2304].astype(F32), axis=0, keepdims=True)
    mixed_again.wait()
    sums = [jnp.zeros((8, D), F32) for _ in range(2)]
    for s in range(8):
        rows = slice(64 * s, 64 * s + 64)
        upstream = fd[rows, :]
        scaled, inverse = row_norm(fb[rows, :])
        grad = fa[rows, :] + row_norm_back(upstream, scaled, inverse, small[0:1, :])
        sums[0] = sums[0] + fold(upstream * scaled)
        sums[1] = sums[1] + fold(upstream)
        carried = wide(tht[rows, :], 6) * grad
        fa[rows, :] = grad - carried
        fd[rows, :] = carried
    carry = pair(fd.at[pl.ds(0, 8), :], cin, 8)
    carry.start()
    for j in range(2):
        sv[j : j + 1, :] = jnp.sum(sums[j], axis=0, keepdims=True)
    sv[12:16, :] = jnp.zeros((4, D), F32)
    small_copy = pair(sv, svr, 9)
    small_copy.start()
    fd[BLOCK : BLOCK + 8, :] = jnp.zeros((8, D), F32)
    pump(PUMPS[21])
    small_copy.wait()
    sv[...] = sv[...] + svr[...]

    def spread_small(slots, spot, names, row):
        slots[spot] = sv[...]
        copies = []
        for d in (1, 2, 3):
            step = sum((names[b][1] * (1 - 2 * bits[names[b][0]])) for b in range(2) if d & (1 << b))
            copies.append(
                pltpu.make_async_remote_copy(
                    src_ref=sv, dst_ref=slots.at[spot], send_sem=rsend.at[row + d], recv_sem=rrecv.at[row + 54 + d],
                    device_id=(core, line + step), device_id_type=MESH,
                )
            )
        for copy in copies:
            copy.start()
        return copies

    def small_advance(stage):
        slots = (svx, svz)[stage]
        for copy in live[("s", stage)]:
            copy.wait()
        sv[...] = (slots[0] + slots[1]) + (slots[2] + slots[3])
        if stage == 0:
            live[("s", 1)] = spread_small(svz, line // 4, (("l", 4), ("h", 8)), 14)

    live[("s", 0)] = spread_small(svx, lax.rem(line, 4), (("x", 1), ("y", 2)), 11)
    carry.wait()
    fd[BLOCK : BLOCK + 1, :] = cin[0:1, :] * (1.0 - core_f)
    for s in range(8):
        rows = slice(64 * s, 64 * s + 64)
        fa[rows, :] = fa[rows, :] + fd[64 * s + 1 : 64 * s + 65, :]
    hidden_out = here(fa.at[pl.ds(0, BLOCK), :], hg, 12)
    hidden_out.start()
    pump(len(ready))

    shift = lax.rem(D - TILE * line + D, D)
    vec[0:8, :] = pltpu.roll(sv[0:8, :], shift, 1)[:, 0:256]
    wide_shift = lax.rem(D - 192 * lax.rem(line, 4), D)
    turned = pltpu.roll(sv[8:16, :], wide_shift, 1)[:, 0:256]
    spot = lax.broadcasted_iota(jnp.int32, (8, 256), 0)
    vec[8:16, :] = jnp.broadcast_to(
        jnp.sum(jnp.where(spot == line // 4, turned, 0.0), axis=0, keepdims=True), (8, 256)
    )
    vec_out = here(vec, vout, 6)
    vec_out.start()
    vec_out.wait()
    for group, ref in enumerate((r1, r2, r3, r4, j1, j2, j3, j4, r1d, r2d, r3d, r4d)):
        far(ref, ref, group, 0, "x").wait_send()
    for spot, ref in ((0, sout), (1, jout)):
        here(ref.at[core], ref.at[core], 16 + spot).wait()
        pair(ref.at[core], ref.at[core], 24 + spot).wait()
    for copy in live[("d", 4)]:
        copy.wait()
    block_out.wait()
    hidden_out.wait()


def finish_kernel(
    blk, hg, sout, jout, dout, vec,
    blk_out, hg_out, fg, fs, joint_out, qb, vb, og_out, ob, sg, ss, ug_out, ub, dg_out, db,
    sin, jin, din, bin_, hin, joint, og, ug, dg, sem,
):
    def move(src, dst, spot):
        copy = pltpu.make_async_copy(src, dst, sem.at[spot])
        copy.start()
        return copy

    loads = [move(jout, jin, 0), move(sout, sin, 1), move(dout, din, 2)]
    quarter = BLOCK // 4
    wholes = [move(hg.at[pl.ds(quarter * n, quarter), :], hin.at[pl.ds(quarter * n, quarter), :], 9 + n) for n in range(4)]
    wholes.append(move(blk, bin_, 13))
    for j, ref in enumerate((fg, fs, qb, vb, ob, sg, ss, db)):
        ref[...] = vec[j, 0:48]
    ub[...] = vec[8, 0:192]
    stores = []
    loads[0].wait()
    for c in range(2):
        for g in range(3):
            for j in range(3):
                start = 768 * j + 256 * g + 128 * c
                joint[:, start : start + 128] = jin[c, 3 * g + j].astype(F32)
    stores.append(move(joint, joint_out, 5))
    for n in range(4):
        wholes[n].wait()
        span = pl.ds(quarter * n, quarter)
        stores.append(move(hin.at[span, :], hg_out.at[span, :], 14 + n))
    wholes[4].wait()
    stores.append(move(bin_, blk_out, 4))
    loads[1].wait()
    for c in range(2):
        for n in range(4):
            start = 768 * n + 384 * c
            ug[:, start : start + 384] = sin[c, n].astype(F32)
        og[:, 384 * c : 384 * c + 384] = sin[c, 4].astype(F32)
    stores.append(move(ug, ug_out, 6))
    stores.append(move(og, og_out, 7))
    loads[2].wait()
    for c in range(2):
        dg[:, 384 * c : 384 * c + 384] = din[c].astype(F32)
    stores.append(move(dg, dg_out, 8))
    for copy in stores:
        copy.wait()


def fused_local(
    hidden, segments, thoughts, padding, cotangent, first_gain, first_shift, joint_weight, query_bias, value_bias,
    output_weight, output_bias, second_gain, second_shift, up_weight, up_bias, down_weight, down_bias,
):
    rows = (first_gain, first_shift, query_bias, value_bias, output_bias, second_gain, second_shift, down_bias)
    shape = jax.ShapeDtypeStruct
    vmem, anywhere = (pl.BlockSpec(memory_space=pltpu.VMEM), pl.BlockSpec(memory_space=pl.ANY))
    v = pltpu.VMEM
    dma = pltpu.SemaphoreType.DMA
    blk, hg, sout, jout, dout, vec, _ = pl.pallas_call(
        step_kernel,
        out_shape=(
            shape((BLOCK, D), BF16),
            shape((BLOCK, D), F32),
            shape((2, 5, TILE, PIECE), BF16),
            shape((2, 9, TILE, 128), BF16),
            shape((2, 192, PIECE), BF16),
            shape((16, 256), F32),
            shape((2, D, BLOCK), BF16),
        ),
        in_specs=[anywhere, vmem, vmem, pl.BlockSpec(memory_space=pltpu.SMEM), anywhere] + [vmem] * 9 + [anywhere] * 4,
        out_specs=(anywhere,) * 7,
        scratch_shapes=[
            v((FF, D), BF16), v((D, FF), BF16), v((D, D), BF16),
            v((BLOCK + 8, D), F32), v((BLOCK, D), F32), v((BLOCK + 8, D), F32),
            v((BLOCK, D), BF16), v((2, D, BLOCK), BF16), v((BLOCK, D), BF16),
            v((768, D), BF16), v((768, D), BF16), v((D, 768), BF16), v((D, 768), BF16),
            v((24, WINDOW, 256), BF16), v((24, 8, 256), F32), v((2, D, BLOCK), BF16), v((BLOCK, D), BF16),
            v((BLOCK, PIECE), BF16), v((BLOCK, FF), BF16), v((BLOCK, FF), BF16), v((BLOCK, FF), BF16), v((BLOCK, 1536), BF16),
            v((16, D), BF16), v((BLOCK, D), BF16), v((BLOCK, PIECE), BF16), v((BLOCK, D), BF16),
            v((768, 128), F32), v((768, 128), F32),
            v((2, 2, 2, 2, 192, PIECE), BF16), v((5, 2, 2, 2, 2, TILE, PIECE), BF16), v((9, 2, 2, 2, 2, TILE, 128), BF16),
            v((4, 2, 192, PIECE), BF16), v((4, 192, PIECE), BF16), v((2, 192, PIECE), BF16), v((192, PIECE), BF16),
            v((5, 2, 2, 2, TILE, PIECE), BF16), v((5, 2, 2, TILE, PIECE), BF16), v((5, 2, TILE, PIECE), BF16), v((5, TILE, PIECE), BF16),
            v((9, 2, 2, 2, TILE, 128), BF16), v((9, 2, 2, TILE, 128), BF16), v((9, 2, TILE, 128), BF16), v((9, TILE, 128), BF16),
            v((4, WINDOW, 128), F32), v((768, 128), F32), v((BLOCK, 128), F32), v((8, FF), F32),
            v((16, D), F32), v((16, D), F32), v((4, 16, D), F32), v((4, 16, D), F32), v((8, D), F32), v((16, D), F32), v((BLOCK, D), BF16), v((BLOCK, D), BF16), v((16, 256), F32),
            dma((18,)), dma((27,)), dma((27,)), dma((18,)), dma((72,)),
        ],
        compiler_params=pltpu.CompilerParams(collective_id=0, has_side_effects=True, vmem_limit_bytes=66 << 20),
    )(
        hidden[0], segments, thoughts, padding, cotangent[0], *rows, up_bias, joint_weight, output_weight, up_weight, down_weight
    )
    vector = shape((TILE,), F32)
    results = pl.pallas_call(
        finish_kernel,
        out_shape=(
            shape((BLOCK, D), BF16), shape((BLOCK, D), F32),
            vector, vector, shape((TILE, 3 * D), F32), vector, vector, shape((TILE, D), F32), vector, vector, vector,
            shape((TILE, FF), F32), shape((192,), F32), shape((192, D), F32), vector,
        ),
        in_specs=[anywhere] * 5 + [vmem],
        out_specs=(
            anywhere, anywhere, vmem, vmem, anywhere, vmem, vmem, anywhere, vmem, vmem, vmem, anywhere, vmem, anywhere, vmem,
        ),
        scratch_shapes=[
            v((2, 5, TILE, PIECE), BF16), v((2, 9, TILE, 128), BF16), v((2, 192, PIECE), BF16), v((BLOCK, D), BF16), v((BLOCK, D), F32),
            v((TILE, 3 * D), F32), v((TILE, D), F32), v((TILE, FF), F32), v((192, D), F32), dma((18,)),
        ],
    )(blk, hg, sout, jout, dout, vec)
    return (results[0][None], results[1][None]) + tuple(results[2:])


MESH = pl.DeviceIdType.MESH


def solution(mesh):
    placed = (
        P("rows", "seq", None),
        P("rows", None),
        P("rows", "seq"),
        P("rows"),
        P("rows", "seq", None),
        P(),
        P(),
        P(),
        P(),
        P(),
        P(),
        P(),
        P(),
        P(),
        P(),
        P(),
        P(),
        P(),
    )
    fused = mesh.shape["seq"] == 2 and mesh.shape["rows"] == 16
    return jax.shard_map(
        fused_local if fused else local,
        mesh=mesh,
        in_specs=placed,
        out_specs=(
            P("rows", "seq", None),
            P("rows", "seq", None),
            P("rows"),
            P("rows"),
            P("rows", None),
            P("rows"),
            P("rows"),
            P("rows", None),
            P("rows"),
            P("rows"),
            P("rows"),
            P("rows", None),
            P("rows"),
            P("rows", None),
            P("rows"),
        ),
        check_vma=False,
    )
```

```python
import functools
import math

import jax
import jax.numpy as jnp
from jax import lax
from jax.experimental import pallas as pl
from jax.experimental.pallas import tpu as pltpu
from jax.sharding import PartitionSpec as P

D = 768
H = 12
HD = 64
LEN = 1024


EPSILON = 1e-05
NEGATIVE = -1e30
GELU_SCALE = math.sqrt(2.0 / math.pi)
GELU_CUBIC = 0.044715


def from_behind(value, axis, steps):
    count = lax.axis_size(axis)
    leading, last = (max(0, -steps), min(count, count - steps))
    return lax.ppermute(value, axis, [(source, source + steps) for source in range(leading, last)])


def normalize(values):
    centered = values - jnp.mean(values, axis=-1, keepdims=True)
    inverse = lax.rsqrt(jnp.mean(centered * centered, axis=-1, keepdims=True) + EPSILON)
    return (centered * inverse, inverse)


def normalize_back(upstream, scaled, inverse, gain):
    weighted = upstream * gain
    inner = (
        weighted
        - jnp.mean(weighted, axis=-1, keepdims=True)
        - scaled * jnp.mean(weighted * scaled, axis=-1, keepdims=True)
    )
    return (
        inverse * inner,
        jnp.sum(upstream * scaled, axis=(0, 1)),
        jnp.sum(upstream, axis=(0, 1)),
    )


def gelu_pair(values):
    inner = GELU_SCALE * (values + GELU_CUBIC * values * values * values)
    tangent = jnp.tanh(inner)
    result = 0.5 * values * (1.0 + tangent)
    gelu_slope = 0.5 * (1.0 + tangent) + 0.5 * values * (1.0 - tangent * tangent) * GELU_SCALE * (
        1.0 + 3.0 * GELU_CUBIC * values * values
    )
    return (result, gelu_slope)


def project(values, weight):
    return jnp.einsum("rsd,de->rse", values, weight, preferred_element_type=jnp.float32)


def project_back(values, weight):
    return jnp.einsum("rse,de->rsd", values, weight, preferred_element_type=jnp.float32)


def outer_sum(left, right):
    return jnp.einsum("rsd,rse->de", left, right, preferred_element_type=jnp.float32)


def visibility(query_place, query_segment, key_place, key_segment, limits):
    earlier = key_place[None, None, :] <= query_place[None, :, None]
    shared = key_segment[:, None, :] == query_segment[:, :, None]
    unpadded = (key_place[None, None, :] < limits[:, None, None]) | (
        key_place[None, None, :] == query_place[None, :, None]
    )
    return earlier & shared & unpadded


def local(
    hidden,
    segments,
    thoughts,
    padding,
    cotangent,
    first_gain,
    first_shift,
    joint_weight,
    query_bias,
    value_bias,
    output_weight,
    output_bias,
    second_gain,
    second_shift,
    up_weight,
    up_bias,
    down_weight,
    down_bias,
):
    rows_here, span = (hidden.shape[0], hidden.shape[1])
    scale = HD ** (-0.5)
    key_size = min(512, LEN)
    position_base = lax.axis_index("seq") * span
    query_place = position_base + jnp.arange(span, dtype=jnp.int32)
    query_segment = lax.dynamic_slice_in_dim(segments, position_base, span, 1)
    limits = LEN - padding
    thought_mask = thoughts.astype(jnp.float32)[:, :, None]
    gain_first = first_gain.astype(jnp.float32)
    gain_second = second_gain.astype(jnp.float32)
    incoming = from_behind(hidden[:, span - 1, :], "seq", 1)
    inputs = hidden.astype(jnp.float32)
    previous = jnp.concatenate([incoming.astype(jnp.float32)[:, None, :], inputs[:, :-1]], axis=1)
    mixed = inputs + thought_mask * (previous - inputs)
    first_scaled, first_inverse = normalize(mixed)
    normed = (first_scaled * gain_first + first_shift.astype(jnp.float32)).astype(jnp.bfloat16)
    joint = project(normed, joint_weight)
    query_low = (joint[:, :, :D] + query_bias.astype(jnp.float32)).astype(jnp.bfloat16)
    key_low = joint[:, :, D : 2 * D].astype(jnp.bfloat16)
    value_low = (joint[:, :, 2 * D :] + value_bias.astype(jnp.float32)).astype(jnp.bfloat16)
    query_heads = query_low.reshape(rows_here, span, H, HD)

    def allowed_for(width_keys, offset):
        key_place = offset + jnp.arange(width_keys, dtype=jnp.int32)
        key_segment = lax.dynamic_slice_in_dim(segments, offset, width_keys, 1)
        return visibility(query_place, query_segment, key_place, key_segment, limits)[:, None]

    empty_stats = jnp.zeros((rows_here, H, span), jnp.float32)
    initial = (
        empty_stats + NEGATIVE,
        empty_stats,
        jnp.zeros((rows_here, span, H, HD), jnp.float32),
    )
    key_whole, value_whole = (
        lax.all_gather(key_low, "seq", axis=1, tiled=True),
        lax.all_gather(value_low, "seq", axis=1, tiled=True),
    )
    running = initial
    for first_key in range(0, LEN, key_size):
        attend_key_part = key_whole[:, first_key : first_key + key_size]
        attend_value_part = value_whole[:, first_key : first_key + key_size]
        attend_width_keys = attend_key_part.shape[1]
        attend_allowed = allowed_for(attend_width_keys, jnp.int32(first_key))
        update_highest, update_denominator, update_accumulated = running
        update_key_heads = attend_key_part.reshape(rows_here, attend_width_keys, H, HD)
        update_value_heads = attend_value_part.reshape(rows_here, attend_width_keys, H, HD)
        update_scores = (
            jnp.einsum(
                "rshd,rnhd->rhsn", query_heads, update_key_heads, preferred_element_type=jnp.float32
            )
            * scale
        )
        update_scores = jnp.where(attend_allowed, update_scores, NEGATIVE)
        fresh_max = jnp.maximum(update_highest, jnp.max(update_scores, axis=-1))
        exponent = jnp.where(attend_allowed, jnp.exp(update_scores - fresh_max[..., None]), 0.0)
        factor = jnp.exp(update_highest - fresh_max)
        update_denominator = update_denominator * factor + jnp.sum(exponent, axis=-1)
        weighted = jnp.einsum(
            "rhsn,rnhd->rshd",
            exponent.astype(jnp.bfloat16),
            update_value_heads,
            preferred_element_type=jnp.float32,
        )
        update_accumulated = update_accumulated * jnp.swapaxes(factor, 1, 2)[..., None] + weighted
        running = (fresh_max, update_denominator, update_accumulated)
    highest, denominator, accumulated = running
    attention_out = accumulated / jnp.swapaxes(denominator, 1, 2)[..., None]
    logsum = highest + jnp.log(denominator)
    attended = attention_out.reshape(rows_here, span, D).astype(jnp.bfloat16)
    middle = mixed + project(attended, output_weight) + output_bias.astype(jnp.float32)
    second_scaled, second_inverse = normalize(middle)
    second = (second_scaled * gain_second + second_shift.astype(jnp.float32)).astype(jnp.bfloat16)
    units = project(second, up_weight) + up_bias.astype(jnp.float32)
    activated_full, gelu_slope = gelu_pair(units)
    activated = activated_full.astype(jnp.bfloat16)
    block_output = (
        middle + project(activated, down_weight) + down_bias.astype(jnp.float32)
    ).astype(jnp.bfloat16)
    upstream = cotangent.astype(jnp.float32)
    down_bias_grad = jnp.sum(upstream, axis=(0, 1))
    down_weight_grad = outer_sum(activated, cotangent)
    unit_grad = project_back(cotangent, down_weight) * gelu_slope
    up_bias_grad = jnp.sum(unit_grad, axis=(0, 1))
    unit_low = unit_grad.astype(jnp.bfloat16)
    up_weight_grad = outer_sum(second, unit_low)
    middle_part, second_gain_grad, second_shift_grad = normalize_back(
        project_back(unit_low, up_weight), second_scaled, second_inverse, gain_second
    )
    middle_grad = upstream + middle_part
    output_bias_grad = jnp.sum(middle_grad, axis=(0, 1))
    middle_low = middle_grad.astype(jnp.bfloat16)
    output_weight_grad = outer_sum(attended, middle_low)
    attended_grad = project_back(middle_low, output_weight).astype(jnp.bfloat16)
    grad_heads = attended_grad.reshape(rows_here, span, H, HD)
    delta = jnp.swapaxes(jnp.sum(grad_heads.astype(jnp.float32) * attention_out, axis=-1), 1, 2)

    def attend_back(key_part, value_part, offset):
        width_keys = key_part.shape[1]
        allowed = allowed_for(width_keys, offset)
        key_heads = key_part.reshape(rows_here, width_keys, H, HD)
        value_heads = value_part.reshape(rows_here, width_keys, H, HD)
        scores = (
            jnp.einsum(
                "rshd,rnhd->rhsn", query_heads, key_heads, preferred_element_type=jnp.float32
            )
            * scale
        )
        scores = jnp.where(allowed, scores, NEGATIVE)
        probs = jnp.where(allowed, jnp.exp(scores - logsum[..., None]), 0.0)
        probs_low = probs.astype(jnp.bfloat16)
        value_term = jnp.einsum(
            "rhsn,rshd->rnhd", probs_low, grad_heads, preferred_element_type=jnp.float32
        )
        prob_grad = jnp.einsum(
            "rshd,rnhd->rhsn", grad_heads, value_heads, preferred_element_type=jnp.float32
        )
        score_grad = (probs * (prob_grad - delta[..., None])).astype(jnp.bfloat16)
        query_term = (
            jnp.einsum("rhsn,rnhd->rshd", score_grad, key_heads, preferred_element_type=jnp.float32)
            * scale
        )
        key_term = (
            jnp.einsum(
                "rhsn,rshd->rnhd", score_grad, query_heads, preferred_element_type=jnp.float32
            )
            * scale
        )
        return (
            query_term,
            key_term.reshape(rows_here, width_keys, D),
            value_term.reshape(rows_here, width_keys, D),
        )

    back_keys, back_values = (key_whole, value_whole)
    query_grad = jnp.zeros((rows_here, span, H, HD), jnp.float32)
    key_terms = []
    value_terms = []
    for first_key in range(0, LEN, key_size):
        query_term, key_term, value_term = attend_back(
            back_keys[:, first_key : first_key + key_size],
            back_values[:, first_key : first_key + key_size],
            jnp.int32(first_key),
        )
        query_grad = query_grad + query_term
        key_terms.append(key_term)
        value_terms.append(value_term)
    key_grad, value_grad = (
        lax.psum_scatter(
            jnp.concatenate(key_terms, axis=1).astype(jnp.bfloat16),
            "seq",
            scatter_dimension=1,
            tiled=True,
        ).astype(jnp.float32),
        lax.psum_scatter(
            jnp.concatenate(value_terms, axis=1).astype(jnp.bfloat16),
            "seq",
            scatter_dimension=1,
            tiled=True,
        ).astype(jnp.float32),
    )
    query_grad_low = query_grad.reshape(rows_here, span, D).astype(jnp.bfloat16)
    key_grad_low = key_grad.astype(jnp.bfloat16)
    value_grad_low = value_grad.astype(jnp.bfloat16)
    query_bias_grad = jnp.sum(query_grad_low.astype(jnp.float32), axis=(0, 1))
    value_bias_grad = jnp.sum(value_grad_low.astype(jnp.float32), axis=(0, 1))
    joint_low = jnp.concatenate([query_grad_low, key_grad_low, value_grad_low], axis=-1)
    joint_grad = outer_sum(normed, joint_low)
    mixed_part, first_gain_grad, first_shift_grad = normalize_back(
        project_back(joint_low, joint_weight), first_scaled, first_inverse, gain_first
    )
    mixed_grad = middle_grad + mixed_part
    carried = thought_mask * mixed_grad
    following = from_behind(carried[:, 0, :], "seq", -1)
    hidden_grad = (
        mixed_grad - carried + jnp.concatenate([carried[:, 1:], following[:, None, :]], axis=1)
    )
    (
        first_gain_grad,
        first_shift_grad,
        joint_grad,
        query_bias_grad,
        value_bias_grad,
        output_weight_grad,
        output_bias_grad,
        second_gain_grad,
        second_shift_grad,
        up_weight_grad,
        up_bias_grad,
        down_weight_grad,
        down_bias_grad,
    ) = (
        lax.psum_scatter(
            first_gain_grad.astype(jnp.bfloat16), "rows", scatter_dimension=0, tiled=True
        ).astype(jnp.float32),
        lax.psum_scatter(
            first_shift_grad.astype(jnp.bfloat16), "rows", scatter_dimension=0, tiled=True
        ).astype(jnp.float32),
        lax.psum_scatter(
            joint_grad.astype(jnp.bfloat16), "rows", scatter_dimension=0, tiled=True
        ).astype(jnp.float32),
        lax.psum_scatter(
            query_bias_grad.astype(jnp.bfloat16), "rows", scatter_dimension=0, tiled=True
        ).astype(jnp.float32),
        lax.psum_scatter(
            value_bias_grad.astype(jnp.bfloat16), "rows", scatter_dimension=0, tiled=True
        ).astype(jnp.float32),
        lax.psum_scatter(
            output_weight_grad.astype(jnp.bfloat16), "rows", scatter_dimension=0, tiled=True
        ).astype(jnp.float32),
        lax.psum_scatter(
            output_bias_grad.astype(jnp.bfloat16), "rows", scatter_dimension=0, tiled=True
        ).astype(jnp.float32),
        lax.psum_scatter(
            second_gain_grad.astype(jnp.bfloat16), "rows", scatter_dimension=0, tiled=True
        ).astype(jnp.float32),
        lax.psum_scatter(
            second_shift_grad.astype(jnp.bfloat16), "rows", scatter_dimension=0, tiled=True
        ).astype(jnp.float32),
        lax.psum_scatter(
            up_weight_grad.astype(jnp.bfloat16), "rows", scatter_dimension=0, tiled=True
        ).astype(jnp.float32),
        lax.psum_scatter(
            up_bias_grad.astype(jnp.bfloat16), "rows", scatter_dimension=0, tiled=True
        ).astype(jnp.float32),
        lax.psum_scatter(
            down_weight_grad.astype(jnp.bfloat16), "rows", scatter_dimension=0, tiled=True
        ).astype(jnp.float32),
        lax.psum_scatter(
            down_bias_grad.astype(jnp.bfloat16), "rows", scatter_dimension=0, tiled=True
        ).astype(jnp.float32),
    )
    (
        first_gain_grad,
        first_shift_grad,
        joint_grad,
        query_bias_grad,
        value_bias_grad,
        output_weight_grad,
        output_bias_grad,
        second_gain_grad,
        second_shift_grad,
        up_weight_grad,
        up_bias_grad,
        down_weight_grad,
        down_bias_grad,
    ) = (
        lax.psum(first_gain_grad.astype(jnp.bfloat16), "seq").astype(jnp.float32),
        lax.psum(first_shift_grad.astype(jnp.bfloat16), "seq").astype(jnp.float32),
        lax.psum(joint_grad.astype(jnp.bfloat16), "seq").astype(jnp.float32),
        lax.psum(query_bias_grad.astype(jnp.bfloat16), "seq").astype(jnp.float32),
        lax.psum(value_bias_grad.astype(jnp.bfloat16), "seq").astype(jnp.float32),
        lax.psum(output_weight_grad.astype(jnp.bfloat16), "seq").astype(jnp.float32),
        lax.psum(output_bias_grad.astype(jnp.bfloat16), "seq").astype(jnp.float32),
        lax.psum(second_gain_grad.astype(jnp.bfloat16), "seq").astype(jnp.float32),
        lax.psum(second_shift_grad.astype(jnp.bfloat16), "seq").astype(jnp.float32),
        lax.psum(up_weight_grad.astype(jnp.bfloat16), "seq").astype(jnp.float32),
        lax.psum(up_bias_grad.astype(jnp.bfloat16), "seq").astype(jnp.float32),
        lax.psum(down_weight_grad.astype(jnp.bfloat16), "seq").astype(jnp.float32),
        lax.psum(down_bias_grad.astype(jnp.bfloat16), "seq").astype(jnp.float32),
    )
    return (
        block_output,
        hidden_grad,
        first_gain_grad,
        first_shift_grad,
        joint_grad,
        query_bias_grad,
        value_bias_grad,
        output_weight_grad,
        output_bias_grad,
        second_gain_grad,
        second_shift_grad,
        up_weight_grad,
        up_bias_grad,
        down_weight_grad,
        down_bias_grad,
    )


F32, BF16 = (jnp.float32, jnp.bfloat16)
BLOCK = 512
FF = 3072
PIECE = 384
TILE = 48
WINDOW = 384
PLANE_ORDERS = ["yx", "xy", "yx", "xy"]
UNIT_ORDERS = ["lyxh", "lhyx", "lyhx", "xyhl", "lxyh"]
JOINT_ORDERS = ["xhly", "ylhx", "xylh", "xylh", "lyxh", "yxlh", "ylxh", "yxlh", "yxlh"]
SCHEDULE = [
    ("D", 0, 0), ("U", 0, 0), ("D", 1, 0), ("D", 0, 1), ("U", 1, 0), ("D", 2, 0), ("U", 0, 1), ("U", 2, 0),
    ("D", 3, 0), ("D", 1, 1), ("U", 1, 1), ("U", 2, 1), ("U", 6, 0), ("U", 3, 0), ("U", 4, 0), ("D", 3, 1),
    ("D", 2, 1), ("U", 2, 2), ("U", 0, 2), ("U", 9, 0), ("U", 10, 0), ("U", 6, 1), ("U", 1, 2), ("U", 5, 0),
    ("U", 7, 0), ("U", 3, 1), ("U", 0, 3), ("U", 8, 0), ("U", 6, 2), ("U", 11, 0), ("U", 5, 1), ("U", 12, 0),
    ("U", 4, 1), ("U", 2, 3), ("Z", 0, 2), ("U", 10, 1), ("U", 13, 0), ("U", 3, 2), ("U", 9, 1), ("U", 11, 1),
    ("U", 5, 2), ("U", 1, 3), ("U", 6, 3), ("U", 10, 2), ("U", 12, 1), ("U", 7, 1), ("U", 3, 3), ("U", 13, 1),
    ("U", 8, 1), ("U", 9, 2), ("S", 0, 0), ("U", 11, 2), ("U", 10, 3), ("U", 4, 2), ("U", 5, 3), ("U", 12, 2),
    ("U", 7, 2), ("Z", 0, 3), ("U", 13, 2), ("U", 8, 2), ("U", 9, 3), ("S", 0, 1), ("U", 11, 3), ("U", 12, 3),
    ("U", 7, 3), ("U", 4, 3), ("U", 13, 3), ("U", 8, 3),
]
PUMPS = [0, 0, 0, 0, 2, 0, 1, 0, 2, 1, 0, 0, 2, 2, 0, 2, 3, 2, 1, 4, 2, 2, 4]


def nn(left, right):
    return lax.dot_general(left, right, (((1,), (0,)), ((), ())), preferred_element_type=F32)


def nt(left, right):
    return lax.dot_general(left, right, (((1,), (1,)), ((), ())), preferred_element_type=F32)


def tn(left, right):
    return lax.dot_general(left, right, (((0,), (0,)), ((), ())), preferred_element_type=F32)


def wide(column, copies):
    return jnp.concatenate([column] * copies, axis=1)


def row_norm(values):
    centered = values - jnp.mean(values, axis=-1, keepdims=True)
    inverse = lax.rsqrt(jnp.mean(centered * centered, axis=-1, keepdims=True) + EPSILON)
    return (centered * inverse, inverse)


def row_norm_back(upstream, scaled, inverse, gain):
    weighted = upstream * gain
    return inverse * (
        weighted
        - jnp.mean(weighted, axis=-1, keepdims=True)
        - scaled * jnp.mean(weighted * scaled, axis=-1, keepdims=True)
    )


def fold(values):
    return jnp.sum(values.reshape(values.shape[0] // 8, 8, values.shape[1]), axis=0)


def split_pair(values, lane):
    zero = jnp.zeros_like(values)
    return jnp.concatenate([jnp.where(lane < HD, values, zero), jnp.where(lane < HD, zero, values)], axis=0)


def join_pair(values):
    return jnp.concatenate([values[:HD, :128], values[HD:, 128:]], axis=0)


def step_kernel(
    hid, seg, tho, pad, cott, v0, v1, v2, v3, v4, v5, v6, v7, v8, jw, ow, uw, dw,
    blk, hg, sout, jout, dout, vout, nth,
    wb1, wb2, wo, fa, fb, fd, fe, nb, st, q, kk, vv, kt, vt, ps, il, at, att, cotp, act, xx, ulo, ulp,
    hin, hs, mlp, do, dka, dva, gd, gs, gj, r1d, r2d, r3d, r4d, r1, r2, r3, r4, j1, j2, j3, j4,
    mask, ksg, tht, ubg, sv, svr, svx, svz, cin, small, hidv, cot, vec, lsem, psend, precv, rsend, rrecv,
):
    core, line = (lax.axis_index("seq"), lax.axis_index("rows"))
    other = 1 - core
    bits = {"x": lax.rem(line, 2), "y": lax.rem(line // 2, 2), "l": lax.rem(line // 4, 2), "h": line // 8}
    peer = {
        "c": (other, line),
        "x": (core, line + 1 - 2 * bits["x"]),
        "y": (core, line + 2 - 4 * bits["y"]),
        "l": (core, line + 4 - 8 * bits["l"]),
        "h": (core, line + 8 - 16 * bits["h"]),
    }
    base = core * BLOCK
    core_f = core.astype(F32)
    half = pl.multiple_of(core * PIECE, 128)
    other_half = pl.multiple_of(other * PIECE, 128)

    def here(src, dst, spot):
        return pltpu.make_async_copy(src, dst, lsem.at[spot])

    def pair(src, dst, spot):
        return pltpu.make_async_remote_copy(
            src_ref=src, dst_ref=dst, send_sem=psend.at[spot], recv_sem=precv.at[spot],
            device_id=peer["c"], device_id_type=MESH,
        )

    def far(src, dst, group, spot, bit):
        return pltpu.make_async_remote_copy(
            src_ref=src, dst_ref=dst, send_sem=rsend.at[group], recv_sem=rrecv.at[spot],
            device_id=peer[bit], device_id_type=MESH,
        )

    hidden_in = here(hid, hidv, 13)
    hidden_in.start()
    joint_in = [here(jw.at[:, pl.ds(j * D, D)], wb1.at[pl.ds(j * D, D), :], j) for j in range(3)]
    for j in (1, 2, 0):
        joint_in[j].start()
    out_in = here(ow, wo, 3)
    up_in = here(uw, wb2, 4)
    cot_in = here(cott, cot, 14)

    barrier = pltpu.get_barrier_semaphore()
    across = (core, line + 3 - 2 * bits["x"] - 4 * bits["y"])
    along = (core, line + 12 - 8 * bits["l"] - 16 * bits["h"])
    for device in list(peer.values()) + [across, along]:
        pl.semaphore_signal(barrier, inc=1, device_id=device, device_id_type=MESH)

    for j, ref in enumerate((v0, v1, v2, v3, v4, v5, v6, v7)):
        small[j : j + 1, :] = ref[...].astype(F32).reshape(1, D)
    for j in range(4):
        small[8 + j : 9 + j, :] = v8[D * j : D * j + D].astype(F32).reshape(1, D)
    flags = tho[...].astype(F32)
    tht[...] = jnp.broadcast_to(flags, (128, BLOCK)).T
    hidden_in.wait()
    fa[8 : BLOCK + 8, :] = hidv[...].astype(F32)

    def mix(s):
        inputs = fa[8 + 64 * s : 72 + 64 * s, :]
        previous = fa[7 + 64 * s : 71 + 64 * s, :]
        mixed = inputs + wide(tht[64 * s : 64 * s + 64, :], 6) * (previous - inputs)
        fb[64 * s : 64 * s + 64, :] = mixed
        scaled, _ = row_norm(mixed)
        nb[64 * s : 64 * s + 64, :] = (scaled * small[0:1, :] + small[1:2, :]).astype(BF16)

    def project_rows(rows, out):
        @pl.loop(0, 3)
        def _(n):
            cols = pl.ds(pl.multiple_of(256 * n, 256), 256)
            kk[out, cols] = nn(nb[rows, :], wb1[768:1536, cols]).astype(BF16)
            vv[out, cols] = (nn(nb[rows, :], wb1[1536:2304, cols]) + small[3:4, cols]).astype(BF16)
            query = (nn(nb[rows, :], wb1[0:768, cols]) + small[2:3, cols]).astype(BF16)
            q[rows, cols] = (query.astype(F32) * 0.125).astype(BF16)

    for s in range(4, 8):
        mix(s)
    for copy in joint_in:
        copy.wait()
    for copy in (cot_in, out_in, up_in):
        copy.start()
    project_rows(slice(256, 512), slice(512, 768))
    pl.semaphore_wait(barrier, 7)
    edge = pair(hidv.at[pl.ds(BLOCK - 16, 16), :], hin, 0)
    send_keys = pair(kk.at[pl.ds(BLOCK, 256), :], kk.at[pl.ds(0, 256), :], 2)
    send_values = pair(vv.at[pl.ds(BLOCK, 256), :], vv.at[pl.ds(0, 256), :], 3)
    for copy in (edge, send_keys, send_values):
        copy.start()
    for s in range(1, 4):
        mix(s)
    vt[:, 512:768] = vv[512:768, :].T

    first_start = pl.multiple_of(jnp.maximum(base - 256, 0), 128)
    for j, start in enumerate((first_start, base, base + 256)):
        start = pl.multiple_of(start, 128)
        piece = seg[:, pl.ds(start, 256)].astype(F32)
        ksg[256 * j : 256 * j + 256, :] = jnp.broadcast_to(piece, (128, 256)).T
    limit = LEN - pad[0]
    for i in range(4):
        spot = lax.broadcasted_iota(jnp.int32, (WINDOW, 128), 0)
        lane = lax.broadcasted_iota(jnp.int32, (WINDOW, 128), 1)
        key_place = spot + (base - 256 + 128 * i)
        query_place = lane + (base + 128 * i)
        query_segment = seg[:, pl.ds(pl.multiple_of(base + 128 * i, 128), 128)].astype(F32)
        seen = (
            (key_place <= query_place)
            & (ksg[128 * i : 128 * i + WINDOW, :] == query_segment)
            & ((key_place < limit) | (key_place == query_place))
            & (key_place >= 0)
        )
        mask[i] = jnp.where(seen, 0.0, NEGATIVE)

    edge.wait()
    fa[0:8, :] = jnp.broadcast_to(hin[15:16, :].astype(F32) * core_f, (8, D))
    mix(0)
    project_rows(slice(0, 256), slice(256, 512))
    spill = here(fb, hg, 7)
    spill.start()
    down_in = here(dw, wb1, 5)
    down_in.start()
    vt[:, 256:512] = vv[256:512, :].T
    send_keys.wait()
    send_values.wait()
    vt[:, 0:256] = vv[0:256, :].T

    for p in range(6):
        cols = slice(128 * p, 128 * p + 128)
        lane = lax.broadcasted_iota(jnp.int32, (128, 128), 1)
        spans = [(slice(128 * i, 128 * i + 128), slice(128 * i, 128 * i + WINDOW)) for i in range(4)]
        scores = [nt(kk[keys, cols], split_pair(q[rows, cols], lane)) for rows, keys in spans]
        scores = [scores[i] + wide(mask[i], 2) for i in range(4)]
        highest = [jnp.max(score, axis=0, keepdims=True) for score in scores]
        weights = [jnp.exp(scores[i] - highest[i]) for i in range(4)]
        inverse = [1.0 / jnp.sum(weight, axis=0, keepdims=True) for weight in weights]
        low = [weight.astype(BF16) for weight in weights]
        result = [nn(vt[cols, spans[i][1]], low[i]) for i in range(4)]
        for i in range(4):
            ps[4 * p + i] = low[i]
            il[4 * p + i] = jnp.broadcast_to(inverse[i], (8, 256))
            at[core, cols, spans[i][0]] = join_pair(result[i] * inverse[i]).astype(BF16)

    send_attended = pair(at.at[core], at.at[core], 4)
    send_attended.start()
    att[...] = at[core].T

    out_in.wait()
    spill.wait()

    @pl.loop(0, 3)
    def _(n):
        cols = pl.ds(pl.multiple_of(256 * n, 256), 256)
        fb[:, cols] = fb[:, cols] + nn(att[...], wo[:, cols]) + small[4:5, cols]

    for s in range(8):
        rows = slice(64 * s, 64 * s + 64)
        scaled, _ = row_norm(fb[rows, :])
        do[rows, :] = (scaled * small[5:6, :] + small[6:7, :]).astype(BF16)
    st[core] = do[...].T
    send_second = pair(st.at[core], st.at[core], 5)
    send_second.start()
    cot_in.wait()
    send_cot = pair(cot.at[:, pl.ds(other_half, PIECE)], cotp, 6)
    send_cot.start()

    place = {"h": 0, "l": 1, "y": 2, "x": 3}
    live, ready = ({}, [])
    orders = UNIT_ORDERS + JOINT_ORDERS
    mine = (bits["h"], bits["l"], bits["y"], bits["x"])

    def refs_of(item):
        return (gs, (r1, r2, r3, r4), item) if item < 5 else (gj, (j1, j2, j3, j4), item - 5)

    def part(item, stage, own):
        spot = [slice(None)] * 4
        for bit in orders[item][:stage]:
            spot[place[bit]] = bits[bit]
        bit = orders[item][stage]
        spot[place[bit]] = bits[bit] if own else 1 - bits[bit]
        return (refs_of(item)[2],) + tuple(spot)

    def launch(item, stage):
        ref, recv, at_item = refs_of(item)
        group = stage if item < 5 else 4 + stage
        copy = far(ref.at[part(item, stage, False)], recv[stage].at[at_item], group, 4 * item + stage, orders[item][stage])
        copy.start()
        live[(item, stage)] = copy

    def advance(item, stage):
        live[(item, stage)].wait_recv()
        ref, recv, at_item = refs_of(item)
        spot = part(item, stage, True)
        ref[spot] = ref[spot] + recv[stage][at_item]
        if stage < 3:
            launch(item, stage + 1)
            return
        result = ref.at[(at_item,) + mine]
        target = (sout if item < 5 else jout).at[core, at_item]
        for copy in (here(result, target, 16 if item < 5 else 17), pair(result, target, 24 if item < 5 else 25)):
            copy.start()

    def plane_part(z, stage, own):
        first, then = PLANE_ORDERS[z]
        spot = {"x": slice(None), "y": slice(None)}
        if stage == 0:
            spot[first] = bits[first] if own else 1 - bits[first]
        else:
            spot[first] = bits[first]
            spot[then] = bits[then] if own else 1 - bits[then]
        return ((z // 2, z % 2, spot["y"], spot["x"]), first if stage == 0 else then)

    def plane_launch(z, stage):
        spot, bit = plane_part(z, stage, False)
        copy = far(gd.at[spot], (r1d, r2d)[stage].at[z], 8 + stage, 56 + 2 * z + stage, bit)
        copy.start()
        live[("plane", z, stage)] = copy

    def plane_advance(z, stage):
        live[("plane", z, stage)].wait_recv()
        spot, _ = plane_part(z, stage, True)
        gd[spot] = gd[spot] + (r1d, r2d)[stage][z]
        live["planes"] = live.get("planes", 0) + stage
        if stage == 0:
            plane_launch(z, 1)
        elif live["planes"] == 4:
            down_launch(2)

    def down_launch(stage):
        if stage == 2:
            spot, target, bit = ((slice(None), 1 - bits["l"], bits["y"], bits["x"]), r3d, "l")
        else:
            spot, target, bit = ((1 - bits["h"], bits["l"], bits["y"], bits["x"]), r4d, "h")
        copy = far(gd.at[spot], target, 8 + stage, 62 + stage, bit)
        copy.start()
        live[("d", stage)] = copy

    def down_advance(stage):
        live[("d", stage)].wait_recv()
        if stage == 2:
            spot = (slice(None), bits["l"], bits["y"], bits["x"])
            gd[spot] = gd[spot] + r3d[...]
            down_launch(3)
            return
        gd[mine] = gd[mine] + r4d[...]
        copies = (here(gd.at[mine], dout.at[core], 15), pair(gd.at[mine], dout.at[core], 26))
        for copy in copies:
            copy.start()
        live[("d", 4)] = copies

    def act_copy(z, start, width):
        cols = pl.ds(start, width)
        return pair(act.at[:, cols], xx.at[:, cols], 10 + z)

    def unit_copy(z):
        start = pl.multiple_of(768 * z + PIECE * other, 128)
        return pair(ulo.at[:, pl.ds(start, PIECE)], ulp.at[:, pl.ds(PIECE * z, PIECE)], 14 + z)

    def pump(count):
        for _ in range(min(count, len(ready))):
            name, spot, stage = ready.pop(0)
            if name == "D":
                plane_advance(spot, stage)
            elif name == "Z":
                down_advance(stage)
            elif name == "S":
                small_advance(stage)
            else:
                advance(spot, stage)

    ready.extend(SCHEDULE)

    up_in.wait()
    down_in.wait()
    fa[...] = jnp.zeros_like(fa)

    def feed(z, first, last):
        @pl.loop(first, last)
        def _(f):
            cols = pl.ds(pl.multiple_of(768 * z + 256 * f, 256), 256)
            up_part = wb2[:, cols]
            units = nn(do[...], up_part) + small[8 + z : 9 + z, pl.ds(pl.multiple_of(256 * f, 256), 256)]
            back = nt(cot[...], wb1[cols, :])
            total = jnp.zeros((8, 256), F32)
            for s in range(8):
                rows = slice(64 * s, 64 * s + 64)
                value = units[rows, :]
                square = value * value
                gate = 0.5 + 0.5 * jnp.tanh(value * (GELU_SCALE + GELU_SCALE * GELU_CUBIC * square))
                result = value * gate
                slope = gate + 2.0 * result * (1.0 - gate) * (GELU_SCALE + 3.0 * GELU_SCALE * GELU_CUBIC * square)
                grad = back[rows, :] * slope
                total = total + fold(grad)
                act[rows, cols] = result.astype(BF16)
                ulo[rows, cols] = grad.astype(BF16)
            ubg[:, cols] = total
            fa[0:BLOCK, :] += nt(ulo[:, cols], up_part)
            act_copy(z, pl.multiple_of(768 * z + 256 * f, 256), 256).start()

        if last == 3:
            unit_copy(z).start()

    def feed_grads(z):
        if z == 0:
            send_cot.wait()
        act_copy(z, 768 * z, 768).wait()

        @pl.loop(0, 2)
        def _(y):
            cols = pl.ds(pl.multiple_of(768 * z + 384 * y, 128), 384)
            total = tn(act[:, cols], cot[:, pl.ds(half, PIECE)]) + tn(xx[:, cols], cotp[...])
            gd[z // 2, z % 2, y] = total.astype(BF16).reshape(2, 192, PIECE)

        plane_launch(z, 0)
        if z == 0:
            send_second.wait()
        unit_copy(z).wait()
        start = pl.multiple_of(768 * z + PIECE * core, 128)
        total = nn(st[core], ulo[:, pl.ds(start, PIECE)]) + nn(st[other], ulp[:, 384 * z : 384 * z + 384])
        gs[z] = total.astype(BF16).reshape(2, 2, 2, 2, TILE, PIECE)
        launch(z, 0)

    feed(0, 0, 3)
    feed(1, 0, 1)
    feed_grads(0)
    kt[:, 0:BLOCK] = nb[...].T
    keep_normed = here(kt.at[:, pl.ds(0, BLOCK)], nth.at[core], 9)
    send_normed = pair(kt.at[:, pl.ds(0, BLOCK)], nth.at[core], 1)
    keep_normed.start()
    send_normed.start()
    pump(PUMPS[0])
    feed(1, 1, 3)
    pump(PUMPS[1])
    feed(2, 0, 1)
    feed_grads(1)
    pump(PUMPS[2])
    feed(2, 1, 3)
    pump(PUMPS[3])
    feed(3, 0, 1)
    feed_grads(2)
    pump(PUMPS[4])
    feed(3, 1, 3)
    pump(PUMPS[5])
    joint_again = here(jw, wb2.at[:, pl.ds(0, 3 * D)], 6)
    joint_again.start()

    sums = [jnp.zeros((8, D), F32) for _ in range(4)]
    for s in range(8):
        rows = slice(64 * s, 64 * s + 64)
        upstream = fa[rows, :]
        scaled, inverse = row_norm(fb[rows, :])
        direct = cot[rows, :].astype(F32)
        result = direct + row_norm_back(upstream, scaled, inverse, small[5:6, :])
        fa[rows, :] = result
        nb[rows, :] = result.astype(BF16)
        for j, term in enumerate((result, upstream * scaled, upstream, direct)):
            sums[j] = sums[j] + fold(term)
    for j in range(4):
        sv[4 + j : 5 + j, :] = jnp.sum(sums[j], axis=0, keepdims=True)
    for j in range(4):
        sv[8 + j : 9 + j, :] = jnp.sum(ubg[:, 768 * j : 768 * j + 768], axis=0, keepdims=True)
    send_middle = pair(nb.at[:, pl.ds(other_half, PIECE)], mlp, 7)
    send_middle.start()
    pump(PUMPS[6])
    feed_grads(3)
    pump(PUMPS[7])

    @pl.loop(0, 3)
    def _(n):
        cols = pl.ds(pl.multiple_of(256 * n, 256), 256)
        do[:, cols] = nt(nb[...], wo[cols, :]).astype(BF16)

    pump(PUMPS[8])
    send_middle.wait()
    send_attended.wait()
    total = nn(at[core], nb[:, pl.ds(half, PIECE)]) + nn(at[other], mlp[...])
    gs[4] = total.astype(BF16).reshape(2, 2, 2, 2, TILE, PIECE)
    launch(4, 0)
    pump(PUMPS[9])
    keep_normed.wait()
    send_normed.wait()
    for j in range(3):
        kt[:, 256 * j : 256 * j + 256] = kk[256 * j : 256 * j + 256, :].T
    mixed_in = here(hg, fe, 8)
    mixed_in.start()
    normed_again = here(nth, st, 10)
    normed_again.start()

    def attend_back(p):
        cols = slice(128 * p, 128 * p + 128)
        lane = lax.broadcasted_iota(jnp.int32, (128, 128), 1)
        dka[...] = jnp.zeros_like(dka)
        dva[...] = jnp.zeros_like(dva)
        spans = [(slice(128 * i, 128 * i + 128), slice(128 * i, 128 * i + WINDOW)) for i in range(4)]
        grads, deltas = ([], [])
        for i in range(4):
            rows = spans[i][0]
            inverse = il[4 * p + i]
            spread = jnp.concatenate(
                [jnp.broadcast_to(inverse[0:1, :128], (HD, 128)), jnp.broadcast_to(inverse[0:1, 128:], (HD, 128))], axis=0
            ).T
            grad = (do[rows, cols].astype(F32) * spread).astype(BF16)
            product = (grad.astype(F32) * att[rows, cols].astype(F32)).T
            deltas.append(
                jnp.concatenate(
                    [jnp.sum(product[:HD], axis=0, keepdims=True), jnp.sum(product[HD:], axis=0, keepdims=True)], axis=1
                )
            )
            grads.append(split_pair(grad, lane))
        queries = [split_pair(q[rows, cols], lane) for rows, _ in spans]
        prob_grad = [nt(vv[spans[i][1], cols], grads[i]) for i in range(4)]
        low = [ps[4 * p + i] for i in range(4)]
        value_term = [nn(low[i], grads[i]) for i in range(4)]
        score = [(low[i].astype(F32) * (prob_grad[i] - deltas[i])).astype(BF16) for i in range(4)]
        key_term = [nn(score[i], queries[i]) for i in range(4)]
        query_term = [nn(kt[cols, spans[i][1]], score[i]) for i in range(4)]
        for i in range(4):
            xx[spans[i][0], cols] = (join_pair(query_term[i]) * 0.125).T.astype(BF16)
            dka[spans[i][1], :] += key_term[i]
            dva[spans[i][1], :] += value_term[i]
        xx[:, 768 + 128 * p : 896 + 128 * p] = dka[256:, :].astype(BF16)
        xx[:, 1536 + 128 * p : 1664 + 128 * p] = dva[256:, :].astype(BF16)
        hs[0:256, cols] = dka[0:256, :].astype(BF16)
        hs[256:512, cols] = dva[0:256, :].astype(BF16)

    def halo(g):
        return pair(hs.at[:, pl.ds(256 * g, 256)], hidv.at[:, pl.ds(256 * g, 256)], 18 + g)

    def exchange(g, j):
        start = pl.multiple_of(768 * j + 256 * g + 128 * other, 128)
        return pair(xx.at[:, pl.ds(start, 128)], ulp.at[:, pl.ds(384 * g + 128 * j, 128)], 21 + g)

    def settle(g):
        halo(g).wait()
        for j in (1, 2):
            cols = slice(768 * j + 256 * g, 768 * j + 256 * g + 256)
            come = hidv[256 * (j - 1) : 256 * j, 256 * g : 256 * g + 256]
            xx[256:512, cols] = xx[256:512, cols] + come
        for j in range(3):
            exchange(g, j).start()

    def joint_part(g):
        pair(xx.at[:, pl.ds(0, PIECE)], ulp.at[:, pl.ds(384 * g, PIECE)], 21 + g).wait()
        own = [xx[:, pl.ds(pl.multiple_of(768 * j + 256 * g + 128 * core, 128), 128)] for j in range(3)]
        total = nn(st[core], jnp.concatenate(own, axis=1)) + nn(st[other], ulp[:, 384 * g : 384 * g + 384])
        total = total.astype(BF16)
        for j in range(3):
            gj[3 * g + j] = total[:, 128 * j : 128 * j + 128].reshape(2, 2, 2, 2, TILE, 128)
            launch(5 + 3 * g + j, 0)

    def normed_back(first, count):
        @pl.loop(0, 3)
        def _(n):
            rows = pl.ds(pl.multiple_of(256 * n, 256), 256)
            spans = [slice(768 * j + 256 * first, 768 * j + 256 * (first + count)) for j in range(3)]
            total = sum(nt(xx[:, span], wb2[rows, span]) for span in spans)
            if first > 0:
                total = total + fd[0:BLOCK, rows]
            fd[0:BLOCK, rows] = total

    def output_part(n):
        cols = slice(256 * n, 256 * n + 256)
        do[:, cols] = (fb[:, cols] + nn(act[...], wb1[:, cols]) + small[7:8, cols]).astype(BF16)

    for p in range(6):
        attend_back(p)
        g = p // 2
        if p % 2 == 1:
            halo(g).start()
        elif p > 0:
            if p == 2:
                normed_again.wait()
            settle(g - 1)
        if p in (3, 5):
            joint_part(g - 1)
        pump(PUMPS[10 + p])

    joint_again.wait()
    normed_back(0, 2)
    settle(2)
    pump(PUMPS[16])

    joint_part(2)
    pump(PUMPS[17])

    normed_back(2, 1)
    pump(PUMPS[18])
    sv[2:3, :] = jnp.sum(xx[:, 0:768].astype(F32), axis=0, keepdims=True)
    sv[3:4, :] = jnp.sum(xx[:, 1536:2304].astype(F32), axis=0, keepdims=True)
    mixed_in.wait()
    sums = [jnp.zeros((8, D), F32) for _ in range(2)]
    for s in range(8):
        rows = slice(64 * s, 64 * s + 64)
        upstream = fd[rows, :]
        scaled, inverse = row_norm(fe[rows, :])
        grad = fa[rows, :] + row_norm_back(upstream, scaled, inverse, small[0:1, :])
        sums[0] = sums[0] + fold(upstream * scaled)
        sums[1] = sums[1] + fold(upstream)
        carried = wide(tht[rows, :], 6) * grad
        fa[rows, :] = grad - carried
        fd[rows, :] = carried
    carry = pair(fd.at[pl.ds(0, 8), :], cin, 8)
    carry.start()
    for j in range(2):
        sv[j : j + 1, :] = jnp.sum(sums[j], axis=0, keepdims=True)
    sv[12:16, :] = jnp.zeros((4, D), F32)
    small_copy = pair(sv, svr, 9)
    small_copy.start()
    fd[BLOCK : BLOCK + 8, :] = jnp.zeros((8, D), F32)
    pump(PUMPS[19])
    small_copy.wait()
    sv[...] = sv[...] + svr[...]

    def spread_small(slots, spot, names, row):
        slots[spot] = sv[...]
        copies = []
        for d in (1, 2, 3):
            step = sum((names[b][1] * (1 - 2 * bits[names[b][0]])) for b in range(2) if d & (1 << b))
            copies.append(
                pltpu.make_async_remote_copy(
                    src_ref=sv, dst_ref=slots.at[spot], send_sem=rsend.at[row + d], recv_sem=rrecv.at[row + 54 + d],
                    device_id=(core, line + step), device_id_type=MESH,
                )
            )
        for copy in copies:
            copy.start()
        return copies

    def small_advance(stage):
        slots = (svx, svz)[stage]
        for copy in live[("s", stage)]:
            copy.wait()
        sv[...] = (slots[0] + slots[1]) + (slots[2] + slots[3])
        if stage == 0:
            live[("s", 1)] = spread_small(svz, line // 4, (("l", 4), ("h", 8)), 14)

    live[("s", 0)] = spread_small(svx, lax.rem(line, 4), (("x", 1), ("y", 2)), 11)
    carry.wait()
    fd[BLOCK : BLOCK + 1, :] = cin[0:1, :] * (1.0 - core_f)
    for s in range(8):
        rows = slice(64 * s, 64 * s + 64)
        fa[rows, :] = fa[rows, :] + fd[64 * s + 1 : 64 * s + 65, :]
    hidden_out = here(fa.at[pl.ds(0, BLOCK), :], hg, 12)
    hidden_out.start()
    pump(PUMPS[20])

    output_part(0)
    pump(PUMPS[21])
    output_part(1)
    pump(PUMPS[22])
    output_part(2)
    block_out = here(do, blk, 11)
    block_out.start()
    pump(len(ready))

    shift = lax.rem(D - TILE * line + D, D)
    vec[0:8, :] = pltpu.roll(sv[0:8, :], shift, 1)[:, 0:256]
    wide_shift = lax.rem(D - 192 * lax.rem(line, 4), D)
    turned = pltpu.roll(sv[8:16, :], wide_shift, 1)[:, 0:256]
    spot = lax.broadcasted_iota(jnp.int32, (8, 256), 0)
    vec[8:16, :] = jnp.broadcast_to(
        jnp.sum(jnp.where(spot == line // 4, turned, 0.0), axis=0, keepdims=True), (8, 256)
    )
    vec_out = here(vec, vout, 6)
    vec_out.start()
    vec_out.wait()
    for group, ref in enumerate((r1, r2, r3, r4, j1, j2, j3, j4, r1d, r2d, r3d, r4d)):
        far(ref, ref, group, 0, "x").wait_send()
    for spot, ref in ((0, sout), (1, jout)):
        here(ref.at[core], ref.at[core], 16 + spot).wait()
        pair(ref.at[core], ref.at[core], 24 + spot).wait()
    for copy in live[("d", 4)]:
        copy.wait()
    block_out.wait()
    hidden_out.wait()


def finish_kernel(
    blk, hg, sout, jout, dout, vec,
    blk_out, hg_out, fg, fs, joint_out, qb, vb, og_out, ob, sg, ss, ug_out, ub, dg_out, db,
    sin, jin, din, bin_, hin, joint, og, ug, dg, vin, sem,
):
    def move(src, dst, spot):
        copy = pltpu.make_async_copy(src, dst, sem.at[spot])
        copy.start()
        return copy

    loads = [move(jout, jin, 0), move(sout, sin, 1), move(dout, din, 2)]
    quarter = BLOCK // 4
    wholes = [move(hg.at[pl.ds(quarter * n, quarter), :], hin.at[pl.ds(quarter * n, quarter), :], 9 + n) for n in range(4)]
    wholes.append(move(blk, bin_, 13))
    vec_in = move(vec, vin, 18)
    stores = []
    loads[0].wait()
    for c in range(2):
        for g in range(3):
            for j in range(3):
                start = 768 * j + 256 * g + 128 * c
                joint[:, start : start + 128] = jin[c, 3 * g + j].astype(F32)
    stores.append(move(joint, joint_out, 5))
    for n in range(4):
        wholes[n].wait()
        span = pl.ds(quarter * n, quarter)
        stores.append(move(hin.at[span, :], hg_out.at[span, :], 14 + n))
    wholes[4].wait()
    stores.append(move(bin_, blk_out, 4))
    loads[1].wait()
    for c in range(2):
        for n in range(4):
            start = 768 * n + 384 * c
            ug[:, start : start + 384] = sin[c, n].astype(F32)
        og[:, 384 * c : 384 * c + 384] = sin[c, 4].astype(F32)
    stores.append(move(ug, ug_out, 6))
    stores.append(move(og, og_out, 7))
    vec_in.wait()
    for j, ref in enumerate((fg, fs, qb, vb, ob, sg, ss, db)):
        ref[...] = vin[j, 0:48]
    ub[...] = vin[8, 0:192]
    loads[2].wait()
    for c in range(2):
        dg[:, 384 * c : 384 * c + 384] = din[c].astype(F32)
    stores.append(move(dg, dg_out, 8))
    for copy in stores:
        copy.wait()


def fused_local(
    hidden, segments, thoughts, padding, cotangent, first_gain, first_shift, joint_weight, query_bias, value_bias,
    output_weight, output_bias, second_gain, second_shift, up_weight, up_bias, down_weight, down_bias,
):
    rows = (first_gain, first_shift, query_bias, value_bias, output_bias, second_gain, second_shift, down_bias)
    shape = jax.ShapeDtypeStruct
    vmem, anywhere = (pl.BlockSpec(memory_space=pltpu.VMEM), pl.BlockSpec(memory_space=pl.ANY))
    v = pltpu.VMEM
    dma = pltpu.SemaphoreType.DMA
    blk, hg, sout, jout, dout, vec, _ = pl.pallas_call(
        step_kernel,
        out_shape=(
            shape((BLOCK, D), BF16),
            shape((BLOCK, D), F32),
            shape((2, 5, TILE, PIECE), BF16),
            shape((2, 9, TILE, 128), BF16),
            shape((2, 192, PIECE), BF16),
            shape((16, 256), F32),
            shape((2, D, BLOCK), BF16),
        ),
        in_specs=[anywhere, vmem, vmem, pl.BlockSpec(memory_space=pltpu.SMEM), anywhere] + [vmem] * 9 + [anywhere] * 4,
        out_specs=(anywhere,) * 7,
        scratch_shapes=[
            v((FF, D), BF16), v((D, FF), BF16), v((D, D), BF16),
            v((BLOCK + 8, D), F32), v((BLOCK, D), F32), v((BLOCK + 8, D), F32), v((BLOCK, D), F32),
            v((BLOCK, D), BF16), v((2, D, BLOCK), BF16), v((BLOCK, D), BF16),
            v((768, D), BF16), v((768, D), BF16), v((D, 768), BF16), v((D, 768), BF16),
            v((24, WINDOW, 256), BF16), v((24, 8, 256), F32), v((2, D, BLOCK), BF16), v((BLOCK, D), BF16),
            v((BLOCK, PIECE), BF16), v((BLOCK, FF), BF16), v((BLOCK, FF), BF16), v((BLOCK, FF), BF16), v((BLOCK, 1536), BF16),
            v((16, D), BF16), v((BLOCK, D), BF16), v((BLOCK, PIECE), BF16), v((BLOCK, D), BF16),
            v((768, 128), F32), v((768, 128), F32),
            v((2, 2, 2, 2, 192, PIECE), BF16), v((5, 2, 2, 2, 2, TILE, PIECE), BF16), v((9, 2, 2, 2, 2, TILE, 128), BF16),
            v((4, 2, 192, PIECE), BF16), v((4, 192, PIECE), BF16), v((2, 192, PIECE), BF16), v((192, PIECE), BF16),
            v((5, 2, 2, 2, TILE, PIECE), BF16), v((5, 2, 2, TILE, PIECE), BF16), v((5, 2, TILE, PIECE), BF16), v((5, TILE, PIECE), BF16),
            v((9, 2, 2, 2, TILE, 128), BF16), v((9, 2, 2, TILE, 128), BF16), v((9, 2, TILE, 128), BF16), v((9, TILE, 128), BF16),
            v((4, WINDOW, 128), F32), v((768, 128), F32), v((BLOCK, 128), F32), v((8, FF), F32),
            v((16, D), F32), v((16, D), F32), v((4, 16, D), F32), v((4, 16, D), F32), v((8, D), F32), v((16, D), F32), v((BLOCK, D), BF16), v((BLOCK, D), BF16), v((16, 256), F32),
            dma((18,)), dma((27,)), dma((27,)), dma((18,)), dma((72,)),
        ],
        compiler_params=pltpu.CompilerParams(collective_id=0, has_side_effects=True, vmem_limit_bytes=66 << 20),
    )(
        hidden[0], segments, thoughts, padding, cotangent[0], *rows, up_bias, joint_weight, output_weight, up_weight, down_weight
    )
    vector = shape((TILE,), F32)
    results = pl.pallas_call(
        finish_kernel,
        out_shape=(
            shape((BLOCK, D), BF16), shape((BLOCK, D), F32),
            vector, vector, shape((TILE, 3 * D), F32), vector, vector, shape((TILE, D), F32), vector, vector, vector,
            shape((TILE, FF), F32), shape((192,), F32), shape((192, D), F32), vector,
        ),
        in_specs=[anywhere] * 6,
        out_specs=(
            anywhere, anywhere, vmem, vmem, anywhere, vmem, vmem, anywhere, vmem, vmem, vmem, anywhere, vmem, anywhere, vmem,
        ),
        scratch_shapes=[
            v((2, 5, TILE, PIECE), BF16), v((2, 9, TILE, 128), BF16), v((2, 192, PIECE), BF16), v((BLOCK, D), BF16), v((BLOCK, D), F32),
            v((TILE, 3 * D), F32), v((TILE, D), F32), v((TILE, FF), F32), v((192, D), F32), v((16, 256), F32), dma((19,)),
        ],
    )(blk, hg, sout, jout, dout, vec)
    return (results[0][None], results[1][None]) + tuple(results[2:])


MESH = pl.DeviceIdType.MESH


def solution(mesh):
    placed = (
        P("rows", "seq", None),
        P("rows", None),
        P("rows", "seq"),
        P("rows"),
        P("rows", "seq", None),
        P(),
        P(),
        P(),
        P(),
        P(),
        P(),
        P(),
        P(),
        P(),
        P(),
        P(),
        P(),
        P(),
    )
    fused = mesh.shape["seq"] == 2 and mesh.shape["rows"] == 16
    return jax.shard_map(
        fused_local if fused else local,
        mesh=mesh,
        in_specs=placed,
        out_specs=(
            P("rows", "seq", None),
            P("rows", "seq", None),
            P("rows"),
            P("rows"),
            P("rows", None),
            P("rows"),
            P("rows"),
            P("rows", None),
            P("rows"),
            P("rows"),
            P("rows"),
            P("rows", None),
            P("rows"),
            P("rows", None),
            P("rows"),
        ),
        check_vma=False,
    )
```

```python
import functools
import math

import jax
import jax.numpy as jnp
from jax import lax
from jax.experimental import pallas as pl
from jax.experimental.pallas import tpu as pltpu
from jax.sharding import PartitionSpec as P

D = 768
H = 12
HD = 64
LEN = 1024


EPSILON = 1e-05
NEGATIVE = -1e30
GELU_SCALE = math.sqrt(2.0 / math.pi)
GELU_CUBIC = 0.044715


def from_behind(value, axis, steps):
    count = lax.axis_size(axis)
    leading, last = (max(0, -steps), min(count, count - steps))
    return lax.ppermute(value, axis, [(source, source + steps) for source in range(leading, last)])


def normalize(values):
    centered = values - jnp.mean(values, axis=-1, keepdims=True)
    inverse = lax.rsqrt(jnp.mean(centered * centered, axis=-1, keepdims=True) + EPSILON)
    return (centered * inverse, inverse)


def normalize_back(upstream, scaled, inverse, gain):
    weighted = upstream * gain
    inner = (
        weighted
        - jnp.mean(weighted, axis=-1, keepdims=True)
        - scaled * jnp.mean(weighted * scaled, axis=-1, keepdims=True)
    )
    return (
        inverse * inner,
        jnp.sum(upstream * scaled, axis=(0, 1)),
        jnp.sum(upstream, axis=(0, 1)),
    )


def gelu_pair(values):
    inner = GELU_SCALE * (values + GELU_CUBIC * values * values * values)
    tangent = jnp.tanh(inner)
    result = 0.5 * values * (1.0 + tangent)
    gelu_slope = 0.5 * (1.0 + tangent) + 0.5 * values * (1.0 - tangent * tangent) * GELU_SCALE * (
        1.0 + 3.0 * GELU_CUBIC * values * values
    )
    return (result, gelu_slope)


def project(values, weight):
    return jnp.einsum("rsd,de->rse", values, weight, preferred_element_type=jnp.float32)


def project_back(values, weight):
    return jnp.einsum("rse,de->rsd", values, weight, preferred_element_type=jnp.float32)


def outer_sum(left, right):
    return jnp.einsum("rsd,rse->de", left, right, preferred_element_type=jnp.float32)


def visibility(query_place, query_segment, key_place, key_segment, limits):
    earlier = key_place[None, None, :] <= query_place[None, :, None]
    shared = key_segment[:, None, :] == query_segment[:, :, None]
    unpadded = (key_place[None, None, :] < limits[:, None, None]) | (
        key_place[None, None, :] == query_place[None, :, None]
    )
    return earlier & shared & unpadded


def local(
    hidden,
    segments,
    thoughts,
    padding,
    cotangent,
    first_gain,
    first_shift,
    joint_weight,
    query_bias,
    value_bias,
    output_weight,
    output_bias,
    second_gain,
    second_shift,
    up_weight,
    up_bias,
    down_weight,
    down_bias,
):
    rows_here, span = (hidden.shape[0], hidden.shape[1])
    scale = HD ** (-0.5)
    key_size = min(512, LEN)
    position_base = lax.axis_index("seq") * span
    query_place = position_base + jnp.arange(span, dtype=jnp.int32)
    query_segment = lax.dynamic_slice_in_dim(segments, position_base, span, 1)
    limits = LEN - padding
    thought_mask = thoughts.astype(jnp.float32)[:, :, None]
    gain_first = first_gain.astype(jnp.float32)
    gain_second = second_gain.astype(jnp.float32)
    incoming = from_behind(hidden[:, span - 1, :], "seq", 1)
    inputs = hidden.astype(jnp.float32)
    previous = jnp.concatenate([incoming.astype(jnp.float32)[:, None, :], inputs[:, :-1]], axis=1)
    mixed = inputs + thought_mask * (previous - inputs)
    first_scaled, first_inverse = normalize(mixed)
    normed = (first_scaled * gain_first + first_shift.astype(jnp.float32)).astype(jnp.bfloat16)
    joint = project(normed, joint_weight)
    query_low = (joint[:, :, :D] + query_bias.astype(jnp.float32)).astype(jnp.bfloat16)
    key_low = joint[:, :, D : 2 * D].astype(jnp.bfloat16)
    value_low = (joint[:, :, 2 * D :] + value_bias.astype(jnp.float32)).astype(jnp.bfloat16)
    query_heads = query_low.reshape(rows_here, span, H, HD)

    def allowed_for(width_keys, offset):
        key_place = offset + jnp.arange(width_keys, dtype=jnp.int32)
        key_segment = lax.dynamic_slice_in_dim(segments, offset, width_keys, 1)
        return visibility(query_place, query_segment, key_place, key_segment, limits)[:, None]

    empty_stats = jnp.zeros((rows_here, H, span), jnp.float32)
    initial = (
        empty_stats + NEGATIVE,
        empty_stats,
        jnp.zeros((rows_here, span, H, HD), jnp.float32),
    )
    key_whole, value_whole = (
        lax.all_gather(key_low, "seq", axis=1, tiled=True),
        lax.all_gather(value_low, "seq", axis=1, tiled=True),
    )
    running = initial
    for first_key in range(0, LEN, key_size):
        attend_key_part = key_whole[:, first_key : first_key + key_size]
        attend_value_part = value_whole[:, first_key : first_key + key_size]
        attend_width_keys = attend_key_part.shape[1]
        attend_allowed = allowed_for(attend_width_keys, jnp.int32(first_key))
        update_highest, update_denominator, update_accumulated = running
        update_key_heads = attend_key_part.reshape(rows_here, attend_width_keys, H, HD)
        update_value_heads = attend_value_part.reshape(rows_here, attend_width_keys, H, HD)
        update_scores = (
            jnp.einsum(
                "rshd,rnhd->rhsn", query_heads, update_key_heads, preferred_element_type=jnp.float32
            )
            * scale
        )
        update_scores = jnp.where(attend_allowed, update_scores, NEGATIVE)
        fresh_max = jnp.maximum(update_highest, jnp.max(update_scores, axis=-1))
        exponent = jnp.where(attend_allowed, jnp.exp(update_scores - fresh_max[..., None]), 0.0)
        factor = jnp.exp(update_highest - fresh_max)
        update_denominator = update_denominator * factor + jnp.sum(exponent, axis=-1)
        weighted = jnp.einsum(
            "rhsn,rnhd->rshd",
            exponent.astype(jnp.bfloat16),
            update_value_heads,
            preferred_element_type=jnp.float32,
        )
        update_accumulated = update_accumulated * jnp.swapaxes(factor, 1, 2)[..., None] + weighted
        running = (fresh_max, update_denominator, update_accumulated)
    highest, denominator, accumulated = running
    attention_out = accumulated / jnp.swapaxes(denominator, 1, 2)[..., None]
    logsum = highest + jnp.log(denominator)
    attended = attention_out.reshape(rows_here, span, D).astype(jnp.bfloat16)
    middle = mixed + project(attended, output_weight) + output_bias.astype(jnp.float32)
    second_scaled, second_inverse = normalize(middle)
    second = (second_scaled * gain_second + second_shift.astype(jnp.float32)).astype(jnp.bfloat16)
    units = project(second, up_weight) + up_bias.astype(jnp.float32)
    activated_full, gelu_slope = gelu_pair(units)
    activated = activated_full.astype(jnp.bfloat16)
    block_output = (
        middle + project(activated, down_weight) + down_bias.astype(jnp.float32)
    ).astype(jnp.bfloat16)
    upstream = cotangent.astype(jnp.float32)
    down_bias_grad = jnp.sum(upstream, axis=(0, 1))
    down_weight_grad = outer_sum(activated, cotangent)
    unit_grad = project_back(cotangent, down_weight) * gelu_slope
    up_bias_grad = jnp.sum(unit_grad, axis=(0, 1))
    unit_low = unit_grad.astype(jnp.bfloat16)
    up_weight_grad = outer_sum(second, unit_low)
    middle_part, second_gain_grad, second_shift_grad = normalize_back(
        project_back(unit_low, up_weight), second_scaled, second_inverse, gain_second
    )
    middle_grad = upstream + middle_part
    output_bias_grad = jnp.sum(middle_grad, axis=(0, 1))
    middle_low = middle_grad.astype(jnp.bfloat16)
    output_weight_grad = outer_sum(attended, middle_low)
    attended_grad = project_back(middle_low, output_weight).astype(jnp.bfloat16)
    grad_heads = attended_grad.reshape(rows_here, span, H, HD)
    delta = jnp.swapaxes(jnp.sum(grad_heads.astype(jnp.float32) * attention_out, axis=-1), 1, 2)

    def attend_back(key_part, value_part, offset):
        width_keys = key_part.shape[1]
        allowed = allowed_for(width_keys, offset)
        key_heads = key_part.reshape(rows_here, width_keys, H, HD)
        value_heads = value_part.reshape(rows_here, width_keys, H, HD)
        scores = (
            jnp.einsum(
                "rshd,rnhd->rhsn", query_heads, key_heads, preferred_element_type=jnp.float32
            )
            * scale
        )
        scores = jnp.where(allowed, scores, NEGATIVE)
        probs = jnp.where(allowed, jnp.exp(scores - logsum[..., None]), 0.0)
        probs_low = probs.astype(jnp.bfloat16)
        value_term = jnp.einsum(
            "rhsn,rshd->rnhd", probs_low, grad_heads, preferred_element_type=jnp.float32
        )
        prob_grad = jnp.einsum(
            "rshd,rnhd->rhsn", grad_heads, value_heads, preferred_element_type=jnp.float32
        )
        score_grad = (probs * (prob_grad - delta[..., None])).astype(jnp.bfloat16)
        query_term = (
            jnp.einsum("rhsn,rnhd->rshd", score_grad, key_heads, preferred_element_type=jnp.float32)
            * scale
        )
        key_term = (
            jnp.einsum(
                "rhsn,rshd->rnhd", score_grad, query_heads, preferred_element_type=jnp.float32
            )
            * scale
        )
        return (
            query_term,
            key_term.reshape(rows_here, width_keys, D),
            value_term.reshape(rows_here, width_keys, D),
        )

    back_keys, back_values = (key_whole, value_whole)
    query_grad = jnp.zeros((rows_here, span, H, HD), jnp.float32)
    key_terms = []
    value_terms = []
    for first_key in range(0, LEN, key_size):
        query_term, key_term, value_term = attend_back(
            back_keys[:, first_key : first_key + key_size],
            back_values[:, first_key : first_key + key_size],
            jnp.int32(first_key),
        )
        query_grad = query_grad + query_term
        key_terms.append(key_term)
        value_terms.append(value_term)
    key_grad, value_grad = (
        lax.psum_scatter(
            jnp.concatenate(key_terms, axis=1).astype(jnp.bfloat16),
            "seq",
            scatter_dimension=1,
            tiled=True,
        ).astype(jnp.float32),
        lax.psum_scatter(
            jnp.concatenate(value_terms, axis=1).astype(jnp.bfloat16),
            "seq",
            scatter_dimension=1,
            tiled=True,
        ).astype(jnp.float32),
    )
    query_grad_low = query_grad.reshape(rows_here, span, D).astype(jnp.bfloat16)
    key_grad_low = key_grad.astype(jnp.bfloat16)
    value_grad_low = value_grad.astype(jnp.bfloat16)
    query_bias_grad = jnp.sum(query_grad_low.astype(jnp.float32), axis=(0, 1))
    value_bias_grad = jnp.sum(value_grad_low.astype(jnp.float32), axis=(0, 1))
    joint_low = jnp.concatenate([query_grad_low, key_grad_low, value_grad_low], axis=-1)
    joint_grad = outer_sum(normed, joint_low)
    mixed_part, first_gain_grad, first_shift_grad = normalize_back(
        project_back(joint_low, joint_weight), first_scaled, first_inverse, gain_first
    )
    mixed_grad = middle_grad + mixed_part
    carried = thought_mask * mixed_grad
    following = from_behind(carried[:, 0, :], "seq", -1)
    hidden_grad = (
        mixed_grad - carried + jnp.concatenate([carried[:, 1:], following[:, None, :]], axis=1)
    )
    (
        first_gain_grad,
        first_shift_grad,
        joint_grad,
        query_bias_grad,
        value_bias_grad,
        output_weight_grad,
        output_bias_grad,
        second_gain_grad,
        second_shift_grad,
        up_weight_grad,
        up_bias_grad,
        down_weight_grad,
        down_bias_grad,
    ) = (
        lax.psum_scatter(
            first_gain_grad.astype(jnp.bfloat16), "rows", scatter_dimension=0, tiled=True
        ).astype(jnp.float32),
        lax.psum_scatter(
            first_shift_grad.astype(jnp.bfloat16), "rows", scatter_dimension=0, tiled=True
        ).astype(jnp.float32),
        lax.psum_scatter(
            joint_grad.astype(jnp.bfloat16), "rows", scatter_dimension=0, tiled=True
        ).astype(jnp.float32),
        lax.psum_scatter(
            query_bias_grad.astype(jnp.bfloat16), "rows", scatter_dimension=0, tiled=True
        ).astype(jnp.float32),
        lax.psum_scatter(
            value_bias_grad.astype(jnp.bfloat16), "rows", scatter_dimension=0, tiled=True
        ).astype(jnp.float32),
        lax.psum_scatter(
            output_weight_grad.astype(jnp.bfloat16), "rows", scatter_dimension=0, tiled=True
        ).astype(jnp.float32),
        lax.psum_scatter(
            output_bias_grad.astype(jnp.bfloat16), "rows", scatter_dimension=0, tiled=True
        ).astype(jnp.float32),
        lax.psum_scatter(
            second_gain_grad.astype(jnp.bfloat16), "rows", scatter_dimension=0, tiled=True
        ).astype(jnp.float32),
        lax.psum_scatter(
            second_shift_grad.astype(jnp.bfloat16), "rows", scatter_dimension=0, tiled=True
        ).astype(jnp.float32),
        lax.psum_scatter(
            up_weight_grad.astype(jnp.bfloat16), "rows", scatter_dimension=0, tiled=True
        ).astype(jnp.float32),
        lax.psum_scatter(
            up_bias_grad.astype(jnp.bfloat16), "rows", scatter_dimension=0, tiled=True
        ).astype(jnp.float32),
        lax.psum_scatter(
            down_weight_grad.astype(jnp.bfloat16), "rows", scatter_dimension=0, tiled=True
        ).astype(jnp.float32),
        lax.psum_scatter(
            down_bias_grad.astype(jnp.bfloat16), "rows", scatter_dimension=0, tiled=True
        ).astype(jnp.float32),
    )
    (
        first_gain_grad,
        first_shift_grad,
        joint_grad,
        query_bias_grad,
        value_bias_grad,
        output_weight_grad,
        output_bias_grad,
        second_gain_grad,
        second_shift_grad,
        up_weight_grad,
        up_bias_grad,
        down_weight_grad,
        down_bias_grad,
    ) = (
        lax.psum(first_gain_grad.astype(jnp.bfloat16), "seq").astype(jnp.float32),
        lax.psum(first_shift_grad.astype(jnp.bfloat16), "seq").astype(jnp.float32),
        lax.psum(joint_grad.astype(jnp.bfloat16), "seq").astype(jnp.float32),
        lax.psum(query_bias_grad.astype(jnp.bfloat16), "seq").astype(jnp.float32),
        lax.psum(value_bias_grad.astype(jnp.bfloat16), "seq").astype(jnp.float32),
        lax.psum(output_weight_grad.astype(jnp.bfloat16), "seq").astype(jnp.float32),
        lax.psum(output_bias_grad.astype(jnp.bfloat16), "seq").astype(jnp.float32),
        lax.psum(second_gain_grad.astype(jnp.bfloat16), "seq").astype(jnp.float32),
        lax.psum(second_shift_grad.astype(jnp.bfloat16), "seq").astype(jnp.float32),
        lax.psum(up_weight_grad.astype(jnp.bfloat16), "seq").astype(jnp.float32),
        lax.psum(up_bias_grad.astype(jnp.bfloat16), "seq").astype(jnp.float32),
        lax.psum(down_weight_grad.astype(jnp.bfloat16), "seq").astype(jnp.float32),
        lax.psum(down_bias_grad.astype(jnp.bfloat16), "seq").astype(jnp.float32),
    )
    return (
        block_output,
        hidden_grad,
        first_gain_grad,
        first_shift_grad,
        joint_grad,
        query_bias_grad,
        value_bias_grad,
        output_weight_grad,
        output_bias_grad,
        second_gain_grad,
        second_shift_grad,
        up_weight_grad,
        up_bias_grad,
        down_weight_grad,
        down_bias_grad,
    )


F32, BF16 = (jnp.float32, jnp.bfloat16)
BLOCK = 512
FF = 3072
PIECE = 384
TILE = 48
WINDOW = 384
PLANE_ORDERS = ["yx", "xy", "yx", "xy"]
UNIT_ORDERS = ["lyxh", "lhyx", "lyhx", "xyhl", "lxyh"]
JOINT_ORDERS = ["xhly", "ylhx", "xylh", "xylh", "lyxh", "yxlh", "ylxh", "yxlh", "yxlh"]
SCHEDULE = [
    ("D", 0, 0), ("U", 0, 0), ("D", 1, 0), ("D", 0, 1), ("U", 1, 0), ("D", 2, 0), ("U", 0, 1), ("U", 2, 0),
    ("D", 3, 0), ("D", 1, 1), ("U", 1, 1), ("U", 2, 1), ("U", 6, 0), ("U", 3, 0), ("U", 4, 0), ("D", 3, 1),
    ("D", 2, 1), ("U", 2, 2), ("U", 0, 2), ("U", 9, 0), ("U", 10, 0), ("U", 6, 1), ("U", 1, 2), ("U", 5, 0),
    ("U", 7, 0), ("U", 3, 1), ("U", 0, 3), ("U", 8, 0), ("U", 6, 2), ("U", 11, 0), ("U", 5, 1), ("U", 12, 0),
    ("U", 4, 1), ("U", 2, 3), ("Z", 0, 2), ("U", 10, 1), ("U", 13, 0), ("U", 3, 2), ("U", 9, 1), ("U", 11, 1),
    ("U", 5, 2), ("U", 1, 3), ("U", 6, 3), ("U", 10, 2), ("U", 12, 1), ("U", 7, 1), ("U", 3, 3), ("U", 13, 1),
    ("U", 8, 1), ("U", 9, 2), ("S", 0, 0), ("U", 11, 2), ("U", 10, 3), ("U", 4, 2), ("U", 5, 3), ("U", 12, 2),
    ("U", 7, 2), ("Z", 0, 3), ("U", 13, 2), ("U", 8, 2), ("U", 9, 3), ("S", 0, 1), ("U", 11, 3), ("U", 12, 3),
    ("U", 7, 3), ("U", 4, 3), ("U", 13, 3), ("U", 8, 3),
]
PUMPS = [0, 0, 0, 0, 2, 0, 1, 0, 2, 1, 0, 0, 2, 2, 0, 2, 3, 2, 1, 4, 2, 2, 4]


def nn(left, right):
    return lax.dot_general(left, right, (((1,), (0,)), ((), ())), preferred_element_type=F32)


def nt(left, right):
    return lax.dot_general(left, right, (((1,), (1,)), ((), ())), preferred_element_type=F32)


def tn(left, right):
    return lax.dot_general(left, right, (((0,), (0,)), ((), ())), preferred_element_type=F32)


def wide(column, copies):
    return jnp.concatenate([column] * copies, axis=1)


def row_norm(values):
    centered = values - jnp.mean(values, axis=-1, keepdims=True)
    inverse = lax.rsqrt(jnp.mean(centered * centered, axis=-1, keepdims=True) + EPSILON)
    return (centered * inverse, inverse)


def row_norm_back(upstream, scaled, inverse, gain):
    weighted = upstream * gain
    return inverse * (
        weighted
        - jnp.mean(weighted, axis=-1, keepdims=True)
        - scaled * jnp.mean(weighted * scaled, axis=-1, keepdims=True)
    )


def fold(values):
    return jnp.sum(values.reshape(values.shape[0] // 8, 8, values.shape[1]), axis=0)


def split_pair(values, lane):
    zero = jnp.zeros_like(values)
    return jnp.concatenate([jnp.where(lane < HD, values, zero), jnp.where(lane < HD, zero, values)], axis=0)


def join_pair(values):
    return jnp.concatenate([values[:HD, :128], values[HD:, 128:]], axis=0)


def step_kernel(
    hid, seg, tho, pad, cott, v0, v1, v2, v3, v4, v5, v6, v7, v8, jw, ow, uw, dw,
    blk, hg, sout, jout, dout, vout, nth,
    wb1, wb2, wo, fa, fb, fd, fe, nb, st, q, kk, vv, kt, vt, ps, il, at, att, cotp, act, xx, ulo, ulp,
    hin, hs, mlp, do, dka, dva, gd, gs, gj, r1d, r2d, r3d, r4d, r1, r2, r3, r4, j1, j2, j3, j4,
    mask, ksg, tht, ubg, sv, svr, svx, svz, cin, small, hidv, cot, vec, lsem, psend, precv, rsend, rrecv,
):
    core, line = (lax.axis_index("seq"), lax.axis_index("rows"))
    other = 1 - core
    bits = {"x": lax.rem(line, 2), "y": lax.rem(line // 2, 2), "l": lax.rem(line // 4, 2), "h": line // 8}
    peer = {
        "c": (other, line),
        "x": (core, line + 1 - 2 * bits["x"]),
        "y": (core, line + 2 - 4 * bits["y"]),
        "l": (core, line + 4 - 8 * bits["l"]),
        "h": (core, line + 8 - 16 * bits["h"]),
    }
    base = core * BLOCK
    core_f = core.astype(F32)
    half = pl.multiple_of(core * PIECE, 128)
    other_half = pl.multiple_of(other * PIECE, 128)

    def here(src, dst, spot):
        return pltpu.make_async_copy(src, dst, lsem.at[spot])

    def pair(src, dst, spot):
        return pltpu.make_async_remote_copy(
            src_ref=src, dst_ref=dst, send_sem=psend.at[spot], recv_sem=precv.at[spot],
            device_id=peer["c"], device_id_type=MESH,
        )

    def far(src, dst, group, spot, bit):
        return pltpu.make_async_remote_copy(
            src_ref=src, dst_ref=dst, send_sem=rsend.at[group], recv_sem=rrecv.at[spot],
            device_id=peer[bit], device_id_type=MESH,
        )

    hidden_in = here(hid, hidv, 13)
    hidden_in.start()
    joint_in = [here(jw.at[:, pl.ds(j * D, D)], wb1.at[pl.ds(j * D, D), :], j) for j in range(3)]
    for j in (1, 2, 0):
        joint_in[j].start()
    out_in = here(ow, wo, 3)
    up_in = here(uw, wb2, 4)
    cot_in = here(cott, cot, 14)

    barrier = pltpu.get_barrier_semaphore()
    across = (core, line + 3 - 2 * bits["x"] - 4 * bits["y"])
    along = (core, line + 12 - 8 * bits["l"] - 16 * bits["h"])
    for device in list(peer.values()) + [across, along]:
        pl.semaphore_signal(barrier, inc=1, device_id=device, device_id_type=MESH)

    for j, ref in enumerate((v0, v1, v2, v3, v4, v5, v6, v7)):
        small[j : j + 1, :] = ref[...].astype(F32).reshape(1, D)
    for j in range(4):
        small[8 + j : 9 + j, :] = v8[D * j : D * j + D].astype(F32).reshape(1, D)
    flags = tho[...].astype(F32)
    tht[...] = jnp.broadcast_to(flags, (128, BLOCK)).T
    hidden_in.wait()
    fa[8 : BLOCK + 8, :] = hidv[...].astype(F32)

    def mix(s):
        inputs = fa[8 + 64 * s : 72 + 64 * s, :]
        previous = fa[7 + 64 * s : 71 + 64 * s, :]
        mixed = inputs + wide(tht[64 * s : 64 * s + 64, :], 6) * (previous - inputs)
        fb[64 * s : 64 * s + 64, :] = mixed
        scaled, _ = row_norm(mixed)
        nb[64 * s : 64 * s + 64, :] = (scaled * small[0:1, :] + small[1:2, :]).astype(BF16)

    def project_rows(rows, out):
        @pl.loop(0, 3)
        def _(n):
            cols = pl.ds(pl.multiple_of(256 * n, 256), 256)
            kk[out, cols] = nn(nb[rows, :], wb1[768:1536, cols]).astype(BF16)
            vv[out, cols] = (nn(nb[rows, :], wb1[1536:2304, cols]) + small[3:4, cols]).astype(BF16)
            query = (nn(nb[rows, :], wb1[0:768, cols]) + small[2:3, cols]).astype(BF16)
            q[rows, cols] = (query.astype(F32) * 0.125).astype(BF16)

    for s in range(4, 8):
        mix(s)
    for copy in joint_in:
        copy.wait()
    for copy in (cot_in, out_in, up_in):
        copy.start()
    project_rows(slice(256, 512), slice(512, 768))
    pl.semaphore_wait(barrier, 7)
    edge = pair(hidv.at[pl.ds(BLOCK - 16, 16), :], hin, 0)
    send_keys = pair(kk.at[pl.ds(BLOCK, 256), :], kk.at[pl.ds(0, 256), :], 2)
    send_values = pair(vv.at[pl.ds(BLOCK, 256), :], vv.at[pl.ds(0, 256), :], 3)
    for copy in (edge, send_keys, send_values):
        copy.start()
    for s in range(1, 4):
        mix(s)
    vt[:, 512:768] = vv[512:768, :].T

    first_start = pl.multiple_of(jnp.maximum(base - 256, 0), 128)
    for j, start in enumerate((first_start, base, base + 256)):
        start = pl.multiple_of(start, 128)
        piece = seg[:, pl.ds(start, 256)].astype(F32)
        ksg[256 * j : 256 * j + 256, :] = jnp.broadcast_to(piece, (128, 256)).T
    limit = LEN - pad[0]
    for i in range(4):
        spot = lax.broadcasted_iota(jnp.int32, (WINDOW, 128), 0)
        lane = lax.broadcasted_iota(jnp.int32, (WINDOW, 128), 1)
        key_place = spot + (base - 256 + 128 * i)
        query_place = lane + (base + 128 * i)
        query_segment = seg[:, pl.ds(pl.multiple_of(base + 128 * i, 128), 128)].astype(F32)
        seen = (
            (key_place <= query_place)
            & (ksg[128 * i : 128 * i + WINDOW, :] == query_segment)
            & ((key_place < limit) | (key_place == query_place))
            & (key_place >= 0)
        )
        mask[i] = jnp.where(seen, 0.0, NEGATIVE)

    edge.wait()
    fa[0:8, :] = jnp.broadcast_to(hin[15:16, :].astype(F32) * core_f, (8, D))
    mix(0)
    project_rows(slice(0, 256), slice(256, 512))
    spill = here(fb, hg, 7)
    spill.start()
    down_in = here(dw, wb1, 5)
    down_in.start()
    vt[:, 256:512] = vv[256:512, :].T
    send_keys.wait()
    send_values.wait()
    vt[:, 0:256] = vv[0:256, :].T

    for p in range(6):
        cols = slice(128 * p, 128 * p + 128)
        lane = lax.broadcasted_iota(jnp.int32, (128, 128), 1)
        spans = [(slice(128 * i, 128 * i + 128), slice(128 * i, 128 * i + WINDOW)) for i in range(4)]
        scores = [nt(kk[keys, cols], split_pair(q[rows, cols], lane)) for rows, keys in spans]
        scores = [scores[i] + wide(mask[i], 2) for i in range(4)]
        highest = [jnp.max(score, axis=0, keepdims=True) for score in scores]
        weights = [jnp.exp(scores[i] - highest[i]) for i in range(4)]
        inverse = [1.0 / jnp.sum(weight, axis=0, keepdims=True) for weight in weights]
        low = [weight.astype(BF16) for weight in weights]
        result = [nn(vt[cols, spans[i][1]], low[i]) for i in range(4)]
        for i in range(4):
            ps[4 * p + i] = low[i]
            il[4 * p + i] = jnp.broadcast_to(inverse[i], (8, 256))
            at[core, cols, spans[i][0]] = join_pair(result[i] * inverse[i]).astype(BF16)

    send_attended = pair(at.at[core], at.at[core], 4)
    send_attended.start()
    att[...] = at[core].T

    out_in.wait()
    spill.wait()

    @pl.loop(0, 3)
    def _(n):
        cols = pl.ds(pl.multiple_of(256 * n, 256), 256)
        fb[:, cols] = fb[:, cols] + nn(att[...], wo[:, cols]) + small[4:5, cols]

    for s in range(8):
        rows = slice(64 * s, 64 * s + 64)
        scaled, _ = row_norm(fb[rows, :])
        do[rows, :] = (scaled * small[5:6, :] + small[6:7, :]).astype(BF16)
    st[core] = do[...].T
    send_second = pair(st.at[core], st.at[core], 5)
    send_second.start()
    cot_in.wait()
    send_cot = pair(cot.at[:, pl.ds(other_half, PIECE)], cotp, 6)
    send_cot.start()

    place = {"h": 0, "l": 1, "y": 2, "x": 3}
    live, ready = ({}, [])
    orders = UNIT_ORDERS + JOINT_ORDERS
    mine = (bits["h"], bits["l"], bits["y"], bits["x"])

    def refs_of(item):
        return (gs, (r1, r2, r3, r4), item) if item < 5 else (gj, (j1, j2, j3, j4), item - 5)

    def part(item, stage, own):
        spot = [slice(None)] * 4
        for bit in orders[item][:stage]:
            spot[place[bit]] = bits[bit]
        bit = orders[item][stage]
        spot[place[bit]] = bits[bit] if own else 1 - bits[bit]
        return (refs_of(item)[2],) + tuple(spot)

    def launch(item, stage):
        ref, recv, at_item = refs_of(item)
        group = stage if item < 5 else 4 + stage
        copy = far(ref.at[part(item, stage, False)], recv[stage].at[at_item], group, 4 * item + stage, orders[item][stage])
        copy.start()
        live[(item, stage)] = copy

    def advance(item, stage):
        live[(item, stage)].wait_recv()
        ref, recv, at_item = refs_of(item)
        spot = part(item, stage, True)
        ref[spot] = ref[spot] + recv[stage][at_item]
        if stage < 3:
            launch(item, stage + 1)
            return
        result = ref.at[(at_item,) + mine]
        target = (sout if item < 5 else jout).at[core, at_item]
        for copy in (here(result, target, 16 if item < 5 else 17), pair(result, target, 24 if item < 5 else 25)):
            copy.start()

    def plane_part(z, stage, own):
        first, then = PLANE_ORDERS[z]
        spot = {"x": slice(None), "y": slice(None)}
        if stage == 0:
            spot[first] = bits[first] if own else 1 - bits[first]
        else:
            spot[first] = bits[first]
            spot[then] = bits[then] if own else 1 - bits[then]
        return ((z // 2, z % 2, spot["y"], spot["x"]), first if stage == 0 else then)

    def plane_launch(z, stage):
        spot, bit = plane_part(z, stage, False)
        copy = far(gd.at[spot], (r1d, r2d)[stage].at[z], 8 + stage, 56 + 2 * z + stage, bit)
        copy.start()
        live[("plane", z, stage)] = copy

    def plane_advance(z, stage):
        live[("plane", z, stage)].wait_recv()
        spot, _ = plane_part(z, stage, True)
        gd[spot] = gd[spot] + (r1d, r2d)[stage][z]
        live["planes"] = live.get("planes", 0) + stage
        if stage == 0:
            plane_launch(z, 1)
        elif live["planes"] == 4:
            down_launch(2)

    def down_launch(stage):
        if stage == 2:
            spot, target, bit = ((slice(None), 1 - bits["l"], bits["y"], bits["x"]), r3d, "l")
        else:
            spot, target, bit = ((1 - bits["h"], bits["l"], bits["y"], bits["x"]), r4d, "h")
        copy = far(gd.at[spot], target, 8 + stage, 62 + stage, bit)
        copy.start()
        live[("d", stage)] = copy

    def down_advance(stage):
        live[("d", stage)].wait_recv()
        if stage == 2:
            spot = (slice(None), bits["l"], bits["y"], bits["x"])
            gd[spot] = gd[spot] + r3d[...]
            down_launch(3)
            return
        gd[mine] = gd[mine] + r4d[...]
        copies = (here(gd.at[mine], dout.at[core], 15), pair(gd.at[mine], dout.at[core], 26))
        for copy in copies:
            copy.start()
        live[("d", 4)] = copies

    def act_copy(z, start, width):
        cols = pl.ds(start, width)
        return pair(act.at[:, cols], xx.at[:, cols], 10 + z)

    def unit_copy(z):
        start = pl.multiple_of(768 * z + PIECE * other, 128)
        return pair(ulo.at[:, pl.ds(start, PIECE)], ulp.at[:, pl.ds(PIECE * z, PIECE)], 14 + z)

    def pump(count):
        for _ in range(min(count, len(ready))):
            name, spot, stage = ready.pop(0)
            if name == "D":
                plane_advance(spot, stage)
            elif name == "Z":
                down_advance(stage)
            elif name == "S":
                small_advance(stage)
            else:
                advance(spot, stage)

    ready.extend(SCHEDULE)

    up_in.wait()
    down_in.wait()
    fa[...] = jnp.zeros_like(fa)

    def feed(z, first, last):
        @pl.loop(first, last)
        def _(f):
            cols = pl.ds(pl.multiple_of(768 * z + 256 * f, 256), 256)
            up_part = wb2[:, cols]
            units = nn(do[...], up_part) + small[8 + z : 9 + z, pl.ds(pl.multiple_of(256 * f, 256), 256)]
            back = nt(cot[...], wb1[cols, :])
            total = jnp.zeros((8, 256), F32)
            for s in range(8):
                rows = slice(64 * s, 64 * s + 64)
                value = units[rows, :]
                square = value * value
                gate = 0.5 + 0.5 * jnp.tanh(value * (GELU_SCALE + GELU_SCALE * GELU_CUBIC * square))
                result = value * gate
                slope = gate + 2.0 * result * (1.0 - gate) * (GELU_SCALE + 3.0 * GELU_SCALE * GELU_CUBIC * square)
                grad = back[rows, :] * slope
                total = total + fold(grad)
                act[rows, cols] = result.astype(BF16)
                ulo[rows, cols] = grad.astype(BF16)
            ubg[:, cols] = total
            fa[0:BLOCK, :] += nt(ulo[:, cols], up_part)
            act_copy(z, pl.multiple_of(768 * z + 256 * f, 256), 256).start()

        if last == 3:
            unit_copy(z).start()

    def feed_grads(z):
        if z == 0:
            send_cot.wait()
        act_copy(z, 768 * z, 768).wait()

        @pl.loop(0, 2)
        def _(y):
            cols = pl.ds(pl.multiple_of(768 * z + 384 * y, 128), 384)
            total = tn(act[:, cols], cot[:, pl.ds(half, PIECE)]) + tn(xx[:, cols], cotp[...])
            gd[z // 2, z % 2, y] = total.astype(BF16).reshape(2, 192, PIECE)

        plane_launch(z, 0)
        if z == 0:
            send_second.wait()
        unit_copy(z).wait()
        start = pl.multiple_of(768 * z + PIECE * core, 128)
        total = nn(st[core], ulo[:, pl.ds(start, PIECE)]) + nn(st[other], ulp[:, 384 * z : 384 * z + 384])
        gs[z] = total.astype(BF16).reshape(2, 2, 2, 2, TILE, PIECE)
        launch(z, 0)

    feed(0, 0, 3)
    feed(1, 0, 1)
    feed_grads(0)
    kt[:, 0:BLOCK] = nb[...].T
    keep_normed = here(kt.at[:, pl.ds(0, BLOCK)], nth.at[core], 9)
    send_normed = pair(kt.at[:, pl.ds(0, BLOCK)], nth.at[core], 1)
    keep_normed.start()
    send_normed.start()
    pump(PUMPS[0])
    feed(1, 1, 3)
    pump(PUMPS[1])
    feed(2, 0, 1)
    feed_grads(1)
    pump(PUMPS[2])
    feed(2, 1, 3)
    pump(PUMPS[3])
    feed(3, 0, 1)
    feed_grads(2)
    pump(PUMPS[4])
    feed(3, 1, 3)
    pump(PUMPS[5])
    joint_again = here(jw, wb2.at[:, pl.ds(0, 3 * D)], 6)
    joint_again.start()

    sums = [jnp.zeros((8, D), F32) for _ in range(4)]
    for s in range(8):
        rows = slice(64 * s, 64 * s + 64)
        upstream = fa[rows, :]
        scaled, inverse = row_norm(fb[rows, :])
        direct = cot[rows, :].astype(F32)
        result = direct + row_norm_back(upstream, scaled, inverse, small[5:6, :])
        fa[rows, :] = result
        nb[rows, :] = result.astype(BF16)
        for j, term in enumerate((result, upstream * scaled, upstream, direct)):
            sums[j] = sums[j] + fold(term)
    for j in range(4):
        sv[4 + j : 5 + j, :] = jnp.sum(sums[j], axis=0, keepdims=True)
    for j in range(4):
        sv[8 + j : 9 + j, :] = jnp.sum(ubg[:, 768 * j : 768 * j + 768], axis=0, keepdims=True)
    send_middle = pair(nb.at[:, pl.ds(other_half, PIECE)], mlp, 7)
    send_middle.start()
    pump(PUMPS[6])
    feed_grads(3)
    pump(PUMPS[7])

    @pl.loop(0, 3)
    def _(n):
        cols = pl.ds(pl.multiple_of(256 * n, 256), 256)
        do[:, cols] = nt(nb[...], wo[cols, :]).astype(BF16)

    pump(PUMPS[8])
    send_middle.wait()
    send_attended.wait()
    total = nn(at[core], nb[:, pl.ds(half, PIECE)]) + nn(at[other], mlp[...])
    gs[4] = total.astype(BF16).reshape(2, 2, 2, 2, TILE, PIECE)
    launch(4, 0)
    pump(PUMPS[9])
    keep_normed.wait()
    send_normed.wait()
    for j in range(3):
        kt[:, 256 * j : 256 * j + 256] = kk[256 * j : 256 * j + 256, :].T
    mixed_in = here(hg, fe, 8)
    mixed_in.start()
    normed_again = here(nth, st, 10)
    normed_again.start()

    def attend_back(p):
        cols = slice(128 * p, 128 * p + 128)
        lane = lax.broadcasted_iota(jnp.int32, (128, 128), 1)
        dka[...] = jnp.zeros_like(dka)
        dva[...] = jnp.zeros_like(dva)
        spans = [(slice(128 * i, 128 * i + 128), slice(128 * i, 128 * i + WINDOW)) for i in range(4)]
        grads, deltas = ([], [])
        for i in range(4):
            rows = spans[i][0]
            inverse = il[4 * p + i]
            spread = jnp.concatenate(
                [jnp.broadcast_to(inverse[0:1, :128], (HD, 128)), jnp.broadcast_to(inverse[0:1, 128:], (HD, 128))], axis=0
            ).T
            grad = (do[rows, cols].astype(F32) * spread).astype(BF16)
            product = (grad.astype(F32) * att[rows, cols].astype(F32)).T
            deltas.append(
                jnp.concatenate(
                    [jnp.sum(product[:HD], axis=0, keepdims=True), jnp.sum(product[HD:], axis=0, keepdims=True)], axis=1
                )
            )
            grads.append(split_pair(grad, lane))
        queries = [split_pair(q[rows, cols], lane) for rows, _ in spans]
        prob_grad = [nt(vv[spans[i][1], cols], grads[i]) for i in range(4)]
        low = [ps[4 * p + i] for i in range(4)]
        value_term = [nn(low[i], grads[i]) for i in range(4)]
        score = [(low[i].astype(F32) * (prob_grad[i] - deltas[i])).astype(BF16) for i in range(4)]
        key_term = [nn(score[i], queries[i]) for i in range(4)]
        query_term = [nn(kt[cols, spans[i][1]], score[i]) for i in range(4)]
        for i in range(4):
            xx[spans[i][0], cols] = (join_pair(query_term[i]) * 0.125).T.astype(BF16)
            dka[spans[i][1], :] += key_term[i]
            dva[spans[i][1], :] += value_term[i]
        xx[:, 768 + 128 * p : 896 + 128 * p] = dka[256:, :].astype(BF16)
        xx[:, 1536 + 128 * p : 1664 + 128 * p] = dva[256:, :].astype(BF16)
        hs[0:256, cols] = dka[0:256, :].astype(BF16)
        hs[256:512, cols] = dva[0:256, :].astype(BF16)

    def halo(g):
        return pair(hs.at[:, pl.ds(256 * g, 256)], hidv.at[:, pl.ds(256 * g, 256)], 18 + g)

    def exchange(g, j):
        start = pl.multiple_of(768 * j + 256 * g + 128 * other, 128)
        return pair(xx.at[:, pl.ds(start, 128)], ulp.at[:, pl.ds(384 * g + 128 * j, 128)], 21 + g)

    def settle(g):
        halo(g).wait()
        for j in (1, 2):
            cols = slice(768 * j + 256 * g, 768 * j + 256 * g + 256)
            come = hidv[256 * (j - 1) : 256 * j, 256 * g : 256 * g + 256]
            xx[256:512, cols] = xx[256:512, cols] + come
        for j in range(3):
            exchange(g, j).start()

    def joint_part(g):
        pair(xx.at[:, pl.ds(0, PIECE)], ulp.at[:, pl.ds(384 * g, PIECE)], 21 + g).wait()
        own = [xx[:, pl.ds(pl.multiple_of(768 * j + 256 * g + 128 * core, 128), 128)] for j in range(3)]
        total = nn(st[core], jnp.concatenate(own, axis=1)) + nn(st[other], ulp[:, 384 * g : 384 * g + 384])
        total = total.astype(BF16)
        for j in range(3):
            gj[3 * g + j] = total[:, 128 * j : 128 * j + 128].reshape(2, 2, 2, 2, TILE, 128)
            launch(5 + 3 * g + j, 0)

    def normed_back(first, count):
        @pl.loop(0, 3)
        def _(n):
            rows = pl.ds(pl.multiple_of(256 * n, 256), 256)
            spans = [slice(768 * j + 256 * first, 768 * j + 256 * (first + count)) for j in range(3)]
            total = sum(nt(xx[:, span], wb2[rows, span]) for span in spans)
            if first > 0:
                total = total + fd[0:BLOCK, rows]
            fd[0:BLOCK, rows] = total

    def output_part(n):
        cols = slice(256 * n, 256 * n + 256)
        do[:, cols] = (fb[:, cols] + nn(act[...], wb1[:, cols]) + small[7:8, cols]).astype(BF16)

    for p in range(6):
        attend_back(p)
        g = p // 2
        if p % 2 == 1:
            halo(g).start()
        elif p > 0:
            if p == 2:
                normed_again.wait()
            settle(g - 1)
        if p in (3, 5):
            joint_part(g - 1)
        pump(PUMPS[10 + p])

    joint_again.wait()
    normed_back(0, 2)
    settle(2)
    pump(PUMPS[16])

    joint_part(2)
    pump(PUMPS[17])

    normed_back(2, 1)
    pump(PUMPS[18])
    sv[2:3, :] = jnp.sum(xx[:, 0:768].astype(F32), axis=0, keepdims=True)
    sv[3:4, :] = jnp.sum(xx[:, 1536:2304].astype(F32), axis=0, keepdims=True)
    mixed_in.wait()
    sums = [jnp.zeros((8, D), F32) for _ in range(2)]
    for s in range(8):
        rows = slice(64 * s, 64 * s + 64)
        upstream = fd[rows, :]
        scaled, inverse = row_norm(fe[rows, :])
        grad = fa[rows, :] + row_norm_back(upstream, scaled, inverse, small[0:1, :])
        sums[0] = sums[0] + fold(upstream * scaled)
        sums[1] = sums[1] + fold(upstream)
        carried = wide(tht[rows, :], 6) * grad
        fa[rows, :] = grad - carried
        fd[rows, :] = carried
    carry = pair(fd.at[pl.ds(0, 8), :], cin, 8)
    carry.start()
    for j in range(2):
        sv[j : j + 1, :] = jnp.sum(sums[j], axis=0, keepdims=True)
    sv[12:16, :] = jnp.zeros((4, D), F32)
    small_copy = pair(sv, svr, 9)
    small_copy.start()
    fd[BLOCK : BLOCK + 8, :] = jnp.zeros((8, D), F32)
    pump(PUMPS[19])
    small_copy.wait()
    sv[...] = sv[...] + svr[...]

    def spread_small(slots, spot, names, row):
        slots[spot] = sv[...]
        copies = []
        for d in (1, 2, 3):
            step = sum((names[b][1] * (1 - 2 * bits[names[b][0]])) for b in range(2) if d & (1 << b))
            copies.append(
                pltpu.make_async_remote_copy(
                    src_ref=sv, dst_ref=slots.at[spot], send_sem=rsend.at[row + d], recv_sem=rrecv.at[row + 54 + d],
                    device_id=(core, line + step), device_id_type=MESH,
                )
            )
        for copy in copies:
            copy.start()
        return copies

    def small_advance(stage):
        slots = (svx, svz)[stage]
        for copy in live[("s", stage)]:
            copy.wait()
        sv[...] = (slots[0] + slots[1]) + (slots[2] + slots[3])
        if stage == 0:
            live[("s", 1)] = spread_small(svz, line // 4, (("l", 4), ("h", 8)), 14)

    live[("s", 0)] = spread_small(svx, lax.rem(line, 4), (("x", 1), ("y", 2)), 11)
    carry.wait()
    fd[BLOCK : BLOCK + 1, :] = cin[0:1, :] * (1.0 - core_f)
    for s in range(8):
        rows = slice(64 * s, 64 * s + 64)
        fa[rows, :] = fa[rows, :] + fd[64 * s + 1 : 64 * s + 65, :]
    hidden_out = here(fa.at[pl.ds(0, BLOCK), :], hg, 12)
    hidden_out.start()
    pump(PUMPS[20])

    output_part(0)
    pump(PUMPS[21])
    output_part(1)
    pump(PUMPS[22])
    output_part(2)
    block_out = here(do, blk, 11)
    block_out.start()
    pump(len(ready))

    shift = lax.rem(D - TILE * line + D, D)
    vec[0:8, :] = pltpu.roll(sv[0:8, :], shift, 1)[:, 0:256]
    wide_shift = lax.rem(D - 192 * lax.rem(line, 4), D)
    turned = pltpu.roll(sv[8:16, :], wide_shift, 1)[:, 0:256]
    spot = lax.broadcasted_iota(jnp.int32, (8, 256), 0)
    vec[8:16, :] = jnp.broadcast_to(
        jnp.sum(jnp.where(spot == line // 4, turned, 0.0), axis=0, keepdims=True), (8, 256)
    )
    vec_out = here(vec, vout, 6)
    vec_out.start()
    vec_out.wait()
    for group, ref in enumerate((r1, r2, r3, r4, j1, j2, j3, j4, r1d, r2d, r3d, r4d)):
        far(ref, ref, group, 0, "x").wait_send()
    for spot, ref in ((0, sout), (1, jout)):
        here(ref.at[core], ref.at[core], 16 + spot).wait()
        pair(ref.at[core], ref.at[core], 24 + spot).wait()
    for copy in live[("d", 4)]:
        copy.wait()
    block_out.wait()
    hidden_out.wait()


def finish_kernel(
    blk, hg, sout, jout, dout, vec,
    blk_out, hg_out, fg, fs, joint_out, qb, vb, og_out, ob, sg, ss, ug_out, ub, dg_out, db,
    sin, jin, din, bin_, hin, joint, og, ug, dg, vin, sem,
):
    def move(src, dst, spot):
        copy = pltpu.make_async_copy(src, dst, sem.at[spot])
        copy.start()
        return copy

    quarter = BLOCK // 4
    wholes = [move(hg.at[pl.ds(quarter * n, quarter), :], hin.at[pl.ds(quarter * n, quarter), :], 9 + n) for n in range(4)]
    wholes.append(move(blk, bin_, 13))
    loads = [move(jout, jin, 0), move(sout, sin, 1), move(dout, din, 2)]
    vec_in = move(vec, vin, 18)
    stores = []
    for n in range(4):
        wholes[n].wait()
        span = pl.ds(quarter * n, quarter)
        stores.append(move(hin.at[span, :], hg_out.at[span, :], 14 + n))
    wholes[4].wait()
    stores.append(move(bin_, blk_out, 4))
    loads[0].wait()
    for c in range(2):
        for g in range(3):
            for j in range(3):
                start = 768 * j + 256 * g + 128 * c
                joint[:, start : start + 128] = jin[c, 3 * g + j].astype(F32)
    stores.append(move(joint, joint_out, 5))
    loads[1].wait()
    for c in range(2):
        for n in range(4):
            start = 768 * n + 384 * c
            ug[:, start : start + 384] = sin[c, n].astype(F32)
        og[:, 384 * c : 384 * c + 384] = sin[c, 4].astype(F32)
    stores.append(move(ug, ug_out, 6))
    stores.append(move(og, og_out, 7))
    vec_in.wait()
    for j, ref in enumerate((fg, fs, qb, vb, ob, sg, ss, db)):
        ref[...] = vin[j, 0:48]
    ub[...] = vin[8, 0:192]
    loads[2].wait()
    for c in range(2):
        dg[:, 384 * c : 384 * c + 384] = din[c].astype(F32)
    stores.append(move(dg, dg_out, 8))
    for copy in stores:
        copy.wait()


def fused_local(
    hidden, segments, thoughts, padding, cotangent, first_gain, first_shift, joint_weight, query_bias, value_bias,
    output_weight, output_bias, second_gain, second_shift, up_weight, up_bias, down_weight, down_bias,
):
    rows = (first_gain, first_shift, query_bias, value_bias, output_bias, second_gain, second_shift, down_bias)
    shape = jax.ShapeDtypeStruct
    vmem, anywhere = (pl.BlockSpec(memory_space=pltpu.VMEM), pl.BlockSpec(memory_space=pl.ANY))
    v = pltpu.VMEM
    dma = pltpu.SemaphoreType.DMA
    blk, hg, sout, jout, dout, vec, _ = pl.pallas_call(
        step_kernel,
        out_shape=(
            shape((BLOCK, D), BF16),
            shape((BLOCK, D), F32),
            shape((2, 5, TILE, PIECE), BF16),
            shape((2, 9, TILE, 128), BF16),
            shape((2, 192, PIECE), BF16),
            shape((16, 256), F32),
            shape((2, D, BLOCK), BF16),
        ),
        in_specs=[anywhere, vmem, vmem, pl.BlockSpec(memory_space=pltpu.SMEM), anywhere] + [vmem] * 9 + [anywhere] * 4,
        out_specs=(anywhere,) * 7,
        scratch_shapes=[
            v((FF, D), BF16), v((D, FF), BF16), v((D, D), BF16),
            v((BLOCK + 8, D), F32), v((BLOCK, D), F32), v((BLOCK + 8, D), F32), v((BLOCK, D), F32),
            v((BLOCK, D), BF16), v((2, D, BLOCK), BF16), v((BLOCK, D), BF16),
            v((768, D), BF16), v((768, D), BF16), v((D, 768), BF16), v((D, 768), BF16),
            v((24, WINDOW, 256), BF16), v((24, 8, 256), F32), v((2, D, BLOCK), BF16), v((BLOCK, D), BF16),
            v((BLOCK, PIECE), BF16), v((BLOCK, FF), BF16), v((BLOCK, FF), BF16), v((BLOCK, FF), BF16), v((BLOCK, 1536), BF16),
            v((16, D), BF16), v((BLOCK, D), BF16), v((BLOCK, PIECE), BF16), v((BLOCK, D), BF16),
            v((768, 128), F32), v((768, 128), F32),
            v((2, 2, 2, 2, 192, PIECE), BF16), v((5, 2, 2, 2, 2, TILE, PIECE), BF16), v((9, 2, 2, 2, 2, TILE, 128), BF16),
            v((4, 2, 192, PIECE), BF16), v((4, 192, PIECE), BF16), v((2, 192, PIECE), BF16), v((192, PIECE), BF16),
            v((5, 2, 2, 2, TILE, PIECE), BF16), v((5, 2, 2, TILE, PIECE), BF16), v((5, 2, TILE, PIECE), BF16), v((5, TILE, PIECE), BF16),
            v((9, 2, 2, 2, TILE, 128), BF16), v((9, 2, 2, TILE, 128), BF16), v((9, 2, TILE, 128), BF16), v((9, TILE, 128), BF16),
            v((4, WINDOW, 128), F32), v((768, 128), F32), v((BLOCK, 128), F32), v((8, FF), F32),
            v((16, D), F32), v((16, D), F32), v((4, 16, D), F32), v((4, 16, D), F32), v((8, D), F32), v((16, D), F32), v((BLOCK, D), BF16), v((BLOCK, D), BF16), v((16, 256), F32),
            dma((18,)), dma((27,)), dma((27,)), dma((18,)), dma((72,)),
        ],
        compiler_params=pltpu.CompilerParams(collective_id=0, has_side_effects=True, vmem_limit_bytes=66 << 20),
    )(
        hidden[0], segments, thoughts, padding, cotangent[0], *rows, up_bias, joint_weight, output_weight, up_weight, down_weight
    )
    vector = shape((TILE,), F32)
    results = pl.pallas_call(
        finish_kernel,
        out_shape=(
            shape((BLOCK, D), BF16), shape((BLOCK, D), F32),
            vector, vector, shape((TILE, 3 * D), F32), vector, vector, shape((TILE, D), F32), vector, vector, vector,
            shape((TILE, FF), F32), shape((192,), F32), shape((192, D), F32), vector,
        ),
        in_specs=[anywhere] * 6,
        out_specs=(
            anywhere, anywhere, vmem, vmem, anywhere, vmem, vmem, anywhere, vmem, vmem, vmem, anywhere, vmem, anywhere, vmem,
        ),
        scratch_shapes=[
            v((2, 5, TILE, PIECE), BF16), v((2, 9, TILE, 128), BF16), v((2, 192, PIECE), BF16), v((BLOCK, D), BF16), v((BLOCK, D), F32),
            v((TILE, 3 * D), F32), v((TILE, D), F32), v((TILE, FF), F32), v((192, D), F32), v((16, 256), F32), dma((19,)),
        ],
    )(blk, hg, sout, jout, dout, vec)
    return (results[0][None], results[1][None]) + tuple(results[2:])


MESH = pl.DeviceIdType.MESH


def solution(mesh):
    placed = (
        P("rows", "seq", None),
        P("rows", None),
        P("rows", "seq"),
        P("rows"),
        P("rows", "seq", None),
        P(),
        P(),
        P(),
        P(),
        P(),
        P(),
        P(),
        P(),
        P(),
        P(),
        P(),
        P(),
        P(),
    )
    fused = mesh.shape["seq"] == 2 and mesh.shape["rows"] == 16
    return jax.shard_map(
        fused_local if fused else local,
        mesh=mesh,
        in_specs=placed,
        out_specs=(
            P("rows", "seq", None),
            P("rows", "seq", None),
            P("rows"),
            P("rows"),
            P("rows", None),
            P("rows"),
            P("rows"),
            P("rows", None),
            P("rows"),
            P("rows"),
            P("rows"),
            P("rows", None),
            P("rows"),
            P("rows", None),
            P("rows"),
        ),
        check_vma=False,
    )
```
